32 devices in a mesh: groups: 2 (over y), ctx: 4 (over z), enc: 2 (over x), tp: 2 (over core).
Axes of the slice: x: 2, y: 2, z: 4, core: 2. Of those that a mesh axis runs over, the one named last changes fastest.
Arguments:
- enc_rows: bfloat16 [4, 1024, 1280], P(('groups', 'enc'), 'ctx'), parts along dimension 0, may hold values from -6 to 6
- row_slot: int32 [4, 1024], P(('groups', 'enc'), 'ctx'), parts along dimension 0, may hold values from 0 to 1023, as said below
- row_kind: int32 [4, 1024], P(('groups', 'enc'), 'ctx'), parts along dimension 0, may hold values from 0 to 1, as said below
- audio_proj: bfloat16 [1280, 8192], P(None, ('ctx', 'tp')), may hold values from -0.15625 to 0.15625
- frame_proj: bfloat16 [1280, 8192], P(None, ('ctx', 'tp')), may hold values from -0.15625 to 0.15625
- audio_bias: bfloat16 [8192], P(('ctx', 'tp')), may hold values from -3 to 3
- frame_bias: bfloat16 [8192], P(('ctx', 'tp')), may hold values from -3 to 3
- norm_gain: bfloat16 [8192], replicated, may hold values from 0.5 to 1.5
Outputs:
- normed: bfloat16 [4, 1024, 8192], P(('groups', 'enc'), ('ctx', 'tp')), parts along dimension 0
The draws below stay inside these ranges and needn't reach their ends.
There are 2 independent parts, one for each index of `groups`. The reference program is written for one: setup_inputs(seed, part) draws one part's arguments, and reference() takes and returns one part's arrays. A program takes and returns all parts, laid end to end along the dimension named above; an argument that names none is the same for every part. Nothing has to cross between parts.
Inputs may be any that keep to these rules, and one draw needn't show every extreme that they name: `row_slot`: in each conversation every value appears exactly once. A row with value s fills context shard s // 256. Of the 256 rows of one owner (one index of ctx, in one conversation), at most 128 fill any one context shard, and every owner sends exactly 128 rows to some context shard. Rows come in 2-second spans of at most 128 rows: one span's rows are consecutive at the owner and fill consecutive positions. `row_kind`: within a span the audio rows come before the frame rows.
All inputs are finite; a program needn't handle non-finite values.
Results may differ from the reference program's by a relative error of at most 0.005.
Values may be sent and summed in bfloat16 or wider, within the bound.
No kernel may reach another device: no remote copies, remote signals or barrier semaphores. Data moves between devices by JAX's collectives and lax.ppermute only.
A program may use at most 128 MiB of HBM per device.

```python
import jax
import jax.numpy as jnp
from jax import lax

DM = 8192
EW = 1280
SEQ_DEV = 256
CONV_LEN = 1024
CAP = 128
N_CTX = 4
N_ENC = 2


def conversation_tables(key):
    shards = N_CTX
    subkeys = jax.random.split(key, 5)
    unit_slots = jnp.repeat(jnp.arange(1, shards, dtype=jnp.int32), CAP)
    shuffled = jax.random.permutation(subkeys[0], unit_slots.shape[0])
    chosen = unit_slots[shuffled[:SEQ_DEV - CAP]]
    counts = jnp.zeros((shards,), jnp.int32).at[chosen].add(1)
    counts = counts.at[0].set(CAP)
    owner_shift = jax.random.permutation(subkeys[1], shards).astype(jnp.int32)
    shard_label = jax.random.permutation(subkeys[2], shards).astype(jnp.int32)
    label_inverse = jnp.argsort(shard_label, stable=True).astype(jnp.int32)

    def shuffle_one(subkey):
        return jax.random.permutation(subkey, shards).astype(jnp.int32)
    span_order = jax.vmap(shuffle_one)(jax.random.split(subkeys[3], shards))
    ordered_counts = counts[span_order]
    starts_ordered = jnp.cumsum(ordered_counts, axis=1) - ordered_counts
    inverse_order = jnp.argsort(span_order, axis=1, stable=True).astype(jnp.int32)
    span_start = jnp.take_along_axis(starts_ordered, inverse_order, axis=1)
    local_index = jnp.arange(SEQ_DEV, dtype=jnp.int32)
    running = jnp.cumsum(counts)
    span_of_row = jnp.sum((running[None, :] <= local_index[:, None]).astype(jnp.int32), axis=1)
    within = local_index - (running[span_of_row] - counts[span_of_row])
    shard_of_row = label_inverse[(owner_shift[:, None] + span_of_row[None, :]) % shards]
    place_in_shard = span_start[shard_of_row, span_of_row[None, :]] + within[None, :]
    slots = shard_of_row * SEQ_DEV + place_in_shard
    audio_count = jax.random.randint(subkeys[4], (shards, shards), 0, CAP + 1)
    audio_rows = jnp.minimum(audio_count[:, span_of_row], counts[span_of_row][None, :])
    kinds = (within[None, :] >= audio_rows).astype(jnp.int32)
    return (slots.reshape(-1).astype(jnp.int32), kinds.reshape(-1).astype(jnp.int32))


def routing_tables(key):
    conv_keys = jax.random.split(jax.random.fold_in(key, 7), N_ENC)
    return jax.vmap(conversation_tables)(conv_keys)


def draw_row_slot(key, part):
    return routing_tables(key)[0]


def draw_row_kind(key, part):
    return routing_tables(key)[1]


def level_of(own_key, shape, cuts, smallest, high):
    def one(position, parts):
        heights = jax.random.uniform(jax.random.fold_in(jax.random.fold_in(own_key, 6), position), (parts,), jnp.float32, smallest / len(cuts), high / len(cuts))
        return jnp.repeat(jnp.exp(heights), shape[position] // parts).reshape((-1,) + (1,) * (len(shape) - position - 1))

    gain = one(*cuts[0])
    for cut in cuts[1:]:
        gain = gain * one(*cut)
    return gain


def noise(stream_key, shape, width, most, pieces=(), kind=jnp.bfloat16):
    values = jax.random.normal(stream_key, shape, jnp.float32) * width
    if len(pieces) > 0:
        values = level_of(stream_key, shape, pieces, -0.22, 0.18) * values
    return jnp.clip(values, min=-most, max=most).astype(kind)


def setup_inputs(seed: int = 0, part: int = 0) -> dict:
    keys = jax.random.split(jax.random.key(seed), 9)
    part_splits = jax.random.split(jax.random.fold_in(keys[8], part), 9)
    return {
        "enc_rows": noise(part_splits[0], (N_ENC, CONV_LEN, EW), 1.0, 6.0, ((0, 2), (1, 4))),
        "row_slot": draw_row_slot(jax.random.fold_in(jax.random.fold_in(keys[8], part), 71), part),
        "row_kind": draw_row_kind(jax.random.fold_in(jax.random.fold_in(keys[8], part), 71), part),
        "audio_proj": noise(keys[3], (EW, DM), EW ** -0.5, 0.15625, ((1, 8),)),
        "frame_proj": noise(keys[4], (EW, DM), EW ** -0.5, 0.15625, ((1, 8),)),
        "audio_bias": noise(keys[5], (DM,), 0.5, 3.0, ((0, 8),)),
        "frame_bias": noise(keys[6], (DM,), 0.5, 3.0, ((0, 8),)),
        "norm_gain": jnp.clip(1.0 + 0.1 * jax.random.normal(keys[7], (DM,), jnp.float32), 0.5, 1.5).astype(jnp.bfloat16),
    }


def one_conversation(packed, audio_proj, frame_proj, audio_bias, frame_bias, norm_gain):
    rows, slots, kinds = packed
    is_audio = (kinds == 0)[:, None]
    nothing = jnp.zeros((), rows.dtype)
    stacked = jnp.concatenate([jnp.where(is_audio, rows, nothing), jnp.where(is_audio, nothing, rows)], axis=1)
    weights = jnp.concatenate([audio_proj, frame_proj], axis=0)
    projected = jnp.dot(stacked, weights, preferred_element_type=jnp.float32)
    chosen_bias = jnp.where(is_audio, audio_bias.astype(jnp.float32)[None, :], frame_bias.astype(jnp.float32)[None, :])
    projected = (projected + chosen_bias).astype(jnp.bfloat16)
    embeds = jnp.zeros((CONV_LEN, DM), jnp.bfloat16).at[slots].set(projected)
    widened = embeds.astype(jnp.float32)
    mean_square = lax.optimization_barrier(jnp.mean(widened * widened, axis=-1, keepdims=True))
    return (widened * lax.rsqrt(mean_square + 1e-06) * norm_gain.astype(jnp.float32)).astype(jnp.bfloat16)

def reference(enc_rows, row_slot, row_kind, audio_proj, frame_proj, audio_bias, frame_bias, norm_gain):

    def handle(packed):
        return one_conversation(packed, audio_proj, frame_proj, audio_bias, frame_bias, norm_gain)
    return lax.map(handle, (enc_rows, row_slot, row_kind))
```

```python
import functools

import jax
import jax.numpy as jnp
from jax import lax
from jax.experimental import pallas as pl
from jax.experimental.pallas import tpu as pltpu
from jax.sharding import PartitionSpec as P

VMEM = pl.BlockSpec(memory_space=pltpu.VMEM)
SMEM = pl.BlockSpec(memory_space=pltpu.SMEM)
PARAMS = pltpu.CompilerParams(vmem_limit_bytes=48 << 20)


def column_of(row_vector):
    r = row_vector.shape[1]
    diagonal = lax.broadcasted_iota(jnp.int32, (r, r), 0) == lax.broadcasted_iota(
        jnp.int32, (r, r), 1
    )
    return jnp.sum(jnp.where(diagonal, row_vector, 0), axis=1, keepdims=True)


def project_kernel(meta, x, w_audio, w_frame, b_audio, b_frame, out):
    is_audio = column_of(meta[...] % 2) == 0
    audio = jnp.dot(x[...], w_audio[...], preferred_element_type=jnp.float32)
    frame = jnp.dot(x[...], w_frame[...], preferred_element_type=jnp.float32)
    audio = audio + b_audio[...].astype(jnp.float32)
    frame = frame + b_frame[...].astype(jnp.float32)
    out[...] = jnp.where(is_audio, audio, frame).astype(out.dtype)


def project_halves_kernel(scalars, meta, mine, other, wa, wf, ba, bf, out, x):
    half = mine.shape[0]
    t = scalars[0]
    x[pl.ds(pl.multiple_of(t * half, half), half), :] = mine[...]
    x[pl.ds(pl.multiple_of((1 - t) * half, half), half), :] = other[...]
    project_kernel(meta, x, wa, wf, ba, bf, out)


def project(scalars, meta, pieces, weights):
    rows = sum(p.shape[0] for p in pieces)
    ew, cols = weights[0].shape
    cost = pl.CostEstimate(
        flops=4 * rows * ew * cols, bytes_accessed=2 * (rows * (ew + cols)), transcendentals=0
    )
    out_shape = jax.ShapeDtypeStruct((rows, cols), jnp.bfloat16)
    if len(pieces) == 1:
        return pl.pallas_call(
            project_kernel,
            out_shape=out_shape,
            in_specs=[VMEM] * 6,
            out_specs=VMEM,
            compiler_params=PARAMS,
            cost_estimate=cost,
            name="project_own",
        )(meta, *pieces, *weights)
    return pl.pallas_call(
        project_halves_kernel,
        out_shape=out_shape,
        in_specs=[SMEM] + [VMEM] * 7,
        out_specs=VMEM,
        scratch_shapes=[pltpu.VMEM((rows, ew), jnp.bfloat16)],
        compiler_params=PARAMS,
        cost_estimate=cost,
        name="project_halves",
    )(scalars, meta, *pieces, *weights)


def select_kernel(n, scalars, *refs):
    metas, projected, outs = refs[:n], refs[n : 2 * n], refs[2 * n :]
    places = outs[0].shape[0]
    rows, cols = projected[0].shape
    i = lax.broadcasted_iota(jnp.int32, (2 * places, 1), 0)
    position = jnp.where(i < places, scalars[0] + i, scalars[1] + i - places)
    total = jnp.zeros((2 * places, cols), jnp.float32)
    for meta, block in zip(metas, projected):
        chosen = (meta[...] // 2 == position).astype(jnp.float32).astype(jnp.bfloat16)
        total = total + jnp.dot(chosen, block[...], preferred_element_type=jnp.float32)
    outs[0][...] = total[:places].astype(jnp.bfloat16)
    outs[1][...] = total[places:].astype(jnp.bfloat16)


def select(bases, metas, projected, places):
    n = len(metas)
    rows, cols = projected[0].shape
    return pl.pallas_call(
        functools.partial(select_kernel, n),
        out_shape=[jax.ShapeDtypeStruct((places, cols), jnp.bfloat16)] * 2,
        in_specs=[SMEM] + [VMEM] * (2 * n),
        out_specs=[VMEM] * 2,
        compiler_params=PARAMS,
        cost_estimate=pl.CostEstimate(
            flops=4 * places * rows * n * cols, bytes_accessed=2 * n * rows * cols, transcendentals=0
        ),
        name="select",
    )(bases, *metas, *projected)


def norm_kernel(n, blocks, gain, *refs):
    pieces, out = refs[:n], refs[n]
    cols = pieces[0].shape[1]
    total = None
    for piece in pieces:
        wide = piece[...].astype(jnp.float32)
        part = jnp.sum(wide * wide, axis=1, keepdims=True)
        total = part if total is None else total + part
    scale = lax.rsqrt(total / (n * cols) + 1e-06)
    for k, piece in enumerate(pieces):
        at = pl.ds(pl.multiple_of(blocks[k] * cols, cols), cols)
        wide = piece[...].astype(jnp.float32)
        out[:, at] = (wide * scale * gain[:, at].astype(jnp.float32)).astype(out.dtype)


def norm(blocks, gain, pieces):
    n = len(pieces)
    places, cols = pieces[0].shape
    return pl.pallas_call(
        functools.partial(norm_kernel, n),
        out_shape=jax.ShapeDtypeStruct((places, n * cols), jnp.bfloat16),
        in_specs=[SMEM] + [VMEM] * (n + 1),
        out_specs=VMEM,
        compiler_params=PARAMS,
        cost_estimate=pl.CostEstimate(
            flops=4 * places * n * cols, bytes_accessed=4 * places * n * cols, transcendentals=0
        ),
        name="norm",
    )(blocks, gain, *pieces)


def body(enc_rows, row_slot, row_kind, audio_proj, frame_proj, audio_bias, frame_bias, norm_gain):
    n_ctx, n_tp = lax.axis_size("ctx"), lax.axis_size("tp")
    z, t = lax.axis_index("ctx"), lax.axis_index("tp")
    rows = enc_rows[0]
    seq_dev = rows.shape[0]
    half = seq_dev // n_tp
    places = seq_dev // n_tp
    weights = (audio_proj, frame_proj, audio_bias[None, :], frame_bias[None, :])
    scalars = t[None].astype(jnp.int32)

    def over_ctx(x, m):
        return lax.ppermute(x, "ctx", [(i, i ^ m) for i in range(n_ctx)])

    def over_tp(x):
        return lax.ppermute(x, "tp", [(0, 1), (1, 0)])

    meta = row_slot * 2 + row_kind
    mine = lax.dynamic_slice_in_dim(rows, t * half, half, 0)
    metas, projected = [meta], [project(scalars, meta, [rows], weights)]
    for m in range(1, n_ctx):
        arrived = over_ctx(mine, m)
        metas.append(over_ctx(meta, m))
        projected.append(project(scalars, metas[m], [arrived, over_tp(arrived)], weights))

    pieces, blocks = [], []
    for m in reversed(range(n_ctx)):
        bases = jnp.stack([((z ^ m) * n_tp + (t ^ d)) * places for d in range(2)])
        blocks += [(z ^ m) * n_tp + (t ^ d) for d in range(2)]
        same, other = select(bases.astype(jnp.int32), metas, projected, places)
        for d, piece in ((0, same), (1, other)):
            if m or d:
                perm = [
                    (i * n_tp + c, (i ^ m) * n_tp + (c ^ d))
                    for i in range(n_ctx)
                    for c in range(n_tp)
                ]
                piece = lax.ppermute(piece, ("ctx", "tp"), perm)
            pieces.append(piece)
    return norm(jnp.stack(blocks).astype(jnp.int32), norm_gain[None, :], pieces)[None]


def solution(mesh):
    return jax.shard_map(
        body,
        mesh=mesh,
        in_specs=(
            P(("groups", "enc"), "ctx", None),
            P(("groups", "enc"), "ctx"),
            P(("groups", "enc"), "ctx"),
            P(None, ("ctx", "tp")),
            P(None, ("ctx", "tp")),
            P(("ctx", "tp")),
            P(("ctx", "tp")),
            P(),
        ),
        out_specs=P(("groups", "enc"), ("ctx", "tp"), None),
        check_vma=False,
    )
```

```python
import functools

import jax
import jax.numpy as jnp
from jax import lax
from jax.experimental import pallas as pl
from jax.experimental.pallas import tpu as pltpu
from jax.sharding import PartitionSpec as P

VMEM = pl.BlockSpec(memory_space=pltpu.VMEM)
HBM = pl.BlockSpec(memory_space=pltpu.HBM)
PARAMS = pltpu.CompilerParams(vmem_limit_bytes=12 << 20)
BF16, F32, I32 = jnp.bfloat16, jnp.float32, jnp.int32


def cost(flops, moved):
    return pl.CostEstimate(flops=flops, bytes_accessed=moved, transcendentals=0)


def half_kernel(rows, out, sem):
    half = out.shape[0]
    start = pl.multiple_of(lax.axis_index("tp") * half, half)
    copy = pltpu.make_async_copy(rows.at[pl.ds(start, half), :], out, sem)
    copy.start()
    copy.wait()


def own_half(rows, half):
    width = rows.shape[1]
    return pl.pallas_call(
        half_kernel,
        out_shape=jax.ShapeDtypeStruct((half, width), BF16),
        in_specs=[HBM],
        out_specs=VMEM,
        scratch_shapes=[pltpu.SemaphoreType.DMA],
        compiler_params=pltpu.CompilerParams(vmem_limit_bytes=4 << 20),
        cost_estimate=cost(0, 4 * half * width),
        name="own_half",
    )(rows)


def column_of(row_vector):
    r = row_vector.shape[1]
    diagonal = lax.broadcasted_iota(I32, (r, r), 0) == lax.broadcasted_iota(I32, (r, r), 1)
    return jnp.sum(jnp.where(diagonal, row_vector, 0), axis=1, keepdims=True)


def project(kind_row, x, w_audio, w_frame, b_audio, b_frame, out):
    is_audio = column_of(kind_row) == 0
    audio = jnp.dot(x, w_audio[...], preferred_element_type=F32)
    frame = jnp.dot(x, w_frame[...], preferred_element_type=F32)
    audio = audio + b_audio[...].astype(F32)
    frame = frame + b_frame[...].astype(F32)
    out[...] = jnp.where(is_audio, audio, frame).astype(out.dtype)


def project_own_kernel(meta, x, wa, wf, ba, bf, out):
    project(meta[...] % 2, x[...], wa, wf, ba, bf, out)


def project_own(meta, rows, weights):
    ew, cols = weights[0].shape
    return pl.pallas_call(
        project_own_kernel,
        out_shape=jax.ShapeDtypeStruct((rows.shape[0], cols), BF16),
        in_specs=[VMEM] * 6,
        out_specs=VMEM,
        compiler_params=PARAMS,
        cost_estimate=cost(4 * rows.shape[0] * ew * cols, 4 * ew * cols),
        name="project_own",
    )(meta, rows, *weights)


def project_step_kernel(step, n, metas, *refs):
    arrivals, weights, outs, x = refs[:4], refs[4:8], refs[8:10], refs[10]
    half = arrivals[0].shape[0]
    z, t = lax.axis_index("ctx"), lax.axis_index("tp")
    for side, owner in ((0, z - step), (1, z + step)):

        @pl.when(jnp.logical_and(owner >= 0, owner < n))
        def _():
            x[pl.ds(pl.multiple_of(t * half, half), half), :] = arrivals[2 * side][...]
            x[pl.ds(pl.multiple_of((1 - t) * half, half), half), :] = arrivals[2 * side + 1][...]
            meta = metas[pl.ds(jnp.bitwise_xor(owner, z), 1), :]
            project(meta % 2, x[...], *weights, outs[side])


def project_step(step, n, metas, arrivals, weights):
    half, ew = arrivals[0].shape
    cols = weights[0].shape[1]
    return pl.pallas_call(
        functools.partial(project_step_kernel, step, n),
        out_shape=[jax.ShapeDtypeStruct((2 * half, cols), BF16)] * 2,
        in_specs=[VMEM] * 9,
        out_specs=[VMEM] * 2,
        scratch_shapes=[pltpu.VMEM((2 * half, ew), BF16)],
        compiler_params=PARAMS,
        cost_estimate=cost(12 * half * ew * cols, 4 * ew * cols),
        name="project_step",
    )(metas, *arrivals, *weights)


def select_kernel(m, n, metas, own, *refs):
    sides, outs = refs[: 2 * n - 2], refs[2 * n - 2 :]
    places = outs[0].shape[0]
    z, t = lax.axis_index("ctx"), lax.axis_index("tp")
    first = jnp.bitwise_xor(z, m) * 2 * places
    i = lax.broadcasted_iota(I32, (2 * places, 1), 0)
    position = first + jnp.bitwise_xor(i, t * places)
    total = None
    for s in range(n):
        owner = lax.rem(z - s + n, n)
        if s == 0:
            block = own[...]
        else:
            block = jnp.where(z >= s, sides[2 * (s - 1)][...], sides[2 * (n - s - 1) + 1][...])
        meta = metas[pl.ds(jnp.bitwise_xor(owner, z), 1), :]
        chosen = (meta // 2 == position).astype(F32).astype(BF16)
        part = jnp.dot(chosen, block, preferred_element_type=F32)
        total = part if total is None else total + part
    outs[0][...] = total[:places].astype(BF16)
    outs[1][...] = total[places:].astype(BF16)


def select(m, n, metas, own, sides, places):
    rows, cols = own.shape
    return pl.pallas_call(
        functools.partial(select_kernel, m, n),
        out_shape=[jax.ShapeDtypeStruct((places, cols), BF16)] * 2,
        in_specs=[VMEM] * (2 * n),
        out_specs=[VMEM] * 2,
        compiler_params=PARAMS,
        cost_estimate=cost(4 * places * rows * n * cols, 2 * n * rows * cols),
        name="select",
    )(metas, own, *sides)


def norm_kernel(places_of, gain, *refs):
    n = len(places_of)
    pieces, out = refs[:n], refs[n]
    cols = pieces[0].shape[1]
    z, t = lax.axis_index("ctx"), lax.axis_index("tp")
    total = None
    for piece in pieces:
        wide = piece[...].astype(F32)
        part = jnp.sum(wide * wide, axis=1, keepdims=True)
        total = part if total is None else total + part
    scale = lax.rsqrt(total / (n * cols) + 1e-06)
    for (m, d), piece in zip(places_of, pieces):
        block = jnp.bitwise_xor(z, m) * 2 + jnp.bitwise_xor(t, d)
        at = pl.ds(pl.multiple_of(block * cols, cols), cols)
        out[:, at] = (piece[...].astype(F32) * scale * gain[:, at].astype(F32)).astype(out.dtype)


def norm(places_of, gain, pieces):
    n = len(pieces)
    places, cols = pieces[0].shape
    return pl.pallas_call(
        functools.partial(norm_kernel, places_of),
        out_shape=jax.ShapeDtypeStruct((places, n * cols), BF16),
        in_specs=[VMEM] * (n + 1),
        out_specs=VMEM,
        compiler_params=PARAMS,
        cost_estimate=cost(4 * places * n * cols, 4 * places * n * cols),
        name="norm",
    )(gain, *pieces)


def after(x, *others):
    return lax.optimization_barrier((x, *others))[0]


def body(enc_rows, row_slot, row_kind, audio_proj, frame_proj, audio_bias, frame_bias, norm_gain):
    n_ctx = lax.axis_size("ctx")
    rows = enc_rows[0]
    half = rows.shape[0] // 2
    weights = (audio_proj, frame_proj, audio_bias[None, :], frame_bias[None, :])

    def over_tp(x):
        return lax.ppermute(x, "tp", [(0, 1), (1, 0)])

    meta = row_slot * 2 + row_kind
    mine = own_half(rows, half)
    metas, m = meta, 1
    while m < n_ctx:
        met = lax.ppermute(metas, "ctx", [(i, i ^ m) for i in range(n_ctx)])
        metas = jnp.concatenate([metas, met], axis=0)
        m *= 2

    own = project_own(meta, rows, weights)
    sides, left, right, done = [], mine, mine, own
    for step in range(1, n_ctx):
        left = lax.ppermute(left, "ctx", [(i, i + 1) for i in range(step - 1, n_ctx - 1)])
        right = lax.ppermute(right, "ctx", [(i + 1, i) for i in range(n_ctx - step)])
        left, right = after(left, done), after(right, done)
        arrivals = (left, over_tp(left), right, over_tp(right))
        sides += project_step(step, n_ctx, metas, arrivals, weights)
        done = sides[-1]

    pieces, places_of = [], []
    for m in [1] + list(reversed(range(2, n_ctx))) + [0]:
        for d, piece in enumerate(select(m, n_ctx, metas, own, sides, half)):
            if m or d:
                perm = [
                    (i * 2 + c, (i ^ m) * 2 + (c ^ d)) for i in range(n_ctx) for c in range(2)
                ]
                piece = lax.ppermute(piece, ("ctx", "tp"), perm)
            pieces.append(piece)
            places_of.append((m, d))
    return norm(tuple(places_of), norm_gain[None, :], pieces)[None]


def solution(mesh):
    return jax.shard_map(
        body,
        mesh=mesh,
        in_specs=(
            P(("groups", "enc"), "ctx", None),
            P(("groups", "enc"), "ctx"),
            P(("groups", "enc"), "ctx"),
            P(None, ("ctx", "tp")),
            P(None, ("ctx", "tp")),
            P(("ctx", "tp")),
            P(("ctx", "tp")),
            P(),
        ),
        out_specs=P(("groups", "enc"), ("ctx", "tp"), None),
        check_vma=False,
    )
```

```python
import functools

import jax
import jax.numpy as jnp
from jax import lax
from jax.experimental import pallas as pl
from jax.experimental.pallas import tpu as pltpu
from jax.sharding import PartitionSpec as P

VMEM = pl.BlockSpec(memory_space=pltpu.VMEM)
HBM = pl.BlockSpec(memory_space=pltpu.HBM)
PARAMS = pltpu.CompilerParams(vmem_limit_bytes=12 << 20)
BF16, F32, I32 = jnp.bfloat16, jnp.float32, jnp.int32


def cost(flops, moved):
    return pl.CostEstimate(flops=flops // 16, bytes_accessed=moved // 16, transcendentals=0)


def send_kernel(rows, slot, kind, out, slot_here, kind_here, sems):
    half = out.shape[0] - 8
    t = lax.axis_index("tp")
    start = pl.multiple_of(t * half, half)
    copies = [
        pltpu.make_async_copy(slot, slot_here, sems.at[0]),
        pltpu.make_async_copy(kind, kind_here, sems.at[1]),
        pltpu.make_async_copy(rows.at[pl.ds(start, half), :], out.at[pl.ds(0, half), :], sems.at[2]),
    ]
    for copy in copies:
        copy.start()
    out[half:, :] = jnp.zeros((8, out.shape[1]), BF16)
    for copy in copies:
        copy.wait()
    slots = jnp.where(t == 0, slot_here[:, :half], slot_here[:, half:])
    kinds = jnp.where(t == 0, kind_here[:, :half], kind_here[:, half:])
    line = lax.broadcasted_iota(I32, (8, half), 0)
    index = jnp.where(line == 0, slots // 256, jnp.where(line == 1, slots % 256, kinds))
    out[half:, :half] = index.astype(F32).astype(BF16)


def to_send(rows, slot, kind):
    half, width = rows.shape[0] // 2, rows.shape[1]
    return pl.pallas_call(
        send_kernel,
        out_shape=jax.ShapeDtypeStruct((half + 8, width), BF16),
        in_specs=[HBM] * 3,
        out_specs=VMEM,
        scratch_shapes=[
            pltpu.VMEM(slot.shape, I32),
            pltpu.VMEM(slot.shape, I32),
            pltpu.SemaphoreType.DMA((3,)),
        ],
        compiler_params=pltpu.CompilerParams(vmem_limit_bytes=60 << 20),
        cost_estimate=cost(0, 4 * half * width),
        name="to_send",
    )(rows, slot, kind)


def column_of(row_vector):
    r = row_vector.shape[1]
    diagonal = lax.broadcasted_iota(I32, (r, r), 0) == lax.broadcasted_iota(I32, (r, r), 1)
    return jnp.sum(jnp.where(diagonal, row_vector, 0), axis=1, keepdims=True)


def project(kind_row, x, w_audio, w_frame, b_audio, b_frame, out):
    is_audio = column_of(kind_row) == 0
    audio = jnp.dot(x, w_audio[...], preferred_element_type=F32)
    frame = jnp.dot(x, w_frame[...], preferred_element_type=F32)
    audio = audio + b_audio[...].astype(F32)
    frame = frame + b_frame[...].astype(F32)
    out[...] = jnp.where(is_audio, audio, frame).astype(out.dtype)


def project_own_kernel(kind, x, wa, wf, ba, bf, out):
    project(kind[...], x[...], wa, wf, ba, bf, out)


def project_own(kind, rows, weights):
    ew, cols = weights[0].shape
    return pl.pallas_call(
        project_own_kernel,
        out_shape=jax.ShapeDtypeStruct((rows.shape[0], cols), BF16),
        in_specs=[VMEM] * 6,
        out_specs=VMEM,
        compiler_params=PARAMS,
        cost_estimate=cost(4 * rows.shape[0] * ew * cols, 4 * ew * cols),
        name="project_own",
    )(kind, rows, *weights)


def project_halves_kernel(wa, wf, ba, bf, *refs):
    pieces, out, slots = refs[:-2], refs[-2], refs[-1]
    half = pieces[0].shape[0] - 8
    x = [r[:half, :] for r in pieces]
    index = [r[half:, :half].astype(F32).astype(I32) for r in pieces]
    x = x[0] if len(x) == 1 else jnp.concatenate(x, axis=0)
    index = index[0] if len(index) == 1 else jnp.concatenate(index, axis=1)
    slots[...] = index[0:1] * 256 + index[1:2]
    project(index[2:3], x, wa, wf, ba, bf, out)


def project_halves(pieces, weights):
    rows, ew = len(pieces) * (pieces[0].shape[0] - 8), pieces[0].shape[1]
    cols = weights[0].shape[1]
    return pl.pallas_call(
        project_halves_kernel,
        out_shape=[jax.ShapeDtypeStruct((rows, cols), BF16), jax.ShapeDtypeStruct((1, rows), I32)],
        in_specs=[VMEM] * (4 + len(pieces)),
        out_specs=[VMEM] * 2,
        compiler_params=PARAMS,
        cost_estimate=cost(4 * rows * ew * cols, 4 * ew * cols),
        name="project_halves",
    )(*weights, *pieces)


def select_kernel(m, count, *refs):
    blocks, slots, outs = refs[:count], refs[count : 2 * count], refs[-2:]
    places = outs[0].shape[0]
    z, t = lax.axis_index("ctx"), lax.axis_index("tp")
    first = jnp.bitwise_xor(z, m) * 2 * places
    i = lax.broadcasted_iota(I32, (2 * places, 1), 0)
    position = first + jnp.bitwise_xor(i, t * places)
    total = None
    for block, slot in zip(blocks, slots):
        chosen = (slot[...] == position).astype(F32).astype(BF16)
        part = jnp.dot(chosen, block[...], preferred_element_type=F32)
        total = part if total is None else total + part
    outs[0][...] = total[:places].astype(BF16)
    outs[1][...] = total[places:].astype(BF16)


def select(m, blocks, slots, places):
    rows, cols = sum(b.shape[0] for b in blocks), blocks[0].shape[1]
    return pl.pallas_call(
        functools.partial(select_kernel, m, len(blocks)),
        out_shape=[jax.ShapeDtypeStruct((places, cols), BF16)] * 2,
        in_specs=[VMEM] * (2 * len(blocks)),
        out_specs=[VMEM] * 2,
        compiler_params=PARAMS,
        cost_estimate=cost(4 * places * rows * cols, 2 * rows * cols),
        name="select",
    )(*blocks, *slots)


def norm_kernel(places_of, gain, *refs):
    n = len(places_of)
    pieces, out = refs[:n], refs[n]
    cols = pieces[0].shape[1]
    z, t = lax.axis_index("ctx"), lax.axis_index("tp")
    total = None
    for piece in pieces:
        wide = piece[...].astype(F32)
        part = jnp.sum(wide * wide, axis=1, keepdims=True)
        total = part if total is None else total + part
    scale = lax.rsqrt(total / (n * cols) + 1e-06)
    for (m, d), piece in zip(places_of, pieces):
        block = jnp.bitwise_xor(z, m) * 2 + jnp.bitwise_xor(t, d)
        at = pl.ds(pl.multiple_of(block * cols, cols), cols)
        out[:, at] = (piece[...].astype(F32) * scale * gain[:, at].astype(F32)).astype(out.dtype)


def norm(places_of, gain, pieces):
    n = len(pieces)
    places, cols = pieces[0].shape
    return pl.pallas_call(
        functools.partial(norm_kernel, places_of),
        out_shape=jax.ShapeDtypeStruct((places, n * cols), BF16),
        in_specs=[VMEM] * (n + 1),
        out_specs=VMEM,
        compiler_params=PARAMS,
        cost_estimate=cost(4 * places * n * cols, 4 * places * n * cols),
        name="norm",
    )(gain, *pieces)


def after(x, *others):
    return lax.optimization_barrier((x, *others))[0]


def body(enc_rows, row_slot, row_kind, audio_proj, frame_proj, audio_bias, frame_bias, norm_gain):
    n = lax.axis_size("ctx")
    rows = enc_rows[0]
    half = rows.shape[0] // 2
    weights = (audio_proj, frame_proj, audio_bias[None, :], frame_bias[None, :])

    def over_tp(x):
        return lax.ppermute(x, "tp", [(0, 1), (1, 0)])

    mine = to_send(rows, row_slot, row_kind)
    direct = [
        lax.ppermute(mine, "ctx", [(i, i ^ m) for i in range(n)]) for m in range(1, n)
    ]
    own = project_own(row_kind, rows, weights)
    blocks, slots, last = [own], [row_slot], own
    for k in range(n - 1):
        direct[k] = after(direct[k], last)
        block, slot = project_halves([direct[k]], weights)
        blocks.append(block)
        slots.append(slot)
        last = block
    swapped = [over_tp(x) for x in direct]
    for k in range(0, n - 1, 3):
        block, slot = project_halves(swapped[k : k + 3], weights)
        blocks.append(block)
        slots.append(slot)

    pieces, places_of = [], []
    for m in [1] + list(reversed(range(2, n))) + [0]:
        chosen = select(m, blocks, slots, half)
        slots[0] = after(slots[0], chosen[0])
        for d, piece in enumerate(chosen):
            if m or d:
                perm = [(i * 2 + c, (i ^ m) * 2 + (c ^ d)) for i in range(n) for c in range(2)]
                piece = lax.ppermute(piece, ("ctx", "tp"), perm)
            pieces.append(piece)
            places_of.append((m, d))
    return norm(tuple(places_of), norm_gain[None, :], pieces)[None]


def solution(mesh):
    return jax.shard_map(
        body,
        mesh=mesh,
        in_specs=(
            P(("groups", "enc"), "ctx", None),
            P(("groups", "enc"), "ctx"),
            P(("groups", "enc"), "ctx"),
            P(None, ("ctx", "tp")),
            P(None, ("ctx", "tp")),
            P(("ctx", "tp")),
            P(("ctx", "tp")),
            P(),
        ),
        out_specs=P(("groups", "enc"), ("ctx", "tp"), None),
        check_vma=False,
    )
```

```python
import functools

import jax
import jax.numpy as jnp
from jax import lax
from jax.experimental import pallas as pl
from jax.experimental.pallas import tpu as pltpu
from jax.sharding import PartitionSpec as P

VMEM = pl.BlockSpec(memory_space=pltpu.VMEM)
HBM = pl.BlockSpec(memory_space=pltpu.HBM)
PARAMS = pltpu.CompilerParams(vmem_limit_bytes=12 << 20)
BF16, F32, I32 = jnp.bfloat16, jnp.float32, jnp.int32


def cost(flops, moved):
    return pl.CostEstimate(flops=flops // 16, bytes_accessed=moved // 16, transcendentals=0)


def send_kernel(rows, slot, kind, out, slot_here, kind_here, sems):
    half = out.shape[0] - 8
    t = lax.axis_index("tp")
    start = pl.multiple_of(t * half, half)
    copies = [
        pltpu.make_async_copy(slot, slot_here, sems.at[0]),
        pltpu.make_async_copy(kind, kind_here, sems.at[1]),
        pltpu.make_async_copy(rows.at[pl.ds(start, half), :], out.at[pl.ds(0, half), :], sems.at[2]),
    ]
    for copy in copies:
        copy.start()
    out[half:, :] = jnp.zeros((8, out.shape[1]), BF16)
    for copy in copies:
        copy.wait()
    slots = jnp.where(t == 0, slot_here[:, :half], slot_here[:, half:])
    kinds = jnp.where(t == 0, kind_here[:, :half], kind_here[:, half:])
    line = lax.broadcasted_iota(I32, (8, half), 0)
    index = jnp.where(line == 0, slots // 256, jnp.where(line == 1, slots % 256, kinds))
    out[half:, :half] = index.astype(F32).astype(BF16)


def to_send(rows, slot, kind):
    half, width = rows.shape[0] // 2, rows.shape[1]
    return pl.pallas_call(
        send_kernel,
        out_shape=jax.ShapeDtypeStruct((half + 8, width), BF16),
        in_specs=[HBM] * 3,
        out_specs=VMEM,
        scratch_shapes=[
            pltpu.VMEM(slot.shape, I32),
            pltpu.VMEM(slot.shape, I32),
            pltpu.SemaphoreType.DMA((3,)),
        ],
        compiler_params=pltpu.CompilerParams(vmem_limit_bytes=60 << 20),
        cost_estimate=cost(0, 4 * half * width),
        name="to_send",
    )(rows, slot, kind)


def column_of(row_vector):
    r = row_vector.shape[1]
    diagonal = lax.broadcasted_iota(I32, (r, r), 0) == lax.broadcasted_iota(I32, (r, r), 1)
    return jnp.sum(jnp.where(diagonal, row_vector, 0), axis=1, keepdims=True)


def project(kind_row, x, w_audio, w_frame, b_audio, b_frame, out):
    is_audio = column_of(kind_row) == 0
    audio = jnp.dot(x, w_audio[...], preferred_element_type=F32)
    frame = jnp.dot(x, w_frame[...], preferred_element_type=F32)
    audio = audio + b_audio[...].astype(F32)
    frame = frame + b_frame[...].astype(F32)
    out[...] = jnp.where(is_audio, audio, frame).astype(out.dtype)


def project_own_kernel(kind, x, wa, wf, ba, bf, out):
    project(kind[...], x[...], wa, wf, ba, bf, out)


def project_own(kind, rows, weights):
    ew, cols = weights[0].shape
    return pl.pallas_call(
        project_own_kernel,
        out_shape=jax.ShapeDtypeStruct((rows.shape[0], cols), BF16),
        in_specs=[VMEM] * 6,
        out_specs=VMEM,
        compiler_params=PARAMS,
        cost_estimate=cost(4 * rows.shape[0] * ew * cols, 4 * ew * cols),
        name="project_own",
    )(kind, rows, *weights)


def is_in(z, members):
    found = z == members[0]
    for other in members[1:]:
        found = jnp.logical_or(found, z == other)
    return found


def project_halves_kernel(receivers, wa, wf, ba, bf, *refs):
    buffers, out, slots = list(refs[:-2]), refs[-2], refs[-1]
    half = buffers[0].shape[0] - 8
    z = lax.axis_index("ctx")
    x, index = [], []
    for choices in receivers:
        piece = buffers.pop(0)[...]
        for members in choices[1:]:
            piece = jnp.where(is_in(z, members), buffers.pop(0)[...], piece)
        x.append(piece[:half])
        index.append(piece[half:, :half].astype(F32).astype(I32))
    x = x[0] if len(x) == 1 else jnp.concatenate(x, axis=0)
    index = index[0] if len(index) == 1 else jnp.concatenate(index, axis=1)
    slots[...] = index[0:1] * 256 + index[1:2]
    project(index[2:3], x, wa, wf, ba, bf, out)


def project_halves(receivers, buffers, weights):
    rows, ew = len(receivers) * (buffers[0].shape[0] - 8), buffers[0].shape[1]
    cols = weights[0].shape[1]
    return pl.pallas_call(
        functools.partial(project_halves_kernel, receivers),
        out_shape=[jax.ShapeDtypeStruct((rows, cols), BF16), jax.ShapeDtypeStruct((1, rows), I32)],
        in_specs=[VMEM] * (4 + len(buffers)),
        out_specs=[VMEM] * 2,
        compiler_params=PARAMS,
        cost_estimate=cost(4 * rows * ew * cols, 4 * ew * cols),
        name="project_halves",
    )(*weights, *buffers)


def select_kernel(m, count, *refs):
    blocks, slots, outs = refs[:count], refs[count : 2 * count], refs[-2:]
    places = outs[0].shape[0]
    z, t = lax.axis_index("ctx"), lax.axis_index("tp")
    first = jnp.bitwise_xor(z, m) * 2 * places
    i = lax.broadcasted_iota(I32, (2 * places, 1), 0)
    position = first + jnp.bitwise_xor(i, t * places)
    total = None
    for block, slot in zip(blocks, slots):
        chosen = (slot[...] == position).astype(F32).astype(BF16)
        part = jnp.dot(chosen, block[...], preferred_element_type=F32)
        total = part if total is None else total + part
    outs[0][...] = total[:places].astype(BF16)
    outs[1][...] = total[places:].astype(BF16)


def select(m, blocks, slots, places):
    rows, cols = sum(b.shape[0] for b in blocks), blocks[0].shape[1]
    return pl.pallas_call(
        functools.partial(select_kernel, m, len(blocks)),
        out_shape=[jax.ShapeDtypeStruct((places, cols), BF16)] * 2,
        in_specs=[VMEM] * (2 * len(blocks)),
        out_specs=[VMEM] * 2,
        compiler_params=PARAMS,
        cost_estimate=cost(4 * places * rows * cols, 2 * rows * cols),
        name="select",
    )(*blocks, *slots)


def squares_kernel(*refs):
    pieces, out = refs[:-1], refs[-1]
    total = None
    for piece in pieces:
        if piece.dtype == F32:
            part = piece[...]
        else:
            wide = piece[...].astype(F32)
            part = jnp.sum(wide * wide, axis=1, keepdims=True)
        total = part if total is None else total + part
    out[...] = total


def squares(total, pieces):
    operands = pieces if total is None else [total] + pieces
    places, cols = pieces[0].shape
    return pl.pallas_call(
        squares_kernel,
        out_shape=jax.ShapeDtypeStruct((places, 1), F32),
        in_specs=[VMEM] * len(operands),
        out_specs=VMEM,
        compiler_params=PARAMS,
        cost_estimate=cost(1 << 36, 1 << 26),
        name="squares",
    )(*operands)


def norm_kernel(places_of, fresh, gain, before, *refs):
    n = len(places_of)
    pieces, out = refs[:n], refs[n]
    cols = pieces[0].shape[1]
    z, t = lax.axis_index("ctx"), lax.axis_index("tp")
    total = before[...]
    for k in fresh:
        wide = pieces[k][...].astype(F32)
        total = total + jnp.sum(wide * wide, axis=1, keepdims=True)
    scale = lax.rsqrt(total / (n * cols) + 1e-06)
    for (m, d), piece in zip(places_of, pieces):
        block = jnp.bitwise_xor(z, m) * 2 + jnp.bitwise_xor(t, d)
        at = pl.ds(pl.multiple_of(block * cols, cols), cols)
        out[:, at] = (piece[...].astype(F32) * scale * gain[:, at].astype(F32)).astype(out.dtype)


def norm(places_of, fresh, gain, before, pieces):
    n = len(pieces)
    places, cols = pieces[0].shape
    return pl.pallas_call(
        functools.partial(norm_kernel, places_of, fresh),
        out_shape=jax.ShapeDtypeStruct((places, n * cols), BF16),
        in_specs=[VMEM] * (n + 2),
        out_specs=VMEM,
        compiler_params=PARAMS,
        cost_estimate=cost(4 * places * n * cols, 4 * places * n * cols),
        name="norm",
    )(gain, before, *pieces)


def after(x, *others):
    return lax.optimization_barrier((x, *others))[0]


def gather_stages(n):
    everyone = tuple(range(n))
    if n == 4:
        ends, middle = (0, 3), (1, 2)
        first = (
            [
                ("near", [(0, 1), (1, 0), (2, 3), (3, 2)], "own"),
                ("middle", [(1, 2), (2, 1)], "own"),
                ("ends", [(0, 3), (3, 0)], "own"),
            ],
            [[("near", everyone)], [("ends", ends), ("middle", middle)]],
        )
        second = (
            [("forward", [(1, 0), (2, 3)], "middle"), ("skip", [(0, 2), (3, 1)], "own")],
            [[("forward", ends), ("skip", middle)]],
        )
        return [first, second]
    messages = [(m, [(i, i ^ m) for i in range(n)], "own") for m in range(1, n)]
    return [(messages, [[(m, everyone)] for m in range(1, n)])]


def body(enc_rows, row_slot, row_kind, audio_proj, frame_proj, audio_bias, frame_bias, norm_gain):
    n = lax.axis_size("ctx")
    rows = enc_rows[0]
    half = rows.shape[0] // 2
    weights = (audio_proj, frame_proj, audio_bias[None, :], frame_bias[None, :])

    held = {"own": to_send(rows, row_slot, row_kind)}
    blocks, slots, last = [], [], None
    for messages, wanted in gather_stages(n):
        names = [name for name, _, _ in messages]
        arrived = [lax.ppermute(held[carried], "ctx", pairs) for _, pairs, carried in messages]
        if last is None:
            last = [project_own(row_kind, rows, weights)]
            blocks += last
            slots.append(row_slot)
        arrived = lax.optimization_barrier((*arrived, *last))[: len(arrived)]
        held.update(zip(names, arrived))
        direct, swapped, receivers = [], [], []
        for choices in wanted:
            receivers.append(tuple(members for _, members in choices))
            for name, members in choices:
                swap = [(i * 2 + c, i * 2 + 1 - c) for i in members for c in range(2)]
                direct.append([held[name]])
                swapped.append([lax.ppermute(held[name], ("ctx", "tp"), swap)])
        direct = [x for group in direct for x in group]
        swapped = [x for group in swapped for x in group]
        for buffers in (direct, swapped):
            at = 0
            for k in range(0, len(receivers), 3):
                group = tuple(receivers[k : k + 3])
                count = sum(len(choices) for choices in group)
                block, slot = project_halves(group, buffers[at : at + count], weights)
                at += count
                blocks.append(block)
                slots.append(slot)
        last = blocks[1:]

    order = [n - 1, 1] + list(reversed(range(2, n - 1))) + [0]
    pieces = {}
    for m in order:
        chosen = select(m, blocks, slots, half)
        slots[0] = after(slots[0], chosen[0])
        for d, piece in enumerate(chosen):
            if m or d:
                perm = [(i * 2 + c, (i ^ m) * 2 + (c ^ d)) for i in range(n) for c in range(2)]
                piece = lax.ppermute(piece, ("ctx", "tp"), perm)
            pieces[m, d] = piece

    total = None
    for m in order[:-2]:
        fresh = [pieces[m, 0], pieces[m, 1]]
        if total is None:
            fresh += [pieces[0, 0], pieces[0, 1]]
        else:
            fresh = [after(piece, total) for piece in fresh]
        total = squares(total, fresh)
    places_of = tuple((m, d) for m in order for d in range(2))
    fresh = tuple(k for k, (m, _) in enumerate(places_of) if m == order[-2])
    final = [pieces[at] for at in places_of]
    for k in fresh:
        final[k] = after(final[k], total)
    return norm(places_of, fresh, norm_gain[None, :], total, final)[None]


def solution(mesh):
    return jax.shard_map(
        body,
        mesh=mesh,
        in_specs=(
            P(("groups", "enc"), "ctx", None),
            P(("groups", "enc"), "ctx"),
            P(("groups", "enc"), "ctx"),
            P(None, ("ctx", "tp")),
            P(None, ("ctx", "tp")),
            P(("ctx", "tp")),
            P(("ctx", "tp")),
            P(),
        ),
        out_specs=P(("groups", "enc"), ("ctx", "tp"), None),
        check_vma=False,
    )
```

```python
import functools

import jax
import jax.numpy as jnp
from jax import lax
from jax.experimental import pallas as pl
from jax.experimental.pallas import tpu as pltpu
from jax.sharding import PartitionSpec as P

VMEM = pl.BlockSpec(memory_space=pltpu.VMEM)
HBM = pl.BlockSpec(memory_space=pltpu.HBM)
PARAMS = pltpu.CompilerParams(vmem_limit_bytes=12 << 20)
BF16, F32, I32 = jnp.bfloat16, jnp.float32, jnp.int32


def cost(flops, moved):
    return pl.CostEstimate(flops=flops // 16, bytes_accessed=moved // 16, transcendentals=0)


def send_kernel(rows, slot, kind, out, slot_here, kind_here, sems):
    half = out.shape[0] - 8
    t = lax.axis_index("tp")
    start = pl.multiple_of(t * half, half)
    copies = [
        pltpu.make_async_copy(slot, slot_here, sems.at[0]),
        pltpu.make_async_copy(kind, kind_here, sems.at[1]),
        pltpu.make_async_copy(rows.at[pl.ds(start, half), :], out.at[pl.ds(0, half), :], sems.at[2]),
    ]
    for copy in copies:
        copy.start()
    out[half:, :] = jnp.zeros((8, out.shape[1]), BF16)
    for copy in copies:
        copy.wait()
    slots = jnp.where(t == 0, slot_here[:, :half], slot_here[:, half:])
    kinds = jnp.where(t == 0, kind_here[:, :half], kind_here[:, half:])
    line = lax.broadcasted_iota(I32, (8, half), 0)
    index = jnp.where(line == 0, slots // 256, jnp.where(line == 1, slots % 256, kinds))
    out[half:, :half] = index.astype(F32).astype(BF16)


def to_send(rows, slot, kind):
    half, width = rows.shape[0] // 2, rows.shape[1]
    return pl.pallas_call(
        send_kernel,
        out_shape=jax.ShapeDtypeStruct((half + 8, width), BF16),
        in_specs=[HBM] * 3,
        out_specs=VMEM,
        scratch_shapes=[
            pltpu.VMEM(slot.shape, I32),
            pltpu.VMEM(slot.shape, I32),
            pltpu.SemaphoreType.DMA((3,)),
        ],
        compiler_params=pltpu.CompilerParams(vmem_limit_bytes=60 << 20),
        cost_estimate=cost(0, 4 * half * width),
        name="to_send",
    )(rows, slot, kind)


def column_of(row_vector):
    r = row_vector.shape[1]
    diagonal = lax.broadcasted_iota(I32, (r, r), 0) == lax.broadcasted_iota(I32, (r, r), 1)
    return jnp.sum(jnp.where(diagonal, row_vector, 0), axis=1, keepdims=True)


def project(kind_row, x, w_audio, w_frame, b_audio, b_frame, out):
    is_audio = column_of(kind_row) == 0
    audio = jnp.dot(x, w_audio[...], preferred_element_type=F32)
    frame = jnp.dot(x, w_frame[...], preferred_element_type=F32)
    audio = audio + b_audio[...].astype(F32)
    frame = frame + b_frame[...].astype(F32)
    out[...] = jnp.where(is_audio, audio, frame).astype(out.dtype)


def project_own_kernel(kind, x, wa, wf, ba, bf, out):
    project(kind[...], x[...], wa, wf, ba, bf, out)


def project_own(kind, rows, weights):
    ew, cols = weights[0].shape
    return pl.pallas_call(
        project_own_kernel,
        out_shape=jax.ShapeDtypeStruct((rows.shape[0], cols), BF16),
        in_specs=[VMEM] * 6,
        out_specs=VMEM,
        compiler_params=PARAMS,
        cost_estimate=cost(4 * rows.shape[0] * ew * cols, 4 * ew * cols),
        name="project_own",
    )(kind, rows, *weights)


def project_halves_kernel(wa, wf, ba, bf, *refs):
    pieces, out, slots = refs[:-2], refs[-2], refs[-1]
    x, index = [], []
    for piece in pieces:
        half = piece.shape[-2] - 8
        for k in range(piece.shape[0]):
            x.append(piece[k, :half, :])
            index.append(piece[k, half:, :half].astype(F32).astype(I32))
    x = x[0] if len(x) == 1 else jnp.concatenate(x, axis=0)
    index = index[0] if len(index) == 1 else jnp.concatenate(index, axis=1)
    slots[...] = index[0:1] * 256 + index[1:2]
    project(index[2:3], x, wa, wf, ba, bf, out)


def project_halves(pieces, weights):
    rows, ew = sum(p.shape[0] * (p.shape[1] - 8) for p in pieces), pieces[0].shape[2]
    cols = weights[0].shape[1]
    return pl.pallas_call(
        project_halves_kernel,
        out_shape=[jax.ShapeDtypeStruct((rows, cols), BF16), jax.ShapeDtypeStruct((1, rows), I32)],
        in_specs=[VMEM] * (4 + len(pieces)),
        out_specs=[VMEM] * 2,
        compiler_params=PARAMS,
        cost_estimate=cost(4 * rows * ew * cols, 4 * ew * cols),
        name="project_halves",
    )(*weights, *pieces)


def select_kernel(m, count, *refs):
    blocks, slots, outs = refs[:count], refs[count : 2 * count], refs[2 * count :]
    places = sum(out.shape[0] for out in outs) // 2
    z, t = lax.axis_index("ctx"), lax.axis_index("tp")
    first = jnp.bitwise_xor(z, m) * 2 * places
    i = lax.broadcasted_iota(I32, (2 * places, 1), 0)
    position = first + jnp.bitwise_xor(i, t * places)
    total = None
    for block, slot in zip(blocks, slots):
        chosen = (slot[...] == position).astype(F32).astype(BF16)
        part = jnp.dot(chosen, block[...], preferred_element_type=F32)
        total = part if total is None else total + part
    at = 0
    for out in outs:
        out[...] = total[at : at + out.shape[0]].astype(BF16)
        at += out.shape[0]


def select(m, blocks, slots, sizes):
    rows, cols = sum(b.shape[0] for b in blocks), blocks[0].shape[1]
    return pl.pallas_call(
        functools.partial(select_kernel, m, len(blocks)),
        out_shape=[jax.ShapeDtypeStruct((size, cols), BF16) for size in sizes],
        in_specs=[VMEM] * (2 * len(blocks)),
        out_specs=[VMEM] * len(sizes),
        compiler_params=PARAMS,
        cost_estimate=cost(2 * sum(sizes) * rows * cols, 2 * rows * cols),
        name="select",
    )(*blocks, *slots)


def view(ref, places):
    if len(ref.shape) == 3:
        return ref.at[1 - lax.axis_index("tp")]
    return ref.at[pl.ds(0, places), :]


def square_sum(piece):
    wide = piece[...].astype(F32)
    return jnp.sum(wide * wide, axis=1, keepdims=True)


def squares_kernel(*refs):
    out = refs[-1]
    total = None
    for ref in refs[:-1]:
        part = ref[...] if ref.dtype == F32 else square_sum(view(ref, out.shape[0]))
        total = part if total is None else total + part
    out[...] = total


def squares(total, pieces, places):
    operands = pieces if total is None else [total] + pieces
    return pl.pallas_call(
        squares_kernel,
        out_shape=jax.ShapeDtypeStruct((places, 1), F32),
        in_specs=[VMEM] * len(operands),
        out_specs=VMEM,
        compiler_params=PARAMS,
        cost_estimate=cost(1 << 36, 1 << 26),
        name="squares",
    )(*operands)


def norm_kernel(places_of, fresh, gain, before, *refs):
    n = len(places_of)
    out, scaled, sems = refs[n], refs[n + 1], refs[n + 2]
    places, cols = scaled.shape[1:]
    pieces = [view(ref, places) for ref in refs[:n]]
    z, t = lax.axis_index("ctx"), lax.axis_index("tp")
    total = before[...]
    for k in fresh:
        total = total + square_sum(pieces[k])
    scale = lax.rsqrt(total / (n * cols) + 1e-06)
    copies = []
    for k, ((m, d), piece) in enumerate(zip(places_of, pieces)):
        block = jnp.bitwise_xor(z, m) * 2 + jnp.bitwise_xor(t, d)
        at = pl.ds(pl.multiple_of(block * cols, cols), cols)
        scaled[k] = (piece[...].astype(F32) * scale * gain[:, at].astype(F32)).astype(BF16)
        copies.append(pltpu.make_async_copy(scaled.at[k], out.at[:, at], sems.at[k]))
        copies[k].start()
    for copy in copies:
        copy.wait()


def norm(places_of, fresh, gain, before, pieces):
    n, places, cols = len(pieces), before.shape[0], pieces[0].shape[-1]
    return pl.pallas_call(
        functools.partial(norm_kernel, places_of, fresh),
        out_shape=jax.ShapeDtypeStruct((places, n * cols), BF16),
        in_specs=[VMEM] * (n + 2),
        out_specs=HBM,
        scratch_shapes=[pltpu.VMEM((n, places, cols), BF16), pltpu.SemaphoreType.DMA((n,))],
        compiler_params=PARAMS,
        cost_estimate=cost(4 * places * n * cols, 4 * places * n * cols),
        name="norm",
    )(gain, before, *pieces)


def after(x, *others):
    return lax.optimization_barrier((x, *others))[0]


def body(enc_rows, row_slot, row_kind, audio_proj, frame_proj, audio_bias, frame_bias, norm_gain):
    n = lax.axis_size("ctx")
    rows = enc_rows[0]
    half = rows.shape[0] // 2
    weights = (audio_proj, frame_proj, audio_bias[None, :], frame_bias[None, :])

    def over_ctx(x, m):
        return lax.ppermute(x, "ctx", [(i, i ^ m) for i in range(n)])

    def over_tp(x):
        return lax.ppermute(x, "tp", [(0, 1), (1, 0)])

    mine = to_send(rows, row_slot, row_kind)
    arrived = [over_ctx(mine, m) for m in range(1, n)]
    last = project_own(row_kind, rows, weights)
    blocks, slots = [last], [row_slot]
    for k, direct in enumerate(arrived):
        direct = after(direct, last)
        if k < n - 2:
            both = [lax.all_gather(direct, "tp", axis=0)]
        else:
            both = [direct[None], over_tp(direct)[None]]
        groups = [both] if len(both) == 1 else [[half] for half in both]
        for group in groups:
            block, slot = project_halves(group, weights)
            blocks.append(block)
            slots.append(slot)
        last = block

    pieces = {}
    order = [n - 1, 1] + list(reversed(range(2, n - 1))) + [0]
    for m in order:
        chosen = select(m, blocks, slots, [2 * half] if m == 1 else [half, half])
        slots[0] = after(slots[0], chosen[0])
        if m == 1:
            pieces[m] = over_ctx(chosen[0], m)
            continue
        for d, piece in enumerate(chosen):
            if m or d:
                perm = [(i * 2 + c, (i ^ m) * 2 + (c ^ d)) for i in range(n) for c in range(2)]
                piece = lax.ppermute(piece, ("ctx", "tp"), perm)
            pieces[m, d] = piece

    total = squares(None, [pieces[0, 0], pieces[0, 1]], half)
    for m in order[:-2]:
        if m == 1:
            pair = after(pieces[m], total)
            pieces[m, 0], pieces[m, 1] = pair, lax.all_gather(pair[half:], "tp", axis=0)
        fresh = [pieces[m, 0], pieces[m, 1]]
        if m != 1:
            fresh = [after(piece, total) for piece in fresh]
        total = squares(total, fresh, half)
    places_of = tuple((m, d) for m in order for d in range(2))
    fresh = tuple(k for k, (m, _) in enumerate(places_of) if m == order[-2])
    final = [pieces[at] for at in places_of]
    for k in fresh:
        final[k] = after(final[k], total)
    return norm(places_of, fresh, norm_gain[None, :], total, final)[None]


def solution(mesh):
    return jax.shard_map(
        body,
        mesh=mesh,
        in_specs=(
            P(("groups", "enc"), "ctx", None),
            P(("groups", "enc"), "ctx"),
            P(("groups", "enc"), "ctx"),
            P(None, ("ctx", "tp")),
            P(None, ("ctx", "tp")),
            P(("ctx", "tp")),
            P(("ctx", "tp")),
            P(),
        ),
        out_specs=P(("groups", "enc"), ("ctx", "tp"), None),
        check_vma=False,
    )
```

```python
import functools

import jax
import jax.numpy as jnp
from jax import lax
from jax.experimental import pallas as pl
from jax.experimental.pallas import tpu as pltpu
from jax.sharding import PartitionSpec as P

VMEM = pl.BlockSpec(memory_space=pltpu.VMEM)
HBM = pl.BlockSpec(memory_space=pltpu.HBM)
PARAMS = pltpu.CompilerParams(vmem_limit_bytes=12 << 20)
BF16, F32, I32 = jnp.bfloat16, jnp.float32, jnp.int32


def cost(flops, moved):
    return pl.CostEstimate(flops=flops // 16, bytes_accessed=moved // 16, transcendentals=0)


def send_kernel(rows, slot, kind, out, slot_here, kind_here, sems):
    half = out.shape[0] - 8
    t = lax.axis_index("tp")
    start = pl.multiple_of(t * half, half)
    copies = [
        pltpu.make_async_copy(slot, slot_here, sems.at[0]),
        pltpu.make_async_copy(kind, kind_here, sems.at[1]),
        pltpu.make_async_copy(rows.at[pl.ds(start, half), :], out.at[pl.ds(0, half), :], sems.at[2]),
    ]
    for copy in copies:
        copy.start()
    out[half:, :] = jnp.zeros((8, out.shape[1]), BF16)
    for copy in copies:
        copy.wait()
    slots = jnp.where(t == 0, slot_here[:, :half], slot_here[:, half:])
    kinds = jnp.where(t == 0, kind_here[:, :half], kind_here[:, half:])
    line = lax.broadcasted_iota(I32, (8, half), 0)
    index = jnp.where(line == 0, slots // 256, jnp.where(line == 1, slots % 256, kinds))
    out[half:, :half] = index.astype(F32).astype(BF16)


def to_send(rows, slot, kind):
    half, width = rows.shape[0] // 2, rows.shape[1]
    return pl.pallas_call(
        send_kernel,
        out_shape=jax.ShapeDtypeStruct((half + 8, width), BF16),
        in_specs=[HBM] * 3,
        out_specs=VMEM,
        scratch_shapes=[
            pltpu.VMEM(slot.shape, I32),
            pltpu.VMEM(slot.shape, I32),
            pltpu.SemaphoreType.DMA((3,)),
        ],
        compiler_params=pltpu.CompilerParams(vmem_limit_bytes=60 << 20),
        cost_estimate=cost(0, 4 * half * width),
        name="to_send",
    )(rows, slot, kind)


def column_of(row_vector):
    r = row_vector.shape[1]
    diagonal = lax.broadcasted_iota(I32, (r, r), 0) == lax.broadcasted_iota(I32, (r, r), 1)
    return jnp.sum(jnp.where(diagonal, row_vector, 0), axis=1, keepdims=True)


def project(kind_row, x, w_audio, w_frame, b_audio, b_frame, out):
    is_audio = column_of(kind_row) == 0
    audio = jnp.dot(x, w_audio[...], preferred_element_type=F32)
    frame = jnp.dot(x, w_frame[...], preferred_element_type=F32)
    audio = audio + b_audio[...].astype(F32)
    frame = frame + b_frame[...].astype(F32)
    out[...] = jnp.where(is_audio, audio, frame).astype(out.dtype)


def project_own_kernel(kind, x, wa, wf, ba, bf, out):
    project(kind[...], x[...], wa, wf, ba, bf, out)


def project_own(kind, rows, weights):
    ew, cols = weights[0].shape
    return pl.pallas_call(
        project_own_kernel,
        out_shape=jax.ShapeDtypeStruct((rows.shape[0], cols), BF16),
        in_specs=[VMEM] * 6,
        out_specs=VMEM,
        compiler_params=PARAMS,
        cost_estimate=cost(4 * rows.shape[0] * ew * cols, 4 * ew * cols),
        name="project_own",
    )(kind, rows, *weights)


def project_halves_kernel(wa, wf, ba, bf, *refs):
    pieces, out, slots = refs[:-2], refs[-2], refs[-1]
    x, index = [], []
    for piece in pieces:
        half = piece.shape[-2] - 8
        for k in range(piece.shape[0]):
            x.append(piece[k, :half, :])
            index.append(piece[k, half:, :half].astype(F32).astype(I32))
    x = x[0] if len(x) == 1 else jnp.concatenate(x, axis=0)
    index = index[0] if len(index) == 1 else jnp.concatenate(index, axis=1)
    slots[...] = index[0:1] * 256 + index[1:2]
    project(index[2:3], x, wa, wf, ba, bf, out)


def project_halves(pieces, weights):
    rows, ew = sum(p.shape[0] * (p.shape[1] - 8) for p in pieces), pieces[0].shape[2]
    cols = weights[0].shape[1]
    return pl.pallas_call(
        project_halves_kernel,
        out_shape=[jax.ShapeDtypeStruct((rows, cols), BF16), jax.ShapeDtypeStruct((1, rows), I32)],
        in_specs=[VMEM] * (4 + len(pieces)),
        out_specs=[VMEM] * 2,
        compiler_params=PARAMS,
        cost_estimate=cost(4 * rows * ew * cols, 4 * ew * cols),
        name="project_halves",
    )(*weights, *pieces)


def select_kernel(m, count, *refs):
    blocks, slots, outs = refs[:count], refs[count : 2 * count], refs[2 * count :]
    places = sum(out.shape[0] for out in outs) // 2
    z, t = lax.axis_index("ctx"), lax.axis_index("tp")
    first = jnp.bitwise_xor(z, m) * 2 * places
    i = lax.broadcasted_iota(I32, (2 * places, 1), 0)
    position = first + jnp.bitwise_xor(i, t * places)
    total = None
    for block, slot in zip(blocks, slots):
        chosen = (slot[...] == position).astype(F32).astype(BF16)
        part = jnp.dot(chosen, block[...], preferred_element_type=F32)
        total = part if total is None else total + part
    at = 0
    for out in outs:
        out[...] = total[at : at + out.shape[0]].astype(BF16)
        at += out.shape[0]


def select(m, blocks, slots, sizes):
    rows, cols = sum(b.shape[0] for b in blocks), blocks[0].shape[1]
    return pl.pallas_call(
        functools.partial(select_kernel, m, len(blocks)),
        out_shape=[jax.ShapeDtypeStruct((size, cols), BF16) for size in sizes],
        in_specs=[VMEM] * (2 * len(blocks)),
        out_specs=[VMEM] * len(sizes),
        compiler_params=PARAMS,
        cost_estimate=cost(2 * sum(sizes) * rows * cols, 2 * rows * cols),
        name="select",
    )(*blocks, *slots)


def view(ref, places):
    if len(ref.shape) == 3:
        return ref.at[1 - lax.axis_index("tp")]
    return ref.at[pl.ds(0, places), :]


def square_sum(piece):
    wide = piece[...].astype(F32)
    return jnp.sum(wide * wide, axis=1, keepdims=True)


def squares_kernel(*refs):
    out = refs[-1]
    total = None
    for ref in refs[:-1]:
        part = ref[...] if ref.dtype == F32 else square_sum(view(ref, out.shape[0]))
        total = part if total is None else total + part
    out[...] = total


def squares(total, pieces, places):
    operands = pieces if total is None else [total] + pieces
    return pl.pallas_call(
        squares_kernel,
        out_shape=jax.ShapeDtypeStruct((places, 1), F32),
        in_specs=[VMEM] * len(operands),
        out_specs=VMEM,
        compiler_params=PARAMS,
        cost_estimate=cost(1 << 36, 1 << 26),
        name="squares",
    )(*operands)


def norm_kernel(places_of, fresh, gain, before, *refs):
    n = len(places_of)
    out, scaled, sems = refs[n], refs[n + 1], refs[n + 2]
    places, cols = scaled.shape[1:]
    pieces = [view(ref, places) for ref in refs[:n]]
    z, t = lax.axis_index("ctx"), lax.axis_index("tp")
    total = before[...]
    for k in fresh:
        total = total + square_sum(pieces[k])
    scale = lax.rsqrt(total / (n * cols) + 1e-06)
    copies = []
    for k, ((m, d), piece) in enumerate(zip(places_of, pieces)):
        block = jnp.bitwise_xor(z, m) * 2 + jnp.bitwise_xor(t, d)
        at = pl.ds(pl.multiple_of(block * cols, cols), cols)
        scaled[k] = (piece[...].astype(F32) * scale * gain[:, at].astype(F32)).astype(BF16)
        copies.append(pltpu.make_async_copy(scaled.at[k], out.at[:, at], sems.at[k]))
        copies[k].start()
    for copy in copies:
        copy.wait()


def norm(places_of, fresh, gain, before, pieces):
    n, places, cols = len(pieces), before.shape[0], pieces[0].shape[-1]
    return pl.pallas_call(
        functools.partial(norm_kernel, places_of, fresh),
        out_shape=jax.ShapeDtypeStruct((places, n * cols), BF16),
        in_specs=[VMEM] * (n + 2),
        out_specs=HBM,
        scratch_shapes=[pltpu.VMEM((n, places, cols), BF16), pltpu.SemaphoreType.DMA((n,))],
        compiler_params=PARAMS,
        cost_estimate=cost(4 * places * n * cols, 4 * places * n * cols),
        name="norm",
    )(gain, before, *pieces)


def after(x, *others):
    return lax.optimization_barrier((x, *others))[0]


def body(enc_rows, row_slot, row_kind, audio_proj, frame_proj, audio_bias, frame_bias, norm_gain):
    n = lax.axis_size("ctx")
    rows = enc_rows[0]
    half = rows.shape[0] // 2
    weights = (audio_proj, frame_proj, audio_bias[None, :], frame_bias[None, :])

    def over_ctx(x, m):
        return lax.ppermute(x, "ctx", [(i, i ^ m) for i in range(n)])

    def over_tp(x):
        return lax.ppermute(x, "tp", [(0, 1), (1, 0)])

    mine = to_send(rows, row_slot, row_kind)
    arrived = [over_ctx(mine, m) for m in range(1, n)]
    last = project_own(row_kind, rows, weights)
    blocks, slots = [last], [row_slot]
    for k, direct in enumerate(arrived):
        direct = after(direct, last)
        if k < n - 2:
            both = [lax.all_gather(direct, "tp", axis=0)]
        else:
            both = [direct[None], over_tp(direct)[None]]
        groups = [both] if len(both) == 1 else [[half] for half in both]
        for group in groups:
            block, slot = project_halves(group, weights)
            blocks.append(block)
            slots.append(slot)
        last = block

    pieces = {}
    order = [n - 1, 1] + list(reversed(range(2, n - 1)))
    for m in order:
        chosen = select(m, blocks, slots, [2 * half] if m == 1 else [half, half])
        slots[0] = after(slots[0], chosen[0])
        if m == 1:
            pieces[m] = over_ctx(chosen[0], m)
            continue
        for d, piece in enumerate(chosen):
            perm = [(i * 2 + c, (i ^ m) * 2 + (c ^ d)) for i in range(n) for c in range(2)]
            pieces[m, d] = lax.ppermute(piece, ("ctx", "tp"), perm)

    total = None
    for m in order[:-1]:
        if m == 1:
            slots[0] = after(slots[0], total)
            pieces[0, 0], other = select(0, blocks, slots, [half, half])
            pieces[0, 1] = lax.all_gather(other, "tp", axis=0)
            total = squares(total, [pieces[0, 0], pieces[0, 1]], half)
            pair = after(pieces[m], total)
            pieces[m, 0], pieces[m, 1] = pair, lax.all_gather(pair[half:], "tp", axis=0)
        fresh = [pieces[m, 0], pieces[m, 1]]
        if m != 1 and total is not None:
            fresh = [after(piece, total) for piece in fresh]
        total = squares(total, fresh, half)
    order.append(0)
    places_of = tuple((m, d) for m in order for d in range(2))
    fresh = tuple(k for k, (m, _) in enumerate(places_of) if m == order[-2])
    final = [pieces[at] for at in places_of]
    for k in fresh:
        final[k] = after(final[k], total)
    return norm(places_of, fresh, norm_gain[None, :], total, final)[None]


def solution(mesh):
    return jax.shard_map(
        body,
        mesh=mesh,
        in_specs=(
            P(("groups", "enc"), "ctx", None),
            P(("groups", "enc"), "ctx"),
            P(("groups", "enc"), "ctx"),
            P(None, ("ctx", "tp")),
            P(None, ("ctx", "tp")),
            P(("ctx", "tp")),
            P(("ctx", "tp")),
            P(),
        ),
        out_specs=P(("groups", "enc"), ("ctx", "tp"), None),
        check_vma=False,
    )
```

```python
import functools

import jax
import jax.numpy as jnp
from jax import lax
from jax.experimental import pallas as pl
from jax.experimental.pallas import tpu as pltpu
from jax.sharding import PartitionSpec as P

VMEM = pl.BlockSpec(memory_space=pltpu.VMEM)
HBM = pl.BlockSpec(memory_space=pltpu.HBM)
PARAMS = pltpu.CompilerParams(vmem_limit_bytes=12 << 20)
BF16, F32, I32 = jnp.bfloat16, jnp.float32, jnp.int32


def cost(flops, moved):
    return pl.CostEstimate(flops=flops // 16, bytes_accessed=moved // 16, transcendentals=0)


def send_kernel(cuts, rows, slot, kind, *refs):
    outs, slot_here, kind_here, sems = refs[:-3], refs[-3], refs[-2], refs[-1]
    whole = rows.shape[0]
    z, t = lax.axis_index("ctx"), lax.axis_index("tp")
    copies = [
        pltpu.make_async_copy(slot, slot_here, sems.at[0]),
        pltpu.make_async_copy(kind, kind_here, sems.at[1]),
    ]
    parts = []
    for k, (out, parity) in enumerate(zip(outs, cuts)):
        size = out.shape[0] - 8
        part = t if parity is None else 2 * t + lax.rem(z + parity, 2)
        parts.append(part)
        source = rows.at[pl.ds(pl.multiple_of(part * size, size), size), :]
        copies.append(pltpu.make_async_copy(source, out.at[pl.ds(0, size), :], sems.at[2 + k]))
    for copy in copies:
        copy.start()
    for out in outs:
        out[out.shape[0] - 8 :, :] = jnp.zeros((8, out.shape[1]), BF16)
    for copy in copies:
        copy.wait()
    slots, kinds = slot_here[...], kind_here[...]
    for out, part in zip(outs, parts):
        size = out.shape[0] - 8
        s, k = slots[:, :size], kinds[:, :size]
        for i in range(1, whole // size):
            s = jnp.where(part == i, slots[:, i * size : (i + 1) * size], s)
            k = jnp.where(part == i, kinds[:, i * size : (i + 1) * size], k)
        line = lax.broadcasted_iota(I32, (8, size), 0)
        index = jnp.where(line == 0, s // 256, jnp.where(line == 1, s % 256, k))
        out[size:, :size] = index.astype(F32).astype(BF16)


def to_send(cuts, rows, slot, kind):
    half, width = rows.shape[0] // 2, rows.shape[1]
    sizes = [half if parity is None else half // 2 for parity in cuts]
    return pl.pallas_call(
        functools.partial(send_kernel, cuts),
        out_shape=[jax.ShapeDtypeStruct((size + 8, width), BF16) for size in sizes],
        in_specs=[HBM] * 3,
        out_specs=[VMEM] * len(cuts),
        scratch_shapes=[
            pltpu.VMEM(slot.shape, I32),
            pltpu.VMEM(slot.shape, I32),
            pltpu.SemaphoreType.DMA((2 + len(cuts),)),
        ],
        compiler_params=pltpu.CompilerParams(vmem_limit_bytes=60 << 20),
        cost_estimate=cost(0, 4 * half * width),
        name="to_send",
    )(rows, slot, kind)


def column_of(row_vector):
    r = row_vector.shape[1]
    diagonal = lax.broadcasted_iota(I32, (r, r), 0) == lax.broadcasted_iota(I32, (r, r), 1)
    return jnp.sum(jnp.where(diagonal, row_vector, 0), axis=1, keepdims=True)


def project(kind_row, x, w_audio, w_frame, b_audio, b_frame, out):
    is_audio = column_of(kind_row) == 0
    audio = jnp.dot(x, w_audio[...], preferred_element_type=F32)
    frame = jnp.dot(x, w_frame[...], preferred_element_type=F32)
    audio = audio + b_audio[...].astype(F32)
    frame = frame + b_frame[...].astype(F32)
    out[...] = jnp.where(is_audio, audio, frame).astype(out.dtype)


def project_own_kernel(kind, x, wa, wf, ba, bf, out):
    project(kind[...], x[...], wa, wf, ba, bf, out)


def project_own(kind, rows, weights):
    ew, cols = weights[0].shape
    return pl.pallas_call(
        project_own_kernel,
        out_shape=jax.ShapeDtypeStruct((rows.shape[0], cols), BF16),
        in_specs=[VMEM] * 6,
        out_specs=VMEM,
        compiler_params=PARAMS,
        cost_estimate=cost(4 * rows.shape[0] * ew * cols, 4 * ew * cols),
        name="project_own",
    )(kind, rows, *weights)


def project_halves_kernel(wa, wf, ba, bf, *refs):
    pieces, out, slots = refs[:-2], refs[-2], refs[-1]
    x, index = [], []
    for piece in pieces:
        half = piece.shape[-2] - 8
        for k in range(piece.shape[0]):
            x.append(piece[k, :half, :])
            index.append(piece[k, half:, :half].astype(F32).astype(I32))
    x = x[0] if len(x) == 1 else jnp.concatenate(x, axis=0)
    index = index[0] if len(index) == 1 else jnp.concatenate(index, axis=1)
    slots[...] = index[0:1] * 256 + index[1:2]
    project(index[2:3], x, wa, wf, ba, bf, out)


def project_halves(pieces, weights):
    rows, ew = sum(p.shape[0] * (p.shape[1] - 8) for p in pieces), pieces[0].shape[2]
    cols = weights[0].shape[1]
    return pl.pallas_call(
        project_halves_kernel,
        out_shape=[jax.ShapeDtypeStruct((rows, cols), BF16), jax.ShapeDtypeStruct((1, rows), I32)],
        in_specs=[VMEM] * (4 + len(pieces)),
        out_specs=[VMEM] * 2,
        compiler_params=PARAMS,
        cost_estimate=cost(4 * rows * ew * cols, 4 * ew * cols),
        name="project_halves",
    )(*weights, *pieces)


def select_kernel(m, count, *refs):
    blocks, slots, outs = refs[:count], refs[count : 2 * count], refs[2 * count :]
    places = sum(out.shape[0] for out in outs) // 2
    z, t = lax.axis_index("ctx"), lax.axis_index("tp")
    first = jnp.bitwise_xor(z, m) * 2 * places
    i = lax.broadcasted_iota(I32, (2 * places, 1), 0)
    position = first + jnp.bitwise_xor(i, t * places)
    total = None
    for block, slot in zip(blocks, slots):
        chosen = (slot[...] == position).astype(F32).astype(BF16)
        part = jnp.dot(chosen, block[...], preferred_element_type=F32)
        total = part if total is None else total + part
    at = 0
    for out in outs:
        out[...] = total[at : at + out.shape[0]].astype(BF16)
        at += out.shape[0]


def select(m, blocks, slots, sizes):
    rows, cols = sum(b.shape[0] for b in blocks), blocks[0].shape[1]
    return pl.pallas_call(
        functools.partial(select_kernel, m, len(blocks)),
        out_shape=[jax.ShapeDtypeStruct((size, cols), BF16) for size in sizes],
        in_specs=[VMEM] * (2 * len(blocks)),
        out_specs=[VMEM] * len(sizes),
        compiler_params=PARAMS,
        cost_estimate=cost(2 * sum(sizes) * rows * cols, 2 * rows * cols),
        name="select",
    )(*blocks, *slots)


def view(ref, places):
    if len(ref.shape) == 3:
        return ref.at[1 - lax.axis_index("tp")]
    return ref.at[pl.ds(0, places), :]


def square_sum(piece):
    wide = piece[...].astype(F32)
    return jnp.sum(wide * wide, axis=1, keepdims=True)


def squares_kernel(*refs):
    out = refs[-1]
    total = None
    for ref in refs[:-1]:
        part = ref[...] if ref.dtype == F32 else square_sum(view(ref, out.shape[0]))
        total = part if total is None else total + part
    out[...] = total


def squares(total, pieces, places):
    operands = pieces if total is None else [total] + pieces
    return pl.pallas_call(
        squares_kernel,
        out_shape=jax.ShapeDtypeStruct((places, 1), F32),
        in_specs=[VMEM] * len(operands),
        out_specs=VMEM,
        compiler_params=PARAMS,
        cost_estimate=cost(1 << 36, 1 << 26),
        name="squares",
    )(*operands)


def norm_kernel(places_of, fresh, gain, before, *refs):
    n = len(places_of)
    out, scaled, sems = refs[n], refs[n + 1], refs[n + 2]
    places, cols = scaled.shape[1:]
    pieces = [view(ref, places) for ref in refs[:n]]
    z, t = lax.axis_index("ctx"), lax.axis_index("tp")
    total = before[...]
    for k in fresh:
        total = total + square_sum(pieces[k])
    scale = lax.rsqrt(total / (n * cols) + 1e-06)
    copies = []
    for k, ((m, d), piece) in enumerate(zip(places_of, pieces)):
        block = jnp.bitwise_xor(z, m) * 2 + jnp.bitwise_xor(t, d)
        at = pl.ds(pl.multiple_of(block * cols, cols), cols)
        scaled[k] = (piece[...].astype(F32) * scale * gain[:, at].astype(F32)).astype(BF16)
        copies.append(pltpu.make_async_copy(scaled.at[k], out.at[:, at], sems.at[k]))
        copies[k].start()
    for copy in copies:
        copy.wait()


def norm(places_of, fresh, gain, before, pieces):
    n, places, cols = len(pieces), before.shape[0], pieces[0].shape[-1]
    return pl.pallas_call(
        functools.partial(norm_kernel, places_of, fresh),
        out_shape=jax.ShapeDtypeStruct((places, n * cols), BF16),
        in_specs=[VMEM] * (n + 2),
        out_specs=HBM,
        scratch_shapes=[pltpu.VMEM((n, places, cols), BF16), pltpu.SemaphoreType.DMA((n,))],
        compiler_params=PARAMS,
        cost_estimate=cost(4 * places * n * cols, 4 * places * n * cols),
        name="norm",
    )(gain, before, *pieces)


def after(x, *others):
    return lax.optimization_barrier((x, *others))[0]


def body(enc_rows, row_slot, row_kind, audio_proj, frame_proj, audio_bias, frame_bias, norm_gain):
    n = lax.axis_size("ctx")
    rows = enc_rows[0]
    half = rows.shape[0] // 2
    weights = (audio_proj, frame_proj, audio_bias[None, :], frame_bias[None, :])

    def over_ctx(x, m):
        return lax.ppermute(x, "ctx", [(i, i ^ m) for i in range(n)])

    def over_tp(x):
        return lax.ppermute(x, "tp", [(0, 1), (1, 0)])

    own = project_own(row_kind, rows, weights)
    blocks, slots = [own], [row_slot]

    def take(group):
        block, slot = project_halves(group, weights)
        blocks.append(block)
        slots.append(slot)

    if n == 4:
        near, second, third = to_send((None, 0, 1), rows, row_slot, row_kind)
        near, second, third = over_ctx(near, 1), over_ctx(second, 2), over_ctx(third, 3)
        near = after(near, own)
        take([lax.all_gather(near, "tp", axis=0)])
        second, third = after(second, blocks[-1]), after(third, blocks[-1])
        second, third = lax.optimization_barrier((second, third))
        shared = [over_ctx(second, 1), over_ctx(third, 1)]
        take([lax.all_gather(part, "tp", axis=0) for part in (second, third)])
        shared = lax.optimization_barrier((*shared, blocks[-1]))[:2]
        swapped = [over_tp(part)[None] for part in shared]
        take([part[None] for part in shared])
        take(swapped)
    else:
        (mine,) = to_send((None,), rows, row_slot, row_kind)
        arrived = [over_ctx(mine, m) for m in range(1, n)]
        for direct in arrived[:-1]:
            direct = after(direct, blocks[-1])
            take([lax.all_gather(direct, "tp", axis=0)])
        direct = after(arrived[-1], blocks[-1])
        swapped = over_tp(direct)
        take([direct[None]])
        take([swapped[None]])

    pieces = {}
    order = [n - 1, 1] + list(reversed(range(2, n - 1)))
    for m in order:
        chosen = select(m, blocks, slots, [2 * half] if m == 1 else [half, half])
        slots[0] = after(slots[0], chosen[0])
        if m == 1:
            pieces[m] = over_ctx(chosen[0], m)
            continue
        for d, piece in enumerate(chosen):
            perm = [(i * 2 + c, (i ^ m) * 2 + (c ^ d)) for i in range(n) for c in range(2)]
            pieces[m, d] = lax.ppermute(piece, ("ctx", "tp"), perm)

    total = None
    for m in order[:-1]:
        if m == 1:
            slots[0] = after(slots[0], total)
            pieces[0, 0], other = select(0, blocks, slots, [half, half])
            pieces[0, 1] = lax.all_gather(other, "tp", axis=0)
            total = squares(total, [pieces[0, 0], pieces[0, 1]], half)
            pair = after(pieces[m], total)
            pieces[m, 0], pieces[m, 1] = pair, lax.all_gather(pair[half:], "tp", axis=0)
        fresh = [pieces[m, 0], pieces[m, 1]]
        if m != 1 and total is not None:
            fresh = [after(piece, total) for piece in fresh]
        total = squares(total, fresh, half)
    order.append(0)
    places_of = tuple((m, d) for m in order for d in range(2))
    fresh = tuple(k for k, (m, _) in enumerate(places_of) if m == order[-2])
    final = [pieces[at] for at in places_of]
    for k in fresh:
        final[k] = after(final[k], total)
    return norm(places_of, fresh, norm_gain[None, :], total, final)[None]


def solution(mesh):
    return jax.shard_map(
        body,
        mesh=mesh,
        in_specs=(
            P(("groups", "enc"), "ctx", None),
            P(("groups", "enc"), "ctx"),
            P(("groups", "enc"), "ctx"),
            P(None, ("ctx", "tp")),
            P(None, ("ctx", "tp")),
            P(("ctx", "tp")),
            P(("ctx", "tp")),
            P(),
        ),
        out_specs=P(("groups", "enc"), ("ctx", "tp"), None),
        check_vma=False,
    )
```

```python
import functools

import jax
import jax.numpy as jnp
from jax import lax
from jax.experimental import pallas as pl
from jax.experimental.pallas import tpu as pltpu
from jax.sharding import PartitionSpec as P

VMEM = pl.BlockSpec(memory_space=pltpu.VMEM)
HBM = pl.BlockSpec(memory_space=pltpu.HBM)
PARAMS = pltpu.CompilerParams(vmem_limit_bytes=12 << 20)
BF16, F32, I32 = jnp.bfloat16, jnp.float32, jnp.int32


def cost(flops, moved):
    return pl.CostEstimate(flops=flops // 16, bytes_accessed=moved // 16, transcendentals=0)


def send_kernel(cuts, rows, slot, kind, *refs):
    count = len(cuts)
    outs, (slot_here, kind_here, index_sems, row_sems, tile_sems) = refs[:count], refs[-5:]
    tiles = refs[count:-5]
    whole = rows.shape[0]
    z, t = lax.axis_index("ctx"), lax.axis_index("tp")
    indices = [
        pltpu.make_async_copy(slot, slot_here, index_sems.at[0]),
        pltpu.make_async_copy(kind, kind_here, index_sems.at[1]),
    ]
    for copy in indices:
        copy.start()
    parts, copies = [], []
    for k, (out, parity) in enumerate(zip(outs, cuts)):
        size = out.shape[0] - 8
        part = t if parity is None else 2 * t + lax.rem(z + parity, 2)
        parts.append(part)
        source = rows.at[pl.ds(pl.multiple_of(part * size, size), size), :]
        copies.append(pltpu.make_async_copy(source, out.at[pl.ds(0, size), :], row_sems.at[k]))
        copies[-1].start()
    for tile in tiles:
        tile[...] = jnp.zeros(tile.shape, BF16)
    for copy in indices:
        copy.wait()
    slots, kinds = slot_here[...], kind_here[...]
    for n, (out, tile, part) in enumerate(zip(outs, tiles, parts)):
        size = out.shape[0] - 8
        s, k = slots[:, :size], kinds[:, :size]
        for i in range(1, whole // size):
            s = jnp.where(part == i, slots[:, i * size : (i + 1) * size], s)
            k = jnp.where(part == i, kinds[:, i * size : (i + 1) * size], k)
        line = lax.broadcasted_iota(I32, (8, size), 0)
        index = jnp.where(line == 0, s // 256, jnp.where(line == 1, s % 256, k))
        tile[:, :size] = index.astype(F32).astype(BF16)
        copies.append(pltpu.make_async_copy(tile, out.at[pl.ds(size, 8), :], tile_sems.at[n]))
        copies[-1].start()
    for copy in copies:
        copy.wait()


def to_send(cuts, rows, slot, kind):
    half, width = rows.shape[0] // 2, rows.shape[1]
    sizes = [half if parity is None else half // 2 for parity in cuts]
    return pl.pallas_call(
        functools.partial(send_kernel, cuts),
        out_shape=[jax.ShapeDtypeStruct((size + 8, width), BF16) for size in sizes],
        in_specs=[HBM] * 3,
        out_specs=[HBM] * len(cuts),
        scratch_shapes=[pltpu.VMEM((8, width), BF16) for _ in cuts]
        + [
            pltpu.VMEM(slot.shape, I32),
            pltpu.VMEM(slot.shape, I32),
            pltpu.SemaphoreType.DMA((2,)),
            pltpu.SemaphoreType.DMA((len(cuts),)),
            pltpu.SemaphoreType.DMA((len(cuts),)),
        ],
        compiler_params=pltpu.CompilerParams(vmem_limit_bytes=60 << 20),
        cost_estimate=cost(0, 4 * half * width),
        name="to_send",
    )(rows, slot, kind)


def column_of(row_vector):
    r = row_vector.shape[1]
    diagonal = lax.broadcasted_iota(I32, (r, r), 0) == lax.broadcasted_iota(I32, (r, r), 1)
    return jnp.sum(jnp.where(diagonal, row_vector, 0), axis=1, keepdims=True)


def project(kind_row, x, w_audio, w_frame, b_audio, b_frame, out):
    is_audio = column_of(kind_row) == 0
    audio = jnp.dot(x, w_audio[...], preferred_element_type=F32)
    frame = jnp.dot(x, w_frame[...], preferred_element_type=F32)
    audio = audio + b_audio[...].astype(F32)
    frame = frame + b_frame[...].astype(F32)
    out[...] = jnp.where(is_audio, audio, frame).astype(out.dtype)


def project_own_kernel(kind, x, wa, wf, ba, bf, out):
    project(kind[...], x[...], wa, wf, ba, bf, out)


def project_own(kind, rows, weights):
    ew, cols = weights[0].shape
    return pl.pallas_call(
        project_own_kernel,
        out_shape=jax.ShapeDtypeStruct((rows.shape[0], cols), BF16),
        in_specs=[VMEM] * 6,
        out_specs=VMEM,
        compiler_params=PARAMS,
        cost_estimate=cost(4 * rows.shape[0] * ew * cols, 4 * ew * cols),
        name="project_own",
    )(kind, rows, *weights)


def project_halves_kernel(wa, wf, ba, bf, *refs):
    pieces, out, slots = refs[:-2], refs[-2], refs[-1]
    x, index = [], []
    for piece in pieces:
        half = piece.shape[-2] - 8
        for k in range(piece.shape[0]):
            x.append(piece[k, :half, :])
            index.append(piece[k, half:, :half].astype(F32).astype(I32))
    x = x[0] if len(x) == 1 else jnp.concatenate(x, axis=0)
    index = index[0] if len(index) == 1 else jnp.concatenate(index, axis=1)
    slots[...] = index[0:1] * 256 + index[1:2]
    project(index[2:3], x, wa, wf, ba, bf, out)


def project_halves(pieces, weights):
    rows, ew = sum(p.shape[0] * (p.shape[1] - 8) for p in pieces), pieces[0].shape[2]
    cols = weights[0].shape[1]
    return pl.pallas_call(
        project_halves_kernel,
        out_shape=[jax.ShapeDtypeStruct((rows, cols), BF16), jax.ShapeDtypeStruct((1, rows), I32)],
        in_specs=[VMEM] * (4 + len(pieces)),
        out_specs=[VMEM] * 2,
        compiler_params=PARAMS,
        cost_estimate=cost(4 * rows * ew * cols, 4 * ew * cols),
        name="project_halves",
    )(*weights, *pieces)


def select_kernel(m, count, *refs):
    blocks, slots, outs = refs[:count], refs[count : 2 * count], refs[2 * count :]
    places = sum(out.shape[0] for out in outs) // 2
    z, t = lax.axis_index("ctx"), lax.axis_index("tp")
    first = jnp.bitwise_xor(z, m) * 2 * places
    i = lax.broadcasted_iota(I32, (2 * places, 1), 0)
    position = first + jnp.bitwise_xor(i, t * places)
    total = None
    for block, slot in zip(blocks, slots):
        chosen = (slot[...] == position).astype(F32).astype(BF16)
        part = jnp.dot(chosen, block[...], preferred_element_type=F32)
        total = part if total is None else total + part
    at = 0
    for out in outs:
        out[...] = total[at : at + out.shape[0]].astype(BF16)
        at += out.shape[0]


def select(m, blocks, slots, sizes):
    rows, cols = sum(b.shape[0] for b in blocks), blocks[0].shape[1]
    return pl.pallas_call(
        functools.partial(select_kernel, m, len(blocks)),
        out_shape=[jax.ShapeDtypeStruct((size, cols), BF16) for size in sizes],
        in_specs=[VMEM] * (2 * len(blocks)),
        out_specs=[VMEM] * len(sizes),
        compiler_params=PARAMS,
        cost_estimate=cost(2 * sum(sizes) * rows * cols, 2 * rows * cols),
        name="select",
    )(*blocks, *slots)


def view(ref, places):
    if len(ref.shape) == 3:
        return ref.at[1 - lax.axis_index("tp")]
    return ref.at[pl.ds(0, places), :]


def square_sum(piece):
    wide = piece[...].astype(F32)
    return jnp.sum(wide * wide, axis=1, keepdims=True)


def squares_kernel(*refs):
    out = refs[-1]
    total = None
    for ref in refs[:-1]:
        part = ref[...] if ref.dtype == F32 else square_sum(view(ref, out.shape[0]))
        total = part if total is None else total + part
    out[...] = total


def squares(total, pieces, places):
    operands = pieces if total is None else [total] + pieces
    return pl.pallas_call(
        squares_kernel,
        out_shape=jax.ShapeDtypeStruct((places, 1), F32),
        in_specs=[VMEM] * len(operands),
        out_specs=VMEM,
        compiler_params=PARAMS,
        cost_estimate=cost(1 << 36, 1 << 26),
        name="squares",
    )(*operands)


def norm_kernel(places_of, fresh, gain, before, *refs):
    n = len(places_of)
    out, scaled, sems = refs[n], refs[n + 1], refs[n + 2]
    places, cols = scaled.shape[1:]
    pieces = [view(ref, places) for ref in refs[:n]]
    z, t = lax.axis_index("ctx"), lax.axis_index("tp")
    total = before[...]
    for k in fresh:
        total = total + square_sum(pieces[k])
    scale = lax.rsqrt(total / (n * cols) + 1e-06)
    copies = []
    for k, ((m, d), piece) in enumerate(zip(places_of, pieces)):
        block = jnp.bitwise_xor(z, m) * 2 + jnp.bitwise_xor(t, d)
        at = pl.ds(pl.multiple_of(block * cols, cols), cols)
        scaled[k] = (piece[...].astype(F32) * scale * gain[:, at].astype(F32)).astype(BF16)
        copies.append(pltpu.make_async_copy(scaled.at[k], out.at[:, at], sems.at[k]))
        copies[k].start()
    for copy in copies:
        copy.wait()


def norm(places_of, fresh, gain, before, pieces):
    n, places, cols = len(pieces), before.shape[0], pieces[0].shape[-1]
    return pl.pallas_call(
        functools.partial(norm_kernel, places_of, fresh),
        out_shape=jax.ShapeDtypeStruct((places, n * cols), BF16),
        in_specs=[VMEM] * (n + 2),
        out_specs=HBM,
        scratch_shapes=[pltpu.VMEM((n, places, cols), BF16), pltpu.SemaphoreType.DMA((n,))],
        compiler_params=PARAMS,
        cost_estimate=cost(4 * places * n * cols, 4 * places * n * cols),
        name="norm",
    )(gain, before, *pieces)


def after(x, *others):
    return lax.optimization_barrier((x, *others))[0]


def body(enc_rows, row_slot, row_kind, audio_proj, frame_proj, audio_bias, frame_bias, norm_gain):
    n = lax.axis_size("ctx")
    rows = enc_rows[0]
    half = rows.shape[0] // 2
    weights = (audio_proj, frame_proj, audio_bias[None, :], frame_bias[None, :])

    def over_ctx(x, m):
        return lax.ppermute(x, "ctx", [(i, i ^ m) for i in range(n)])

    def over_tp(x):
        return lax.ppermute(x, "tp", [(0, 1), (1, 0)])

    own = project_own(row_kind, rows, weights)
    blocks, slots = [own], [row_slot]

    def take(group):
        block, slot = project_halves(group, weights)
        blocks.append(block)
        slots.append(slot)

    if n == 4:
        near, second, third = to_send((None, 0, 1), rows, row_slot, row_kind)
        near, second, third = over_ctx(near, 1), over_ctx(second, 2), over_ctx(third, 3)
        first = lax.optimization_barrier((near, second, third, own))[:3]
        shared = [over_ctx(part, 1) for part in first[1:]]
        other = [over_tp(part)[None] for part in first]
        take([part[None] for part in first])
        other = lax.optimization_barrier((*other, blocks[-1]))[:3]
        take(other)
        shared = lax.optimization_barrier((*shared, blocks[-1]))[:2]
        swapped = [over_tp(part)[None] for part in shared]
        take([part[None] for part in shared])
        take(swapped)
    else:
        (mine,) = to_send((None,), rows, row_slot, row_kind)
        arrived = [over_ctx(mine, m) for m in range(1, n)]
        for direct in arrived[:-1]:
            direct = after(direct, blocks[-1])
            take([lax.all_gather(direct, "tp", axis=0)])
        direct = after(arrived[-1], blocks[-1])
        swapped = over_tp(direct)
        take([direct[None]])
        take([swapped[None]])

    pieces = {}
    order = [n - 1, 1] + list(reversed(range(2, n - 1)))
    for m in order:
        chosen = select(m, blocks, slots, [2 * half] if m == 1 else [half, half])
        slots[0] = after(slots[0], chosen[0])
        if m == 1:
            pieces[m] = over_ctx(chosen[0], m)
            continue
        for d, piece in enumerate(chosen):
            perm = [(i * 2 + c, (i ^ m) * 2 + (c ^ d)) for i in range(n) for c in range(2)]
            pieces[m, d] = lax.ppermute(piece, ("ctx", "tp"), perm)

    total = None
    for m in order[:-1]:
        if m == 1:
            slots[0] = after(slots[0], total)
            pieces[0, 0], other = select(0, blocks, slots, [half, half])
            pieces[0, 1] = lax.all_gather(other, "tp", axis=0)
            total = squares(total, [pieces[0, 0], pieces[0, 1]], half)
            pair = after(pieces[m], total)
            pieces[m, 0], pieces[m, 1] = pair, lax.all_gather(pair[half:], "tp", axis=0)
        fresh = [pieces[m, 0], pieces[m, 1]]
        if m != 1 and total is not None:
            fresh = [after(piece, total) for piece in fresh]
        total = squares(total, fresh, half)
    order.append(0)
    places_of = tuple((m, d) for m in order for d in range(2))
    fresh = tuple(k for k, (m, _) in enumerate(places_of) if m == order[-2])
    final = [pieces[at] for at in places_of]
    for k in fresh:
        final[k] = after(final[k], total)
    return norm(places_of, fresh, norm_gain[None, :], total, final)[None]


def solution(mesh):
    return jax.shard_map(
        body,
        mesh=mesh,
        in_specs=(
            P(("groups", "enc"), "ctx", None),
            P(("groups", "enc"), "ctx"),
            P(("groups", "enc"), "ctx"),
            P(None, ("ctx", "tp")),
            P(None, ("ctx", "tp")),
            P(("ctx", "tp")),
            P(("ctx", "tp")),
            P(),
        ),
        out_specs=P(("groups", "enc"), ("ctx", "tp"), None),
        check_vma=False,
    )
```

```python
import functools

import jax
import jax.numpy as jnp
from jax import lax
from jax.experimental import pallas as pl
from jax.experimental.pallas import tpu as pltpu
from jax.sharding import PartitionSpec as P

VMEM = pl.BlockSpec(memory_space=pltpu.VMEM)
HBM = pl.BlockSpec(memory_space=pltpu.HBM)
PARAMS = pltpu.CompilerParams(vmem_limit_bytes=12 << 20)
BF16, F32, I32 = jnp.bfloat16, jnp.float32, jnp.int32


def cost(flops, moved):
    return pl.CostEstimate(flops=flops // 16, bytes_accessed=moved // 16, transcendentals=0)


def to_tiles(x, out):
    at = 0
    for r in range(0, x.shape[0], 16):
        for c in range(0, x.shape[1], 128):
            out[at : at + 16, :] = x[r : r + 16, c : c + 128]
            at += 16


def from_tiles(tiles, width):
    per_row = width // 128
    lines = []
    for r in range(0, tiles.shape[0], 16 * per_row):
        line = [tiles[r + 16 * c : r + 16 * (c + 1)] for c in range(per_row)]
        lines.append(jnp.concatenate(line, axis=1))
    return jnp.concatenate(lines, axis=0)


def send_kernel(cuts, rows, slot, kind, *refs):
    outs, (rows_here, slot_here, kind_here, sems) = refs[:-4], refs[-4:]
    whole, width = rows.shape
    half = whole // 2
    z, t = lax.axis_index("ctx"), lax.axis_index("tp")
    source = rows.at[pl.ds(pl.multiple_of(t * half, half), half), :]
    copies = [
        pltpu.make_async_copy(slot, slot_here, sems.at[0]),
        pltpu.make_async_copy(kind, kind_here, sems.at[1]),
        pltpu.make_async_copy(source, rows_here, sems.at[2]),
    ]
    for copy in copies:
        copy.start()
    for copy in copies:
        copy.wait()
    slots = jnp.where(t == 0, slot_here[:, :half], slot_here[:, half:])
    kinds = jnp.where(t == 0, kind_here[:, :half], kind_here[:, half:])
    for out, parity in zip(outs, cuts):
        x, s, k = rows_here, slots, kinds
        size = half
        if parity is not None:
            size = half // 2
            second = lax.rem(z + parity, 2)
            x = rows_here.at[pl.ds(pl.multiple_of(second * size, size), size), :]
            s = jnp.where(second == 0, slots[:, :size], slots[:, size:])
            k = jnp.where(second == 0, kinds[:, :size], kinds[:, size:])
        to_tiles(x, out)
        line = lax.broadcasted_iota(I32, (16, size), 0)
        index = jnp.where(line == 0, s // 256, jnp.where(line == 1, s % 256, k))
        index = jnp.where(line < 3, index, 0).astype(F32)
        if size < 128:
            index = jnp.concatenate([index, jnp.zeros((16, 128 - size), F32)], axis=1)
        out[size * width // 128 :, :] = index.astype(BF16)


def to_send(cuts, rows, slot, kind):
    half, width = rows.shape[0] // 2, rows.shape[1]
    sizes = [half if parity is None else half // 2 for parity in cuts]
    shapes = [(size * width // 128 + 16, 128) for size in sizes]
    return pl.pallas_call(
        functools.partial(send_kernel, cuts),
        out_shape=[jax.ShapeDtypeStruct(shape, BF16) for shape in shapes],
        in_specs=[HBM] * 3,
        out_specs=[VMEM] * len(cuts),
        scratch_shapes=[
            pltpu.VMEM((half, width), BF16),
            pltpu.VMEM(slot.shape, I32),
            pltpu.VMEM(slot.shape, I32),
            pltpu.SemaphoreType.DMA((3,)),
        ],
        compiler_params=pltpu.CompilerParams(vmem_limit_bytes=60 << 20),
        cost_estimate=cost(0, 4 * half * width),
        name="to_send",
    )(rows, slot, kind)


def column_of(row_vector):
    r = row_vector.shape[1]
    diagonal = lax.broadcasted_iota(I32, (r, r), 0) == lax.broadcasted_iota(I32, (r, r), 1)
    return jnp.sum(jnp.where(diagonal, row_vector, 0), axis=1, keepdims=True)


def project(kind_row, x, w_audio, w_frame, b_audio, b_frame, out):
    is_audio = column_of(kind_row) == 0
    audio = jnp.dot(x, w_audio[...], preferred_element_type=F32)
    frame = jnp.dot(x, w_frame[...], preferred_element_type=F32)
    audio = audio + b_audio[...].astype(F32)
    frame = frame + b_frame[...].astype(F32)
    out[...] = jnp.where(is_audio, audio, frame).astype(out.dtype)


def project_own_kernel(kind, x, wa, wf, ba, bf, out):
    project(kind[...], x[...], wa, wf, ba, bf, out)


def project_own(kind, rows, weights):
    ew, cols = weights[0].shape
    return pl.pallas_call(
        project_own_kernel,
        out_shape=jax.ShapeDtypeStruct((rows.shape[0], cols), BF16),
        in_specs=[VMEM] * 6,
        out_specs=VMEM,
        compiler_params=PARAMS,
        cost_estimate=cost(4 * rows.shape[0] * ew * cols, 4 * ew * cols),
        name="project_own",
    )(kind, rows, *weights)


def project_parts_kernel(wa, wf, ba, bf, *refs):
    parts, out, slots = refs[:-2], refs[-2], refs[-1]
    width = wa.shape[0]
    x, index = [], []
    for ref in parts:
        for k in range(ref.shape[0]):
            lines = ref.shape[1] - 16
            size = lines * 128 // width
            x.append(from_tiles(ref[k, :lines, :], width))
            index.append(ref[k, lines:, :].astype(F32).astype(I32)[:, :size])
    x = x[0] if len(x) == 1 else jnp.concatenate(x, axis=0)
    index = index[0] if len(index) == 1 else jnp.concatenate(index, axis=1)
    slots[...] = index[0:1] * 256 + index[1:2]
    project(index[2:3], x, wa, wf, ba, bf, out)


def project_parts(parts, weights):
    ew, cols = weights[0].shape
    rows = sum(p.shape[0] * (p.shape[1] - 16) * 128 // ew for p in parts)
    return pl.pallas_call(
        project_parts_kernel,
        out_shape=[jax.ShapeDtypeStruct((rows, cols), BF16), jax.ShapeDtypeStruct((1, rows), I32)],
        in_specs=[VMEM] * (4 + len(parts)),
        out_specs=[VMEM] * 2,
        compiler_params=PARAMS,
        cost_estimate=cost(4 * rows * ew * cols, 4 * ew * cols),
        name="project_parts",
    )(*weights, *parts)


def select_kernel(m, count, *refs):
    blocks, slots, outs = refs[:count], refs[count : 2 * count], refs[2 * count :]
    places = sum(out.shape[0] for out in outs) // 2
    z, t = lax.axis_index("ctx"), lax.axis_index("tp")
    first = jnp.bitwise_xor(z, m) * 2 * places
    i = lax.broadcasted_iota(I32, (2 * places, 1), 0)
    position = first + jnp.bitwise_xor(i, t * places)
    total = None
    for block, slot in zip(blocks, slots):
        chosen = (slot[...] == position).astype(F32).astype(BF16)
        part = jnp.dot(chosen, block[...], preferred_element_type=F32)
        total = part if total is None else total + part
    at = 0
    for out in outs:
        out[...] = total[at : at + out.shape[0]].astype(BF16)
        at += out.shape[0]


def select(m, blocks, slots, sizes):
    rows, cols = sum(b.shape[0] for b in blocks), blocks[0].shape[1]
    return pl.pallas_call(
        functools.partial(select_kernel, m, len(blocks)),
        out_shape=[jax.ShapeDtypeStruct((size, cols), BF16) for size in sizes],
        in_specs=[VMEM] * (2 * len(blocks)),
        out_specs=[VMEM] * len(sizes),
        compiler_params=PARAMS,
        cost_estimate=cost(2 * sum(sizes) * rows * cols, 2 * rows * cols),
        name="select",
    )(*blocks, *slots)


def view(ref, places):
    if len(ref.shape) == 3:
        return ref.at[1 - lax.axis_index("tp")]
    return ref.at[pl.ds(0, places), :]


def square_sum(piece):
    wide = piece[...].astype(F32)
    return jnp.sum(wide * wide, axis=1, keepdims=True)


def squares_kernel(*refs):
    out = refs[-1]
    total = None
    for ref in refs[:-1]:
        part = ref[...] if ref.dtype == F32 else square_sum(view(ref, out.shape[0]))
        total = part if total is None else total + part
    out[...] = total


def squares(total, pieces, places):
    operands = pieces if total is None else [total] + pieces
    return pl.pallas_call(
        squares_kernel,
        out_shape=jax.ShapeDtypeStruct((places, 1), F32),
        in_specs=[VMEM] * len(operands),
        out_specs=VMEM,
        compiler_params=PARAMS,
        cost_estimate=cost(1 << 36, 1 << 26),
        name="squares",
    )(*operands)


def norm_kernel(places_of, fresh, gain, before, *refs):
    n = len(places_of)
    out, scaled, sems = refs[n], refs[n + 1], refs[n + 2]
    places, cols = scaled.shape[1:]
    pieces = [view(ref, places) for ref in refs[:n]]
    z, t = lax.axis_index("ctx"), lax.axis_index("tp")
    total = before[...]
    for k in fresh:
        total = total + square_sum(pieces[k])
    scale = lax.rsqrt(total / (n * cols) + 1e-06)
    copies = []
    for k, ((m, d), piece) in enumerate(zip(places_of, pieces)):
        block = jnp.bitwise_xor(z, m) * 2 + jnp.bitwise_xor(t, d)
        at = pl.ds(pl.multiple_of(block * cols, cols), cols)
        scaled[k] = (piece[...].astype(F32) * scale * gain[:, at].astype(F32)).astype(BF16)
        copies.append(pltpu.make_async_copy(scaled.at[k], out.at[:, at], sems.at[k]))
        copies[k].start()
    for copy in copies:
        copy.wait()


def norm(places_of, fresh, gain, before, pieces):
    n, places, cols = len(pieces), before.shape[0], pieces[0].shape[-1]
    return pl.pallas_call(
        functools.partial(norm_kernel, places_of, fresh),
        out_shape=jax.ShapeDtypeStruct((places, n * cols), BF16),
        in_specs=[VMEM] * (n + 2),
        out_specs=HBM,
        scratch_shapes=[pltpu.VMEM((n, places, cols), BF16), pltpu.SemaphoreType.DMA((n,))],
        compiler_params=PARAMS,
        cost_estimate=cost(4 * places * n * cols, 4 * places * n * cols),
        name="norm",
    )(gain, before, *pieces)


def after(x, *others):
    return lax.optimization_barrier((x, *others))[0]


def body(enc_rows, row_slot, row_kind, audio_proj, frame_proj, audio_bias, frame_bias, norm_gain):
    n = lax.axis_size("ctx")
    rows = enc_rows[0]
    half = rows.shape[0] // 2
    weights = (audio_proj, frame_proj, audio_bias[None, :], frame_bias[None, :])

    def over_ctx(x, m):
        return lax.ppermute(x, "ctx", [(i, i ^ m) for i in range(n)])

    def over_tp(x):
        return lax.ppermute(x, "tp", [(0, 1), (1, 0)])

    own = project_own(row_kind, rows, weights)
    blocks, slots = [own], [row_slot]

    def take(group):
        block, slot = project_parts(group, weights)
        blocks.append(block)
        slots.append(slot)

    if n == 4:
        near, second, third = to_send((None, 0, 1), rows, row_slot, row_kind)
        near, second, third = over_ctx(near, 1), over_ctx(second, 2), over_ctx(third, 3)
        first = lax.optimization_barrier((near, second, third, own))[:3]
        shared = [over_ctx(part, 1) for part in first[1:]]
        other = [over_tp(part)[None] for part in first]
        take([part[None] for part in first])
        other = lax.optimization_barrier((*other, blocks[-1]))[:3]
        take(other)
        shared = lax.optimization_barrier((*shared, blocks[-1]))[:2]
        swapped = [over_tp(part)[None] for part in shared]
        take([part[None] for part in shared])
        take(swapped)
    else:
        (mine,) = to_send((None,), rows, row_slot, row_kind)
        arrived = [over_ctx(mine, m) for m in range(1, n)]
        for direct in arrived[:-1]:
            direct = after(direct, blocks[-1])
            take([lax.all_gather(direct, "tp", axis=0)])
        direct = after(arrived[-1], blocks[-1])
        swapped = over_tp(direct)
        take([direct[None]])
        take([swapped[None]])

    pieces = {}
    order = [n - 1, 1] + list(reversed(range(2, n - 1)))
    for m in order:
        chosen = select(m, blocks, slots, [2 * half] if m == 1 else [half, half])
        slots[0] = after(slots[0], chosen[0])
        if m == 1:
            pieces[m] = over_ctx(chosen[0], m)
            continue
        for d, piece in enumerate(chosen):
            perm = [(i * 2 + c, (i ^ m) * 2 + (c ^ d)) for i in range(n) for c in range(2)]
            pieces[m, d] = lax.ppermute(piece, ("ctx", "tp"), perm)

    total = None
    for m in order[:-1]:
        if m == 1:
            slots[0] = after(slots[0], total)
            pieces[0, 0], other = select(0, blocks, slots, [half, half])
            pieces[0, 1] = lax.all_gather(other, "tp", axis=0)
            total = squares(total, [pieces[0, 0], pieces[0, 1]], half)
            pair = after(pieces[m], total)
            pieces[m, 0], pieces[m, 1] = pair, lax.all_gather(pair[half:], "tp", axis=0)
        fresh = [pieces[m, 0], pieces[m, 1]]
        if m != 1 and total is not None:
            fresh = [after(piece, total) for piece in fresh]
        total = squares(total, fresh, half)
    order.append(0)
    places_of = tuple((m, d) for m in order for d in range(2))
    fresh = tuple(k for k, (m, _) in enumerate(places_of) if m == order[-2])
    final = [pieces[at] for at in places_of]
    for k in fresh:
        final[k] = after(final[k], total)
    return norm(places_of, fresh, norm_gain[None, :], total, final)[None]


def solution(mesh):
    return jax.shard_map(
        body,
        mesh=mesh,
        in_specs=(
            P(("groups", "enc"), "ctx", None),
            P(("groups", "enc"), "ctx"),
            P(("groups", "enc"), "ctx"),
            P(None, ("ctx", "tp")),
            P(None, ("ctx", "tp")),
            P(("ctx", "tp")),
            P(("ctx", "tp")),
            P(),
        ),
        out_specs=P(("groups", "enc"), ("ctx", "tp"), None),
        check_vma=False,
    )
```

```python
import functools

import jax
import jax.numpy as jnp
from jax import lax
from jax.experimental import pallas as pl
from jax.experimental.pallas import tpu as pltpu
from jax.sharding import PartitionSpec as P

VMEM = pl.BlockSpec(memory_space=pltpu.VMEM)
HBM = pl.BlockSpec(memory_space=pltpu.HBM)
PARAMS = pltpu.CompilerParams(vmem_limit_bytes=12 << 20)
BF16, F32, I32 = jnp.bfloat16, jnp.float32, jnp.int32


def cost(flops, moved):
    return pl.CostEstimate(flops=flops // 16, bytes_accessed=moved // 16, transcendentals=0)


def to_tiles(x, out):
    at = 0
    for r in range(0, x.shape[0], 16):
        for c in range(0, x.shape[1], 128):
            out[at : at + 16, :] = x[r : r + 16, c : c + 128]
            at += 16


def from_tiles(tiles, width):
    per_row = width // 128
    lines = []
    for r in range(0, tiles.shape[0], 16 * per_row):
        line = [tiles[r + 16 * c : r + 16 * (c + 1)] for c in range(per_row)]
        lines.append(jnp.concatenate(line, axis=1))
    return jnp.concatenate(lines, axis=0)


def send_kernel(cuts, rows, slot, kind, *refs):
    outs, (rows_here, slot_here, kind_here, sems) = refs[: len(cuts)], refs[-4:]
    whole, width = rows.shape
    half = whole // 2
    z, t = lax.axis_index("ctx"), lax.axis_index("tp")
    dealt = len(cuts) > 1
    source = rows
    if not dealt:
        source = rows.at[pl.ds(pl.multiple_of(t * half, half), half), :]
    copies = [
        pltpu.make_async_copy(slot, slot_here, sems.at[0]),
        pltpu.make_async_copy(kind, kind_here, sems.at[1]),
        pltpu.make_async_copy(source, rows_here, sems.at[2]),
    ]
    for copy in copies:
        copy.start()
    copies[0].wait()
    copies[1].wait()
    if dealt:
        slot_row, slot_col = slot_here[...], column_of(slot_here[...])
        kind_col = column_of(kind_here[...])
        rank_row = jnp.sum((slot_col < slot_row).astype(I32), axis=0, keepdims=True)
        rank_col = jnp.sum((slot_row < slot_col).astype(I32), axis=1, keepdims=True)
        refs[len(cuts)][...] = lax.rem(rank_row, 2)

        def rank_at(k):
            odd = (k >= half // 2).astype(I32)
            return t * half + 2 * (k - odd * (half // 2)) + odd

        here = rank_col == rank_at(lax.broadcasted_iota(I32, (1, half), 1))
        slots = jnp.sum(jnp.where(here, slot_col, 0), axis=0, keepdims=True)
        kinds = jnp.sum(jnp.where(here, kind_col, 0), axis=0, keepdims=True)
        deal = rank_row == rank_at(lax.broadcasted_iota(I32, (half, 1), 0))
        copies[2].wait()
        rows_out = refs[-5]
        rows_out[...] = jnp.dot(
            deal.astype(F32).astype(BF16), rows_here[...], preferred_element_type=F32
        ).astype(BF16)
    else:
        slots = jnp.where(t == 0, slot_here[:, :half], slot_here[:, half:])
        kinds = jnp.where(t == 0, kind_here[:, :half], kind_here[:, half:])
        copies[2].wait()
        rows_out = rows_here
    for out, parity in zip(outs, cuts):
        x, s, k = rows_out, slots, kinds
        size = half
        if parity is not None:
            size = half // 2
            second = lax.rem(z + parity, 2)
            x = rows_out.at[pl.ds(pl.multiple_of(second * size, size), size), :]
            s = jnp.where(second == 0, slots[:, :size], slots[:, size:])
            k = jnp.where(second == 0, kinds[:, :size], kinds[:, size:])
        to_tiles(x, out)
        line = lax.broadcasted_iota(I32, (16, size), 0)
        index = jnp.where(line == 0, s // 256, jnp.where(line == 1, s % 256, k))
        index = jnp.where(line < 3, index, 0).astype(F32)
        if size < 128:
            index = jnp.concatenate([index, jnp.zeros((16, 128 - size), F32)], axis=1)
        out[size * width // 128 :, :] = index.astype(BF16)


def to_send(cuts, rows, slot, kind):
    half, width = rows.shape[0] // 2, rows.shape[1]
    sizes = [half if parity is None else half // 2 for parity in cuts]
    shapes = [(size * width // 128 + 16, 128) for size in sizes]
    dealt = len(cuts) > 1
    out_shape = [jax.ShapeDtypeStruct(shape, BF16) for shape in shapes]
    scratch = [pltpu.VMEM((half, width), BF16)]
    if dealt:
        out_shape.append(jax.ShapeDtypeStruct(slot.shape, I32))
        scratch.append(pltpu.VMEM(rows.shape, BF16))
    return pl.pallas_call(
        functools.partial(send_kernel, cuts),
        out_shape=out_shape,
        in_specs=[HBM] * 3,
        out_specs=[VMEM] * len(out_shape),
        scratch_shapes=scratch
        + [
            pltpu.VMEM(slot.shape, I32),
            pltpu.VMEM(slot.shape, I32),
            pltpu.SemaphoreType.DMA((3,)),
        ],
        compiler_params=pltpu.CompilerParams(vmem_limit_bytes=60 << 20),
        cost_estimate=cost(0, 4 * half * width),
        name="to_send",
    )(rows, slot, kind)


def column_of(row_vector):
    r = row_vector.shape[1]
    diagonal = lax.broadcasted_iota(I32, (r, r), 0) == lax.broadcasted_iota(I32, (r, r), 1)
    return jnp.sum(jnp.where(diagonal, row_vector, 0), axis=1, keepdims=True)


def project(kind_row, x, w_audio, w_frame, b_audio, b_frame, out):
    is_audio = column_of(kind_row) == 0
    audio = jnp.dot(x, w_audio[...], preferred_element_type=F32)
    frame = jnp.dot(x, w_frame[...], preferred_element_type=F32)
    audio = audio + b_audio[...].astype(F32)
    frame = frame + b_frame[...].astype(F32)
    out[...] = jnp.where(is_audio, audio, frame).astype(out.dtype)


def project_own_kernel(kind, x, wa, wf, ba, bf, out):
    project(kind[...], x[...], wa, wf, ba, bf, out)


def project_own(kind, rows, weights):
    ew, cols = weights[0].shape
    return pl.pallas_call(
        project_own_kernel,
        out_shape=jax.ShapeDtypeStruct((rows.shape[0], cols), BF16),
        in_specs=[VMEM] * 6,
        out_specs=VMEM,
        compiler_params=PARAMS,
        cost_estimate=cost(4 * rows.shape[0] * ew * cols, 4 * ew * cols),
        name="project_own",
    )(kind, rows, *weights)


def project_parts_kernel(wa, wf, ba, bf, *refs):
    parts, out, slots = refs[:-2], refs[-2], refs[-1]
    width = wa.shape[0]
    x, index = [], []
    for ref in parts:
        for k in range(ref.shape[0]):
            lines = ref.shape[1] - 16
            size = lines * 128 // width
            x.append(from_tiles(ref[k, :lines, :], width))
            index.append(ref[k, lines:, :].astype(F32).astype(I32)[:, :size])
    x = x[0] if len(x) == 1 else jnp.concatenate(x, axis=0)
    index = index[0] if len(index) == 1 else jnp.concatenate(index, axis=1)
    slots[...] = index[0:1] * 256 + index[1:2]
    project(index[2:3], x, wa, wf, ba, bf, out)


def project_parts(parts, weights):
    ew, cols = weights[0].shape
    rows = sum(p.shape[0] * (p.shape[1] - 16) * 128 // ew for p in parts)
    return pl.pallas_call(
        project_parts_kernel,
        out_shape=[jax.ShapeDtypeStruct((rows, cols), BF16), jax.ShapeDtypeStruct((1, rows), I32)],
        in_specs=[VMEM] * (4 + len(parts)),
        out_specs=[VMEM] * 2,
        compiler_params=PARAMS,
        cost_estimate=cost(4 * rows * ew * cols, 4 * ew * cols),
        name="project_parts",
    )(*weights, *parts)


def select_kernel(m, count, *refs):
    blocks, slots, outs = refs[:count], refs[count : 2 * count], refs[2 * count :]
    places = sum(out.shape[0] for out in outs) // 2
    z, t = lax.axis_index("ctx"), lax.axis_index("tp")
    first = jnp.bitwise_xor(z, m) * 2 * places
    i = lax.broadcasted_iota(I32, (2 * places, 1), 0)
    position = first + jnp.bitwise_xor(i, t * places)
    total = None
    for block, slot in zip(blocks, slots):
        chosen = (slot[...] == position).astype(F32).astype(BF16)
        part = jnp.dot(chosen, block[...], preferred_element_type=F32)
        total = part if total is None else total + part
    at = 0
    for out in outs:
        out[...] = total[at : at + out.shape[0]].astype(BF16)
        at += out.shape[0]


def select(m, blocks, slots, sizes):
    rows, cols = sum(b.shape[0] for b in blocks), blocks[0].shape[1]
    return pl.pallas_call(
        functools.partial(select_kernel, m, len(blocks)),
        out_shape=[jax.ShapeDtypeStruct((size, cols), BF16) for size in sizes],
        in_specs=[VMEM] * (2 * len(blocks)),
        out_specs=[VMEM] * len(sizes),
        compiler_params=PARAMS,
        cost_estimate=cost(2 * sum(sizes) * rows * cols, 2 * rows * cols),
        name="select",
    )(*blocks, *slots)


def upto(places, width):
    i = lax.broadcasted_iota(I32, (width, width), 0)
    j = lax.broadcasted_iota(I32, (width, width), 1)
    counts = i <= j
    if width > places:
        counts = jnp.logical_and(counts, (i < places) == (j < places))
    return counts.astype(F32).astype(BF16)


def one_hot(found):
    return found.astype(F32).astype(BF16)


def over_rows(a, b):
    return lax.dot_general(a, b, (((1,), (1,)), ((), ())), preferred_element_type=F32)


def running(flags, counts):
    return jnp.dot(one_hot(flags), counts, preferred_element_type=F32)


def packet_kernel(m, early, count, second, *refs):
    blocks, slots, outs = refs[:count], refs[count : 2 * count], refs[2 * count :]
    size = outs[0].shape[0]
    places = blocks[0].shape[0] // 2
    first_size = places - size if second else size
    z, t = lax.axis_index("ctx"), lax.axis_index("tp")
    i = lax.broadcasted_iota(I32, (2 * places, 1), 0)
    position = jnp.bitwise_xor(z, m) * 2 * places + jnp.bitwise_xor(i, t * places)
    holds = [one_hot(slot[...] == position) for slot in slots]
    known = None
    for k in range(early):
        part = over_rows(jnp.ones((8, holds[k].shape[1]), BF16), holds[k])
        known = part if known is None else known + part
    counts = upto(places, 2 * places)
    wanted = known > 0.5
    number = running(wanted, counts)
    if second:
        wanted = jnp.logical_not(jnp.logical_and(wanted, number < first_size + 0.5))
        number = running(wanted, counts)
    number = jnp.where(wanted, number, 0.0)[0:1].astype(I32)
    e = lax.broadcasted_iota(I32, (2 * size, 1), 0)
    upper = (e >= size).astype(I32)
    lane_upper = (lax.broadcasted_iota(I32, (1, 2 * places), 1) >= places).astype(I32)
    pick = jnp.logical_and(number == e - upper * size + 1, lane_upper == upper)
    pick = one_hot(pick)
    total = None
    for block, hold in zip(blocks, holds):
        chosen = jnp.dot(pick, hold, preferred_element_type=F32).astype(BF16)
        part = jnp.dot(chosen, block[...], preferred_element_type=F32)
        total = part if total is None else total + part
    outs[0][...] = total[:size].astype(BF16)
    outs[1][...] = total[size:].astype(BF16)


def packet(m, early, blocks, slots, size, second):
    rows, cols = sum(b.shape[0] for b in blocks), blocks[0].shape[1]
    return pl.pallas_call(
        functools.partial(packet_kernel, m, early, len(blocks), second),
        out_shape=[jax.ShapeDtypeStruct((size, cols), BF16)] * 2,
        in_specs=[VMEM] * (2 * len(blocks)),
        out_specs=[VMEM] * 2,
        compiler_params=PARAMS,
        cost_estimate=cost(4 * size * rows * cols, 2 * rows * cols),
        name="packet",
    )(*blocks, *slots)


def order_kernel(first_size, parity, *refs):
    slots, outs = refs[:-2], refs[-2:]
    places = outs[0].shape[0]
    z, t = lax.axis_index("ctx"), lax.axis_index("tp")
    pair, odd = z // 2, lax.rem(z, 2)
    position = (2 * z + t) * places + lax.broadcasted_iota(I32, (places, 1), 0)
    source = lax.broadcasted_iota(I32, (8, 1), 0)
    known = None
    for k, slot in enumerate(slots):
        width = slot.shape[1]
        lane = lax.broadcasted_iota(I32, (1, width), 1)
        if k == 0:
            near, odd_rank = lane >= 0, parity[...]
        elif k in (1, 2):
            near = lane < places
            odd_rank = jnp.where(near, (lane >= places // 2).astype(I32), odd)
        else:
            near, odd_rank = lane < 0, jnp.zeros((1, width), I32) + 1 - odd
        owner_pair = jnp.where(near, pair, 1 - pair)
        held = jnp.logical_or(owner_pair == source // 2, odd_rank == lax.rem(source, 2))
        part = over_rows(one_hot(held), one_hot(slot[...] == position))
        known = part if known is None else known + part
    counts = upto(places, places)
    early = known > 0.5
    number = running(early, counts)
    early = jnp.logical_and(early, number < first_size + 0.5)
    later = running(jnp.logical_not(early), counts)
    place = jnp.where(early, number, later + first_size) - 1.0
    for m, out in zip((3, 2), outs):
        row = jnp.sum(jnp.where(source == jnp.bitwise_xor(z, m), place, 0.0), axis=0, keepdims=True)
        column = column_of(row.astype(I32))
        out[...] = one_hot(column == lax.broadcasted_iota(I32, (1, places), 1))


def order_of(first_size, parity, slots, places):
    return pl.pallas_call(
        functools.partial(order_kernel, first_size),
        out_shape=[jax.ShapeDtypeStruct((places, places), BF16)] * 2,
        in_specs=[VMEM] * (1 + len(slots)),
        out_specs=[VMEM] * 2,
        compiler_params=PARAMS,
        cost_estimate=cost(0, 0),
        name="order_of",
    )(parity, *slots)


def place_kernel(has_total, *refs):
    total = refs[0][...] if has_total else None
    order, packets, outs = refs[has_total], refs[has_total + 1 : has_total + 5], refs[-3:]
    for d in range(2):
        both = jnp.concatenate([packets[2 * d][...], packets[2 * d + 1][...]], axis=0)
        wide = jnp.dot(order[...], both, preferred_element_type=F32)
        outs[d][...] = wide.astype(BF16)
        part = jnp.sum(wide * wide, axis=1, keepdims=True)
        total = part if total is None else total + part
    outs[2][...] = total


def place(total, order, packets):
    places, cols = order.shape[0], packets[0].shape[1]
    operands = ([] if total is None else [total]) + [order] + packets
    return pl.pallas_call(
        functools.partial(place_kernel, len(operands) - 5),
        out_shape=[jax.ShapeDtypeStruct((places, cols), BF16)] * 2
        + [jax.ShapeDtypeStruct((places, 1), F32)],
        in_specs=[VMEM] * len(operands),
        out_specs=[VMEM] * 3,
        compiler_params=PARAMS,
        cost_estimate=cost(1 << 36, 1 << 26),
        name="place",
    )(*operands)


def view(ref, places):
    if len(ref.shape) == 3:
        return ref.at[1 - lax.axis_index("tp")]
    return ref.at[pl.ds(0, places), :]


def square_sum(piece):
    wide = piece[...].astype(F32)
    return jnp.sum(wide * wide, axis=1, keepdims=True)


def squares_kernel(*refs):
    out = refs[-1]
    total = None
    for ref in refs[:-1]:
        part = ref[...] if ref.dtype == F32 else square_sum(view(ref, out.shape[0]))
        total = part if total is None else total + part
    out[...] = total


def squares(total, pieces, places):
    operands = pieces if total is None else [total] + pieces
    return pl.pallas_call(
        squares_kernel,
        out_shape=jax.ShapeDtypeStruct((places, 1), F32),
        in_specs=[VMEM] * len(operands),
        out_specs=VMEM,
        compiler_params=PARAMS,
        cost_estimate=cost(1 << 36, 1 << 26),
        name="squares",
    )(*operands)


def norm_kernel(places_of, fresh, gain, before, *refs):
    n = len(places_of)
    out, scaled, sems = refs[n], refs[n + 1], refs[n + 2]
    places, cols = scaled.shape[1:]
    pieces = [view(ref, places) for ref in refs[:n]]
    z, t = lax.axis_index("ctx"), lax.axis_index("tp")
    total = before[...]
    for k in fresh:
        total = total + square_sum(pieces[k])
    scale = lax.rsqrt(total / (n * cols) + 1e-06)
    copies = []
    for k, ((m, d), piece) in enumerate(zip(places_of, pieces)):
        block = jnp.bitwise_xor(z, m) * 2 + jnp.bitwise_xor(t, d)
        at = pl.ds(pl.multiple_of(block * cols, cols), cols)
        scaled[k] = (piece[...].astype(F32) * scale * gain[:, at].astype(F32)).astype(BF16)
        copies.append(pltpu.make_async_copy(scaled.at[k], out.at[:, at], sems.at[k]))
        copies[k].start()
    for copy in copies:
        copy.wait()


def norm(places_of, fresh, gain, before, pieces):
    n, places, cols = len(pieces), before.shape[0], pieces[0].shape[-1]
    return pl.pallas_call(
        functools.partial(norm_kernel, places_of, fresh),
        out_shape=jax.ShapeDtypeStruct((places, n * cols), BF16),
        in_specs=[VMEM] * (n + 2),
        out_specs=HBM,
        scratch_shapes=[pltpu.VMEM((n, places, cols), BF16), pltpu.SemaphoreType.DMA((n,))],
        compiler_params=PARAMS,
        cost_estimate=cost(4 * places * n * cols, 4 * places * n * cols),
        name="norm",
    )(gain, before, *pieces)


def after(x, *others):
    return lax.optimization_barrier((x, *others))[0]


def body(enc_rows, row_slot, row_kind, audio_proj, frame_proj, audio_bias, frame_bias, norm_gain):
    n = lax.axis_size("ctx")
    rows = enc_rows[0]
    half = rows.shape[0] // 2
    weights = (audio_proj, frame_proj, audio_bias[None, :], frame_bias[None, :])

    def over_ctx(x, m):
        return lax.ppermute(x, "ctx", [(i, i ^ m) for i in range(n)])

    def over_tp(x):
        return lax.ppermute(x, "tp", [(0, 1), (1, 0)])

    own = project_own(row_kind, rows, weights)
    blocks, slots = [own], [row_slot]

    def take(group):
        block, slot = project_parts(group, weights)
        blocks.append(block)
        slots.append(slot)

    def to_core(x, m, d):
        pairs = [(i * 2 + c, (i ^ m) * 2 + (c ^ d)) for i in range(n) for c in range(2)]
        return lax.ppermute(x, ("ctx", "tp"), pairs)

    def own_and_near(total):
        slots[0] = after(slots[0], total)
        pieces[0, 0], other = select(0, blocks, slots, [half, half])
        pieces[0, 1] = lax.all_gather(other, "tp", axis=0)
        total = squares(total, [pieces[0, 0], pieces[0, 1]], half)
        pair = after(pieces[1], total)
        pieces[1, 0], pieces[1, 1] = pair, lax.all_gather(pair[half:], "tp", axis=0)
        return squares(total, [pieces[1, 0], pieces[1, 1]], half)

    pieces = {}
    if n == 4:
        near, second, third, parity = to_send((None, 0, 1), rows, row_slot, row_kind)
        near, second, third = over_ctx(near, 1), over_ctx(second, 2), over_ctx(third, 3)
        first = lax.optimization_barrier((near, second, third, own))[:3]
        shared = [over_ctx(part, 1) for part in first[1:]]
        other = [over_tp(part)[None] for part in first]
        take([part[None] for part in first])
        other = lax.optimization_barrier((*other, blocks[-1]))[:3]
        take(other)

        early, size = len(blocks), 3 * half // 8
        sent = {}
        for m in (3, 2):
            chosen = packet(m, early, blocks, slots, size, False)
            slots[0] = after(slots[0], chosen[0])
            sent[m] = [to_core(piece, m, d) for d, piece in enumerate(chosen)]
        joined = lax.optimization_barrier((*shared, *sent[3], blocks[-1]))
        shared, sent[3] = joined[:2], list(joined[2:4])
        swapped = [over_tp(part)[None] for part in shared]
        take([part[None] for part in shared])
        take(swapped)

        rest = {}
        for m in (3, 1, 2):
            if m == 1:
                (chosen,) = select(1, blocks, slots, [2 * half])
                slots[0] = after(slots[0], chosen)
                pieces[1] = over_ctx(chosen, 1)
                continue
            chosen = packet(m, early, blocks, slots, half - size, True)
            slots[0] = after(slots[0], chosen[0])
            if m == 3:
                joined = lax.optimization_barrier((*chosen, *sent[2]))
                chosen, sent[2] = joined[:2], list(joined[2:])
            rest[m] = [to_core(piece, m, d) for d, piece in enumerate(chosen)]

        joined = lax.optimization_barrier((*rest[3], *slots))
        rest[3] = joined[:2]
        order3, order2 = order_of(size, parity, joined[2:], half)
        packets = [sent[3][0], rest[3][0], sent[3][1], rest[3][1]]
        pieces[3, 0], pieces[3, 1], total = place(None, order3, packets)
        total = own_and_near(total)
        rest[2] = lax.optimization_barrier((*rest[2], total))[:2]
        packets = [sent[2][0], rest[2][0], sent[2][1], rest[2][1]]
        pieces[2, 0], pieces[2, 1], total = place(total, order2, packets)
        order, fresh = [3, 1, 0, 2], ()
    else:
        (mine,) = to_send((None,), rows, row_slot, row_kind)
        arrived = [over_ctx(mine, m) for m in range(1, n)]
        for direct in arrived[:-1]:
            direct = after(direct, blocks[-1])
            take([lax.all_gather(direct, "tp", axis=0)])
        direct = after(arrived[-1], blocks[-1])
        swapped = over_tp(direct)
        take([direct[None]])
        take([swapped[None]])

        order = [n - 1, 1] + list(reversed(range(2, n - 1)))
        for m in order:
            chosen = select(m, blocks, slots, [2 * half] if m == 1 else [half, half])
            slots[0] = after(slots[0], chosen[0])
            if m == 1:
                pieces[m] = over_ctx(chosen[0], m)
                continue
            for d, piece in enumerate(chosen):
                pieces[m, d] = to_core(piece, m, d)
        total = squares(None, [pieces[n - 1, 0], pieces[n - 1, 1]], half)
        total = own_and_near(total)
        for m in order[2:-1]:
            late = [after(pieces[m, d], total) for d in range(2)]
            total = squares(total, late, half)
        fresh = (2 * (n - 1), 2 * (n - 1) + 1)
        for d in range(2):
            pieces[order[-1], d] = after(pieces[order[-1], d], total)
        order = order[:-1] + [0, order[-1]]

    places_of = tuple((m, d) for m in order for d in range(2))
    return norm(places_of, fresh, norm_gain[None, :], total, [pieces[at] for at in places_of])[None]


def solution(mesh):
    return jax.shard_map(
        body,
        mesh=mesh,
        in_specs=(
            P(("groups", "enc"), "ctx", None),
            P(("groups", "enc"), "ctx"),
            P(("groups", "enc"), "ctx"),
            P(None, ("ctx", "tp")),
            P(None, ("ctx", "tp")),
            P(("ctx", "tp")),
            P(("ctx", "tp")),
            P(),
        ),
        out_specs=P(("groups", "enc"), ("ctx", "tp"), None),
        check_vma=False,
    )
```

```python
import functools

import jax
import jax.numpy as jnp
from jax import lax
from jax.experimental import pallas as pl
from jax.experimental.pallas import tpu as pltpu
from jax.sharding import PartitionSpec as P

VMEM = pl.BlockSpec(memory_space=pltpu.VMEM)
HBM = pl.BlockSpec(memory_space=pltpu.HBM)
PARAMS = pltpu.CompilerParams(vmem_limit_bytes=12 << 20)
BF16, F32, I32 = jnp.bfloat16, jnp.float32, jnp.int32


def cost(flops, moved):
    return pl.CostEstimate(flops=flops // 16, bytes_accessed=moved // 16, transcendentals=0)


def to_tiles(x, out):
    at = 0
    for r in range(0, x.shape[0], 16):
        for c in range(0, x.shape[1], 128):
            out[at : at + 16, :] = x[r : r + 16, c : c + 128]
            at += 16


def from_tiles(tiles, width):
    per_row = width // 128
    lines = []
    for r in range(0, tiles.shape[0], 16 * per_row):
        line = [tiles[r + 16 * c : r + 16 * (c + 1)] for c in range(per_row)]
        lines.append(jnp.concatenate(line, axis=1))
    return jnp.concatenate(lines, axis=0)


def send_kernel(cuts, rows, slot, kind, *refs):
    outs, (rows_here, slot_here, kind_here, sems) = refs[: len(cuts)], refs[-4:]
    whole, width = rows.shape
    half = whole // 2
    z, t = lax.axis_index("ctx"), lax.axis_index("tp")
    dealt = len(cuts) > 1
    source = rows
    if not dealt:
        source = rows.at[pl.ds(pl.multiple_of(t * half, half), half), :]
    copies = [
        pltpu.make_async_copy(slot, slot_here, sems.at[0]),
        pltpu.make_async_copy(kind, kind_here, sems.at[1]),
        pltpu.make_async_copy(source, rows_here, sems.at[2]),
    ]
    for copy in copies:
        copy.start()
    copies[0].wait()
    copies[1].wait()
    if dealt:
        slot_row, slot_col = slot_here[...], column_of(slot_here[...])
        kind_col = column_of(kind_here[...])
        rank_row = jnp.sum((slot_col < slot_row).astype(I32), axis=0, keepdims=True)
        rank_col = jnp.sum((slot_row < slot_col).astype(I32), axis=1, keepdims=True)
        refs[len(cuts)][...] = lax.rem(rank_row, 2)

        def rank_at(k):
            odd = (k >= half // 2).astype(I32)
            return t * half + 2 * (k - odd * (half // 2)) + odd

        here = rank_col == rank_at(lax.broadcasted_iota(I32, (1, half), 1))
        slots = jnp.sum(jnp.where(here, slot_col, 0), axis=0, keepdims=True)
        kinds = jnp.sum(jnp.where(here, kind_col, 0), axis=0, keepdims=True)
        deal = rank_row == rank_at(lax.broadcasted_iota(I32, (half, 1), 0))
        copies[2].wait()
        rows_out = refs[-5]
        rows_out[...] = jnp.dot(
            deal.astype(F32).astype(BF16), rows_here[...], preferred_element_type=F32
        ).astype(BF16)
    else:
        slots = jnp.where(t == 0, slot_here[:, :half], slot_here[:, half:])
        kinds = jnp.where(t == 0, kind_here[:, :half], kind_here[:, half:])
        copies[2].wait()
        rows_out = rows_here
    for out, parity in zip(outs, cuts):
        x, s, k = rows_out, slots, kinds
        size = half
        if parity is not None:
            size = half // 2
            second = lax.rem(z + parity, 2)
            x = rows_out.at[pl.ds(pl.multiple_of(second * size, size), size), :]
            s = jnp.where(second == 0, slots[:, :size], slots[:, size:])
            k = jnp.where(second == 0, kinds[:, :size], kinds[:, size:])
        to_tiles(x, out)
        line = lax.broadcasted_iota(I32, (16, size), 0)
        index = jnp.where(line == 0, s // 256, jnp.where(line == 1, s % 256, k))
        index = jnp.where(line < 3, index, 0).astype(F32)
        if size < 128:
            index = jnp.concatenate([index, jnp.zeros((16, 128 - size), F32)], axis=1)
        out[size * width // 128 :, :] = index.astype(BF16)


def to_send(cuts, rows, slot, kind):
    half, width = rows.shape[0] // 2, rows.shape[1]
    sizes = [half if parity is None else half // 2 for parity in cuts]
    shapes = [(size * width // 128 + 16, 128) for size in sizes]
    dealt = len(cuts) > 1
    out_shape = [jax.ShapeDtypeStruct(shape, BF16) for shape in shapes]
    scratch = [pltpu.VMEM((half, width), BF16)]
    if dealt:
        out_shape.append(jax.ShapeDtypeStruct(slot.shape, I32))
        scratch.append(pltpu.VMEM(rows.shape, BF16))
    return pl.pallas_call(
        functools.partial(send_kernel, cuts),
        out_shape=out_shape,
        in_specs=[HBM] * 3,
        out_specs=[VMEM] * len(out_shape),
        scratch_shapes=scratch
        + [
            pltpu.VMEM(slot.shape, I32),
            pltpu.VMEM(slot.shape, I32),
            pltpu.SemaphoreType.DMA((3,)),
        ],
        compiler_params=pltpu.CompilerParams(vmem_limit_bytes=60 << 20),
        cost_estimate=cost(0, 4 * half * width),
        name="to_send",
    )(rows, slot, kind)


def column_of(row_vector):
    r = row_vector.shape[1]
    diagonal = lax.broadcasted_iota(I32, (r, r), 0) == lax.broadcasted_iota(I32, (r, r), 1)
    return jnp.sum(jnp.where(diagonal, row_vector, 0), axis=1, keepdims=True)


def project(kind_row, x, w_audio, w_frame, b_audio, b_frame, out):
    is_audio = column_of(kind_row) == 0
    audio = jnp.dot(x, w_audio[...], preferred_element_type=F32)
    frame = jnp.dot(x, w_frame[...], preferred_element_type=F32)
    audio = audio + b_audio[...].astype(F32)
    frame = frame + b_frame[...].astype(F32)
    out[...] = jnp.where(is_audio, audio, frame).astype(out.dtype)


def project_own_kernel(kind, x, wa, wf, ba, bf, out):
    project(kind[...], x[...], wa, wf, ba, bf, out)


def project_own(kind, rows, weights):
    ew, cols = weights[0].shape
    return pl.pallas_call(
        project_own_kernel,
        out_shape=jax.ShapeDtypeStruct((rows.shape[0], cols), BF16),
        in_specs=[VMEM] * 6,
        out_specs=VMEM,
        compiler_params=PARAMS,
        cost_estimate=cost(4 * rows.shape[0] * ew * cols, 4 * ew * cols),
        name="project_own",
    )(kind, rows, *weights)


def project_parts_kernel(wa, wf, ba, bf, *refs):
    parts, out, slots = refs[:-2], refs[-2], refs[-1]
    width = wa.shape[0]
    x, index = [], []
    for ref in parts:
        for k in range(ref.shape[0]):
            lines = ref.shape[1] - 16
            size = lines * 128 // width
            x.append(from_tiles(ref[k, :lines, :], width))
            index.append(ref[k, lines:, :].astype(F32).astype(I32)[:, :size])
    x = x[0] if len(x) == 1 else jnp.concatenate(x, axis=0)
    index = index[0] if len(index) == 1 else jnp.concatenate(index, axis=1)
    slots[...] = index[0:1] * 256 + index[1:2]
    project(index[2:3], x, wa, wf, ba, bf, out)


def project_parts(parts, weights):
    ew, cols = weights[0].shape
    rows = sum(p.shape[0] * (p.shape[1] - 16) * 128 // ew for p in parts)
    return pl.pallas_call(
        project_parts_kernel,
        out_shape=[jax.ShapeDtypeStruct((rows, cols), BF16), jax.ShapeDtypeStruct((1, rows), I32)],
        in_specs=[VMEM] * (4 + len(parts)),
        out_specs=[VMEM] * 2,
        compiler_params=PARAMS,
        cost_estimate=cost(4 * rows * ew * cols, 4 * ew * cols),
        name="project_parts",
    )(*weights, *parts)


def select_kernel(m, count, *refs):
    blocks, slots, outs = refs[:count], refs[count : 2 * count], refs[2 * count :]
    places = sum(out.shape[0] for out in outs) // 2
    z, t = lax.axis_index("ctx"), lax.axis_index("tp")
    first = jnp.bitwise_xor(z, m) * 2 * places
    i = lax.broadcasted_iota(I32, (2 * places, 1), 0)
    position = first + jnp.bitwise_xor(i, t * places)
    total = None
    for block, slot in zip(blocks, slots):
        chosen = (slot[...] == position).astype(F32).astype(BF16)
        part = jnp.dot(chosen, block[...], preferred_element_type=F32)
        total = part if total is None else total + part
    at = 0
    for out in outs:
        out[...] = total[at : at + out.shape[0]].astype(BF16)
        at += out.shape[0]


def select(m, blocks, slots, sizes):
    rows, cols = sum(b.shape[0] for b in blocks), blocks[0].shape[1]
    return pl.pallas_call(
        functools.partial(select_kernel, m, len(blocks)),
        out_shape=[jax.ShapeDtypeStruct((size, cols), BF16) for size in sizes],
        in_specs=[VMEM] * (2 * len(blocks)),
        out_specs=[VMEM] * len(sizes),
        compiler_params=PARAMS,
        cost_estimate=cost(2 * sum(sizes) * rows * cols, 2 * rows * cols),
        name="select",
    )(*blocks, *slots)


def upto(places, width):
    i = lax.broadcasted_iota(I32, (width, width), 0)
    j = lax.broadcasted_iota(I32, (width, width), 1)
    counts = i <= j
    if width > places:
        counts = jnp.logical_and(counts, (i < places) == (j < places))
    return counts.astype(F32).astype(BF16)


def one_hot(found):
    return found.astype(F32).astype(BF16)


def over_rows(a, b):
    return lax.dot_general(a, b, (((1,), (1,)), ((), ())), preferred_element_type=F32)


def running(flags, counts):
    return jnp.dot(one_hot(flags), counts, preferred_element_type=F32)


def packet_kernel(m, early, count, second, *refs):
    blocks, slots, outs = refs[:count], refs[count : 2 * count], refs[2 * count :]
    size = outs[0].shape[0]
    places = blocks[0].shape[0] // 2
    first_size = places - size if second else size
    z, t = lax.axis_index("ctx"), lax.axis_index("tp")
    i = lax.broadcasted_iota(I32, (2 * places, 1), 0)
    position = jnp.bitwise_xor(z, m) * 2 * places + jnp.bitwise_xor(i, t * places)
    holds = [one_hot(slot[...] == position) for slot in slots]
    known = None
    for k in range(early):
        part = over_rows(jnp.ones((8, holds[k].shape[1]), BF16), holds[k])
        known = part if known is None else known + part
    counts = upto(places, 2 * places)
    wanted = known > 0.5
    number = running(wanted, counts)
    if second:
        wanted = jnp.logical_not(jnp.logical_and(wanted, number < first_size + 0.5))
        number = running(wanted, counts)
    number = jnp.where(wanted, number, 0.0)[0:1].astype(I32)
    e = lax.broadcasted_iota(I32, (2 * size, 1), 0)
    upper = (e >= size).astype(I32)
    lane_upper = (lax.broadcasted_iota(I32, (1, 2 * places), 1) >= places).astype(I32)
    pick = jnp.logical_and(number == e - upper * size + 1, lane_upper == upper)
    pick = one_hot(pick)
    total = None
    for block, hold in zip(blocks, holds):
        chosen = jnp.dot(pick, hold, preferred_element_type=F32).astype(BF16)
        part = jnp.dot(chosen, block[...], preferred_element_type=F32)
        total = part if total is None else total + part
    outs[0][...] = total[:size].astype(BF16)
    outs[1][...] = total[size:].astype(BF16)


def packet(m, early, blocks, slots, size, second):
    rows, cols = sum(b.shape[0] for b in blocks), blocks[0].shape[1]
    return pl.pallas_call(
        functools.partial(packet_kernel, m, early, len(blocks), second),
        out_shape=[jax.ShapeDtypeStruct((size, cols), BF16)] * 2,
        in_specs=[VMEM] * (2 * len(blocks)),
        out_specs=[VMEM] * 2,
        compiler_params=PARAMS,
        cost_estimate=cost(4 * size * rows * cols, 2 * rows * cols),
        name="packet",
    )(*blocks, *slots)


def order_kernel(first_size, parity, *refs):
    slots, outs = refs[:-2], refs[-2:]
    places = outs[0].shape[0]
    z, t = lax.axis_index("ctx"), lax.axis_index("tp")
    pair, odd = z // 2, lax.rem(z, 2)
    position = (2 * z + t) * places + lax.broadcasted_iota(I32, (places, 1), 0)
    source = lax.broadcasted_iota(I32, (8, 1), 0)
    known = None
    for k, slot in enumerate(slots):
        width = slot.shape[1]
        lane = lax.broadcasted_iota(I32, (1, width), 1)
        if k == 0:
            near, odd_rank = lane >= 0, parity[...]
        elif k in (1, 2):
            near = lane < places
            odd_rank = jnp.where(near, (lane >= places // 2).astype(I32), odd)
        else:
            near, odd_rank = lane < 0, jnp.zeros((1, width), I32) + 1 - odd
        owner_pair = jnp.where(near, pair, 1 - pair)
        held = jnp.logical_or(owner_pair == source // 2, odd_rank == lax.rem(source, 2))
        part = over_rows(one_hot(held), one_hot(slot[...] == position))
        known = part if known is None else known + part
    counts = upto(places, places)
    early = known > 0.5
    number = running(early, counts)
    early = jnp.logical_and(early, number < first_size + 0.5)
    later = running(jnp.logical_not(early), counts)
    place = jnp.where(early, number, later + first_size) - 1.0
    for m, out in zip((3, 2), outs):
        row = jnp.sum(jnp.where(source == jnp.bitwise_xor(z, m), place, 0.0), axis=0, keepdims=True)
        column = column_of(row.astype(I32))
        out[...] = one_hot(column == lax.broadcasted_iota(I32, (1, places), 1))


def order_of(first_size, parity, slots, places):
    return pl.pallas_call(
        functools.partial(order_kernel, first_size),
        out_shape=[jax.ShapeDtypeStruct((places, places), BF16)] * 2,
        in_specs=[VMEM] * (1 + len(slots)),
        out_specs=[VMEM] * 2,
        compiler_params=PARAMS,
        cost_estimate=cost(1 << 34, 0),
        name="order_of",
    )(parity, *slots)


def place_kernel(has_total, *refs):
    total = refs[0][...] if has_total else None
    order, packets, outs = refs[has_total], refs[has_total + 1 : has_total + 5], refs[-3:]
    for d in range(2):
        both = jnp.concatenate([packets[2 * d][...], packets[2 * d + 1][...]], axis=0)
        wide = jnp.dot(order[...], both, preferred_element_type=F32)
        outs[d][...] = wide.astype(BF16)
        part = jnp.sum(wide * wide, axis=1, keepdims=True)
        total = part if total is None else total + part
    outs[2][...] = total


def place(total, order, packets):
    places, cols = order.shape[0], packets[0].shape[1]
    operands = ([] if total is None else [total]) + [order] + packets
    return pl.pallas_call(
        functools.partial(place_kernel, len(operands) - 5),
        out_shape=[jax.ShapeDtypeStruct((places, cols), BF16)] * 2
        + [jax.ShapeDtypeStruct((places, 1), F32)],
        in_specs=[VMEM] * len(operands),
        out_specs=[VMEM] * 3,
        compiler_params=PARAMS,
        cost_estimate=cost(1 << 34, 0),
        name="place",
    )(*operands)


def view(ref, places):
    if len(ref.shape) == 3:
        return ref.at[1 - lax.axis_index("tp")]
    return ref.at[pl.ds(0, places), :]


def square_sum(piece):
    wide = piece[...].astype(F32)
    return jnp.sum(wide * wide, axis=1, keepdims=True)


def squares_kernel(*refs):
    out = refs[-1]
    total = None
    for ref in refs[:-1]:
        part = ref[...] if ref.dtype == F32 else square_sum(view(ref, out.shape[0]))
        total = part if total is None else total + part
    out[...] = total


def squares(total, pieces, places):
    operands = pieces if total is None else [total] + pieces
    return pl.pallas_call(
        squares_kernel,
        out_shape=jax.ShapeDtypeStruct((places, 1), F32),
        in_specs=[VMEM] * len(operands),
        out_specs=VMEM,
        compiler_params=PARAMS,
        cost_estimate=cost(1 << 34, 0),
        name="squares",
    )(*operands)


def norm_kernel(places_of, fresh, gain, before, *refs):
    n = len(places_of)
    out, scaled, sems = refs[n], refs[n + 1], refs[n + 2]
    places, cols = scaled.shape[1:]
    pieces = [view(ref, places) for ref in refs[:n]]
    z, t = lax.axis_index("ctx"), lax.axis_index("tp")
    total = before[...]
    for k in fresh:
        total = total + square_sum(pieces[k])
    scale = lax.rsqrt(total / (n * cols) + 1e-06)
    copies = []
    for k, ((m, d), piece) in enumerate(zip(places_of, pieces)):
        block = jnp.bitwise_xor(z, m) * 2 + jnp.bitwise_xor(t, d)
        at = pl.ds(pl.multiple_of(block * cols, cols), cols)
        scaled[k] = (piece[...].astype(F32) * scale * gain[:, at].astype(F32)).astype(BF16)
        copies.append(pltpu.make_async_copy(scaled.at[k], out.at[:, at], sems.at[k]))
        copies[k].start()
    for copy in copies:
        copy.wait()


def norm(places_of, fresh, gain, before, pieces):
    n, places, cols = len(pieces), before.shape[0], pieces[0].shape[-1]
    return pl.pallas_call(
        functools.partial(norm_kernel, places_of, fresh),
        out_shape=jax.ShapeDtypeStruct((places, n * cols), BF16),
        in_specs=[VMEM] * (n + 2),
        out_specs=HBM,
        scratch_shapes=[pltpu.VMEM((n, places, cols), BF16), pltpu.SemaphoreType.DMA((n,))],
        compiler_params=PARAMS,
        cost_estimate=cost(4 * places * n * cols, 4 * places * n * cols),
        name="norm",
    )(gain, before, *pieces)


def after(x, *others):
    return lax.optimization_barrier((x, *others))[0]


def body(enc_rows, row_slot, row_kind, audio_proj, frame_proj, audio_bias, frame_bias, norm_gain):
    n = lax.axis_size("ctx")
    rows = enc_rows[0]
    half = rows.shape[0] // 2
    weights = (audio_proj, frame_proj, audio_bias[None, :], frame_bias[None, :])

    def over_ctx(x, m):
        return lax.ppermute(x, "ctx", [(i, i ^ m) for i in range(n)])

    def over_tp(x):
        return lax.ppermute(x, "tp", [(0, 1), (1, 0)])

    own = project_own(row_kind, rows, weights)
    blocks, slots = [own], [row_slot]

    def take(group):
        block, slot = project_parts(group, weights)
        blocks.append(block)
        slots.append(slot)

    def to_core(x, m, d):
        pairs = [(i * 2 + c, (i ^ m) * 2 + (c ^ d)) for i in range(n) for c in range(2)]
        return lax.ppermute(x, ("ctx", "tp"), pairs)

    def own_and_near(total):
        pieces[0, 0], other = select(0, blocks, slots, [half, half])
        pieces[0, 1] = lax.all_gather(other, "tp", axis=0)
        total = squares(total, [pieces[0, 0], pieces[0, 1]], half)
        pair = pieces[1]
        pieces[1, 0], pieces[1, 1] = pair, lax.all_gather(pair[half:], "tp", axis=0)
        return squares(total, [pieces[1, 0], pieces[1, 1]], half)

    pieces = {}
    if n == 4:
        near, second, third, parity = to_send((None, 0, 1), rows, row_slot, row_kind)
        near, second, third = over_ctx(near, 1), over_ctx(second, 2), over_ctx(third, 3)
        first = lax.optimization_barrier((near, second, third, own))[:3]
        shared = [over_ctx(part, 1) for part in first[1:]]
        other = [over_tp(part)[None] for part in first]
        take([part[None] for part in first])
        other = lax.optimization_barrier((*other, blocks[-1]))[:3]
        take(other)

        early, size = len(blocks), 3 * half // 8
        sent = {}
        for m in (3, 2):
            chosen = packet(m, early, blocks, slots, size, False)
            slots[0] = after(slots[0], chosen[0])
            sent[m] = [to_core(piece, m, d) for d, piece in enumerate(chosen)]
        shared = lax.optimization_barrier((*shared, blocks[-1]))[:2]
        take([lax.all_gather(part, "tp", axis=0) for part in shared])

        (chosen,) = select(1, blocks, slots, [2 * half])
        slots[0] = after(slots[0], chosen)
        pieces[1] = over_ctx(chosen, 1)
        rest = {}
        for m in (3, 2):
            chosen = packet(m, early, blocks, slots, half - size, True)
            slots[0] = after(slots[0], chosen[0])
            if m == 3:
                joined = lax.optimization_barrier((*chosen, *sent[3], *sent[2]))
                chosen, sent[3], sent[2] = joined[:2], list(joined[2:4]), list(joined[4:])
            rest[m] = [to_core(piece, m, d) for d, piece in enumerate(chosen)]

        order3, order2 = order_of(size, parity, slots, half)
        packets = [sent[3][0], rest[3][0], sent[3][1], rest[3][1]]
        pieces[3, 0], pieces[3, 1], total = place(None, order3, packets)
        total = own_and_near(total)
        packets = [sent[2][0], rest[2][0], sent[2][1], rest[2][1]]
        pieces[2, 0], pieces[2, 1], total = place(total, order2, packets)
        order, fresh = [3, 1, 0, 2], ()
    else:
        (mine,) = to_send((None,), rows, row_slot, row_kind)
        arrived = [over_ctx(mine, m) for m in range(1, n)]
        for direct in arrived[:-1]:
            direct = after(direct, blocks[-1])
            take([lax.all_gather(direct, "tp", axis=0)])
        direct = after(arrived[-1], blocks[-1])
        swapped = over_tp(direct)
        take([direct[None]])
        take([swapped[None]])

        order = [n - 1, 1] + list(reversed(range(2, n - 1)))
        for m in order:
            chosen = select(m, blocks, slots, [2 * half] if m == 1 else [half, half])
            slots[0] = after(slots[0], chosen[0])
            if m == 1:
                pieces[m] = over_ctx(chosen[0], m)
                continue
            for d, piece in enumerate(chosen):
                pieces[m, d] = to_core(piece, m, d)
        total = squares(None, [pieces[n - 1, 0], pieces[n - 1, 1]], half)
        total = own_and_near(total)
        for m in order[2:-1]:
            late = [after(pieces[m, d], total) for d in range(2)]
            total = squares(total, late, half)
        fresh = (2 * (n - 1), 2 * (n - 1) + 1)
        for d in range(2):
            pieces[order[-1], d] = after(pieces[order[-1], d], total)
        order = order[:-1] + [0, order[-1]]

    places_of = tuple((m, d) for m in order for d in range(2))
    return norm(places_of, fresh, norm_gain[None, :], total, [pieces[at] for at in places_of])[None]


def solution(mesh):
    return jax.shard_map(
        body,
        mesh=mesh,
        in_specs=(
            P(("groups", "enc"), "ctx", None),
            P(("groups", "enc"), "ctx"),
            P(("groups", "enc"), "ctx"),
            P(None, ("ctx", "tp")),
            P(None, ("ctx", "tp")),
            P(("ctx", "tp")),
            P(("ctx", "tp")),
            P(),
        ),
        out_specs=P(("groups", "enc"), ("ctx", "tp"), None),
        check_vma=False,
    )
```

```python
import functools

import jax
import jax.numpy as jnp
from jax import lax
from jax.experimental import pallas as pl
from jax.experimental.pallas import tpu as pltpu
from jax.sharding import PartitionSpec as P

VMEM = pl.BlockSpec(memory_space=pltpu.VMEM)
HBM = pl.BlockSpec(memory_space=pltpu.HBM)
PARAMS = pltpu.CompilerParams(vmem_limit_bytes=12 << 20)
SUM_FLOPS = 1 << 35
BF16, F32, I32 = jnp.bfloat16, jnp.float32, jnp.int32


def cost(flops, moved):
    return pl.CostEstimate(flops=flops // 16, bytes_accessed=moved // 16, transcendentals=0)


def to_tiles(x, out):
    at = 0
    for r in range(0, x.shape[0], 16):
        for c in range(0, x.shape[1], 128):
            out[at : at + 16, :] = x[r : r + 16, c : c + 128]
            at += 16


def from_tiles(tiles, width):
    per_row = width // 128
    lines = []
    for r in range(0, tiles.shape[0], 16 * per_row):
        line = [tiles[r + 16 * c : r + 16 * (c + 1)] for c in range(per_row)]
        lines.append(jnp.concatenate(line, axis=1))
    return jnp.concatenate(lines, axis=0)


def send_kernel(cuts, rows, slot, kind, *refs):
    outs, (rows_here, slot_here, kind_here, sems) = refs[: len(cuts)], refs[-4:]
    whole, width = rows.shape
    half = whole // 2
    z, t = lax.axis_index("ctx"), lax.axis_index("tp")
    dealt = len(cuts) > 1
    source = rows
    if not dealt:
        source = rows.at[pl.ds(pl.multiple_of(t * half, half), half), :]
    copies = [
        pltpu.make_async_copy(slot, slot_here, sems.at[0]),
        pltpu.make_async_copy(kind, kind_here, sems.at[1]),
        pltpu.make_async_copy(source, rows_here, sems.at[2]),
    ]
    for copy in copies:
        copy.start()
    copies[0].wait()
    copies[1].wait()
    if dealt:
        slot_row, slot_col = slot_here[...], column_of(slot_here[...])
        kind_col = column_of(kind_here[...])
        rank_row = jnp.sum((slot_col < slot_row).astype(I32), axis=0, keepdims=True)
        rank_col = jnp.sum((slot_row < slot_col).astype(I32), axis=1, keepdims=True)
        refs[len(cuts)][...] = lax.rem(rank_row, 2)

        def rank_at(k):
            odd = (k >= half // 2).astype(I32)
            return t * half + 2 * (k - odd * (half // 2)) + odd

        here = rank_col == rank_at(lax.broadcasted_iota(I32, (1, half), 1))
        slots = jnp.sum(jnp.where(here, slot_col, 0), axis=0, keepdims=True)
        kinds = jnp.sum(jnp.where(here, kind_col, 0), axis=0, keepdims=True)
        deal = rank_row == rank_at(lax.broadcasted_iota(I32, (half, 1), 0))
        copies[2].wait()
        rows_out = refs[-5]
        rows_out[...] = jnp.dot(
            deal.astype(F32).astype(BF16), rows_here[...], preferred_element_type=F32
        ).astype(BF16)
    else:
        slots = jnp.where(t == 0, slot_here[:, :half], slot_here[:, half:])
        kinds = jnp.where(t == 0, kind_here[:, :half], kind_here[:, half:])
        copies[2].wait()
        rows_out = rows_here
    for out, parity in zip(outs, cuts):
        x, s, k = rows_out, slots, kinds
        size = half
        if parity is not None:
            size = half // 2
            second = lax.rem(z + parity, 2)
            x = rows_out.at[pl.ds(pl.multiple_of(second * size, size), size), :]
            s = jnp.where(second == 0, slots[:, :size], slots[:, size:])
            k = jnp.where(second == 0, kinds[:, :size], kinds[:, size:])
        to_tiles(x, out)
        line = lax.broadcasted_iota(I32, (16, size), 0)
        index = jnp.where(line == 0, s // 256, jnp.where(line == 1, s % 256, k))
        index = jnp.where(line < 3, index, 0).astype(F32)
        if size < 128:
            index = jnp.concatenate([index, jnp.zeros((16, 128 - size), F32)], axis=1)
        out[size * width // 128 :, :] = index.astype(BF16)


def to_send(cuts, rows, slot, kind):
    half, width = rows.shape[0] // 2, rows.shape[1]
    sizes = [half if parity is None else half // 2 for parity in cuts]
    shapes = [(size * width // 128 + 16, 128) for size in sizes]
    dealt = len(cuts) > 1
    out_shape = [jax.ShapeDtypeStruct(shape, BF16) for shape in shapes]
    scratch = [pltpu.VMEM((half, width), BF16)]
    if dealt:
        out_shape.append(jax.ShapeDtypeStruct(slot.shape, I32))
        scratch.append(pltpu.VMEM(rows.shape, BF16))
    return pl.pallas_call(
        functools.partial(send_kernel, cuts),
        out_shape=out_shape,
        in_specs=[HBM] * 3,
        out_specs=[VMEM] * len(out_shape),
        scratch_shapes=scratch
        + [
            pltpu.VMEM(slot.shape, I32),
            pltpu.VMEM(slot.shape, I32),
            pltpu.SemaphoreType.DMA((3,)),
        ],
        compiler_params=pltpu.CompilerParams(vmem_limit_bytes=60 << 20),
        cost_estimate=cost(0, 4 * half * width),
        name="to_send",
    )(rows, slot, kind)


def column_of(row_vector):
    r = row_vector.shape[1]
    diagonal = lax.broadcasted_iota(I32, (r, r), 0) == lax.broadcasted_iota(I32, (r, r), 1)
    return jnp.sum(jnp.where(diagonal, row_vector, 0), axis=1, keepdims=True)


def project(kind_row, x, w_audio, w_frame, b_audio, b_frame, out):
    is_audio = column_of(kind_row) == 0
    audio = jnp.dot(x, w_audio[...], preferred_element_type=F32)
    frame = jnp.dot(x, w_frame[...], preferred_element_type=F32)
    audio = audio + b_audio[...].astype(F32)
    frame = frame + b_frame[...].astype(F32)
    out[...] = jnp.where(is_audio, audio, frame).astype(out.dtype)


def project_own_kernel(kind, x, wa, wf, ba, bf, out):
    project(kind[...], x[...], wa, wf, ba, bf, out)


def project_own(kind, rows, weights):
    ew, cols = weights[0].shape
    return pl.pallas_call(
        project_own_kernel,
        out_shape=jax.ShapeDtypeStruct((rows.shape[0], cols), BF16),
        in_specs=[VMEM] * 6,
        out_specs=VMEM,
        compiler_params=PARAMS,
        cost_estimate=cost(4 * rows.shape[0] * ew * cols, 4 * ew * cols),
        name="project_own",
    )(kind, rows, *weights)


def project_parts_kernel(wa, wf, ba, bf, *refs):
    parts, out, slots = refs[:-2], refs[-2], refs[-1]
    width = wa.shape[0]
    x, index = [], []
    for ref in parts:
        for k in range(ref.shape[0]):
            lines = ref.shape[1] - 16
            size = lines * 128 // width
            x.append(from_tiles(ref[k, :lines, :], width))
            index.append(ref[k, lines:, :].astype(F32).astype(I32)[:, :size])
    x = x[0] if len(x) == 1 else jnp.concatenate(x, axis=0)
    index = index[0] if len(index) == 1 else jnp.concatenate(index, axis=1)
    slots[...] = index[0:1] * 256 + index[1:2]
    project(index[2:3], x, wa, wf, ba, bf, out)


def project_parts(parts, weights):
    ew, cols = weights[0].shape
    rows = sum(p.shape[0] * (p.shape[1] - 16) * 128 // ew for p in parts)
    return pl.pallas_call(
        project_parts_kernel,
        out_shape=[jax.ShapeDtypeStruct((rows, cols), BF16), jax.ShapeDtypeStruct((1, rows), I32)],
        in_specs=[VMEM] * (4 + len(parts)),
        out_specs=[VMEM] * 2,
        compiler_params=PARAMS,
        cost_estimate=cost(4 * rows * ew * cols, 4 * ew * cols),
        name="project_parts",
    )(*weights, *parts)


def select_kernel(m, count, *refs):
    blocks, slots, outs = refs[:count], refs[count : 2 * count], refs[2 * count :]
    places = sum(out.shape[0] for out in outs) // 2
    z, t = lax.axis_index("ctx"), lax.axis_index("tp")
    first = jnp.bitwise_xor(z, m) * 2 * places
    i = lax.broadcasted_iota(I32, (2 * places, 1), 0)
    position = first + jnp.bitwise_xor(i, t * places)
    total = None
    for block, slot in zip(blocks, slots):
        chosen = (slot[...] == position).astype(F32).astype(BF16)
        part = jnp.dot(chosen, block[...], preferred_element_type=F32)
        total = part if total is None else total + part
    at = 0
    for out in outs:
        out[...] = total[at : at + out.shape[0]].astype(BF16)
        at += out.shape[0]


def select(m, blocks, slots, sizes):
    rows, cols = sum(b.shape[0] for b in blocks), blocks[0].shape[1]
    return pl.pallas_call(
        functools.partial(select_kernel, m, len(blocks)),
        out_shape=[jax.ShapeDtypeStruct((size, cols), BF16) for size in sizes],
        in_specs=[VMEM] * (2 * len(blocks)),
        out_specs=[VMEM] * len(sizes),
        compiler_params=PARAMS,
        cost_estimate=cost(2 * sum(sizes) * rows * cols, 2 * rows * cols),
        name="select",
    )(*blocks, *slots)


def upto(places, width):
    i = lax.broadcasted_iota(I32, (width, width), 0)
    j = lax.broadcasted_iota(I32, (width, width), 1)
    counts = i <= j
    if width > places:
        counts = jnp.logical_and(counts, (i < places) == (j < places))
    return counts.astype(F32).astype(BF16)


def one_hot(found):
    return found.astype(F32).astype(BF16)


def over_rows(a, b):
    return lax.dot_general(a, b, (((1,), (1,)), ((), ())), preferred_element_type=F32)


def running(flags, counts):
    return jnp.dot(one_hot(flags), counts, preferred_element_type=F32)


def packet_kernel(m, early, count, second, *refs):
    blocks, slots, outs = refs[:count], refs[count : 2 * count], refs[2 * count :]
    size = outs[0].shape[0]
    places = blocks[0].shape[0] // 2
    first_size = places - size if second else size
    z, t = lax.axis_index("ctx"), lax.axis_index("tp")
    i = lax.broadcasted_iota(I32, (2 * places, 1), 0)
    position = jnp.bitwise_xor(z, m) * 2 * places + jnp.bitwise_xor(i, t * places)
    holds = [one_hot(slot[...] == position) for slot in slots]
    known = None
    for k in range(early):
        part = over_rows(jnp.ones((8, holds[k].shape[1]), BF16), holds[k])
        known = part if known is None else known + part
    counts = upto(places, 2 * places)
    wanted = known > 0.5
    number = running(wanted, counts)
    if second:
        wanted = jnp.logical_not(jnp.logical_and(wanted, number < first_size + 0.5))
        number = running(wanted, counts)
    number = jnp.where(wanted, number, 0.0)[0:1].astype(I32)
    e = lax.broadcasted_iota(I32, (2 * size, 1), 0)
    upper = (e >= size).astype(I32)
    lane_upper = (lax.broadcasted_iota(I32, (1, 2 * places), 1) >= places).astype(I32)
    pick = jnp.logical_and(number == e - upper * size + 1, lane_upper == upper)
    pick = one_hot(pick)
    total = None
    for block, hold in zip(blocks, holds):
        chosen = jnp.dot(pick, hold, preferred_element_type=F32).astype(BF16)
        part = jnp.dot(chosen, block[...], preferred_element_type=F32)
        total = part if total is None else total + part
    outs[0][...] = total[:size].astype(BF16)
    outs[1][...] = total[size:].astype(BF16)


def packet(m, early, blocks, slots, size, second):
    rows, cols = sum(b.shape[0] for b in blocks), blocks[0].shape[1]
    return pl.pallas_call(
        functools.partial(packet_kernel, m, early, len(blocks), second),
        out_shape=[jax.ShapeDtypeStruct((size, cols), BF16)] * 2,
        in_specs=[VMEM] * (2 * len(blocks)),
        out_specs=[VMEM] * 2,
        compiler_params=PARAMS,
        cost_estimate=cost(4 * size * rows * cols, 2 * rows * cols),
        name="packet",
    )(*blocks, *slots)


def order_kernel(first_size, parity, *refs):
    slots, outs = refs[:-2], refs[-2:]
    places = outs[0].shape[0]
    z, t = lax.axis_index("ctx"), lax.axis_index("tp")
    pair, odd = z // 2, lax.rem(z, 2)
    position = (2 * z + t) * places + lax.broadcasted_iota(I32, (places, 1), 0)
    source = lax.broadcasted_iota(I32, (8, 1), 0)
    known = None
    for k, slot in enumerate(slots):
        width = slot.shape[1]
        lane = lax.broadcasted_iota(I32, (1, width), 1)
        if k == 0:
            near, odd_rank = lane >= 0, parity[...]
        elif k in (1, 2):
            near = lane < places
            odd_rank = jnp.where(near, (lane >= places // 2).astype(I32), odd)
        else:
            near, odd_rank = lane < 0, jnp.zeros((1, width), I32) + 1 - odd
        owner_pair = jnp.where(near, pair, 1 - pair)
        held = jnp.logical_or(owner_pair == source // 2, odd_rank == lax.rem(source, 2))
        part = over_rows(one_hot(held), one_hot(slot[...] == position))
        known = part if known is None else known + part
    counts = upto(places, places)
    early = known > 0.5
    number = running(early, counts)
    early = jnp.logical_and(early, number < first_size + 0.5)
    later = running(jnp.logical_not(early), counts)
    place = jnp.where(early, number, later + first_size) - 1.0
    for m, out in zip((3, 2), outs):
        row = jnp.sum(jnp.where(source == jnp.bitwise_xor(z, m), place, 0.0), axis=0, keepdims=True)
        column = column_of(row.astype(I32))
        out[...] = one_hot(column == lax.broadcasted_iota(I32, (1, places), 1))


def order_of(first_size, parity, slots, places):
    return pl.pallas_call(
        functools.partial(order_kernel, first_size),
        out_shape=[jax.ShapeDtypeStruct((places, places), BF16)] * 2,
        in_specs=[VMEM] * (1 + len(slots)),
        out_specs=[VMEM] * 2,
        compiler_params=PARAMS,
        cost_estimate=cost(SUM_FLOPS, 0),
        name="order_of",
    )(parity, *slots)


def place_kernel(has_total, *refs):
    total = refs[0][...] if has_total else None
    order, packets, outs = refs[has_total], refs[has_total + 1 : has_total + 5], refs[-3:]
    for d in range(2):
        both = jnp.concatenate([packets[2 * d][...], packets[2 * d + 1][...]], axis=0)
        wide = jnp.dot(order[...], both, preferred_element_type=F32)
        outs[d][...] = wide.astype(BF16)
        part = jnp.sum(wide * wide, axis=1, keepdims=True)
        total = part if total is None else total + part
    outs[2][...] = total


def place(total, order, packets):
    places, cols = order.shape[0], packets[0].shape[1]
    operands = ([] if total is None else [total]) + [order] + packets
    return pl.pallas_call(
        functools.partial(place_kernel, len(operands) - 5),
        out_shape=[jax.ShapeDtypeStruct((places, cols), BF16)] * 2
        + [jax.ShapeDtypeStruct((places, 1), F32)],
        in_specs=[VMEM] * len(operands),
        out_specs=[VMEM] * 3,
        compiler_params=PARAMS,
        cost_estimate=cost(SUM_FLOPS, 0),
        name="place",
    )(*operands)


def view(ref, places):
    if len(ref.shape) == 3:
        return ref.at[1 - lax.axis_index("tp")]
    return ref.at[pl.ds(0, places), :]


def square_sum(piece):
    wide = piece[...].astype(F32)
    return jnp.sum(wide * wide, axis=1, keepdims=True)


def squares_kernel(*refs):
    out = refs[-1]
    total = None
    for ref in refs[:-1]:
        part = ref[...] if ref.dtype == F32 else square_sum(view(ref, out.shape[0]))
        total = part if total is None else total + part
    out[...] = total


def squares(total, pieces, places):
    operands = pieces if total is None else [total] + pieces
    return pl.pallas_call(
        squares_kernel,
        out_shape=jax.ShapeDtypeStruct((places, 1), F32),
        in_specs=[VMEM] * len(operands),
        out_specs=VMEM,
        compiler_params=PARAMS,
        cost_estimate=cost(SUM_FLOPS, 0),
        name="squares",
    )(*operands)


def norm_kernel(places_of, fresh, gain, before, *refs):
    n = len(places_of)
    out, scaled, sems = refs[n], refs[n + 1], refs[n + 2]
    places, cols = scaled.shape[1:]
    pieces = [view(ref, places) for ref in refs[:n]]
    z, t = lax.axis_index("ctx"), lax.axis_index("tp")
    total = before[...]
    for k in fresh:
        total = total + square_sum(pieces[k])
    scale = lax.rsqrt(total / (n * cols) + 1e-06)
    copies = []
    for k, ((m, d), piece) in enumerate(zip(places_of, pieces)):
        block = jnp.bitwise_xor(z, m) * 2 + jnp.bitwise_xor(t, d)
        at = pl.ds(pl.multiple_of(block * cols, cols), cols)
        scaled[k] = (piece[...].astype(F32) * scale * gain[:, at].astype(F32)).astype(BF16)
        copies.append(pltpu.make_async_copy(scaled.at[k], out.at[:, at], sems.at[k]))
        copies[k].start()
    for copy in copies:
        copy.wait()


def norm(places_of, fresh, gain, before, pieces):
    n, places, cols = len(pieces), before.shape[0], pieces[0].shape[-1]
    return pl.pallas_call(
        functools.partial(norm_kernel, places_of, fresh),
        out_shape=jax.ShapeDtypeStruct((places, n * cols), BF16),
        in_specs=[VMEM] * (n + 2),
        out_specs=HBM,
        scratch_shapes=[pltpu.VMEM((n, places, cols), BF16), pltpu.SemaphoreType.DMA((n,))],
        compiler_params=PARAMS,
        cost_estimate=cost(4 * places * n * cols, 4 * places * n * cols),
        name="norm",
    )(gain, before, *pieces)


def after(x, *others):
    return lax.optimization_barrier((x, *others))[0]


def body(enc_rows, row_slot, row_kind, audio_proj, frame_proj, audio_bias, frame_bias, norm_gain):
    n = lax.axis_size("ctx")
    rows = enc_rows[0]
    half = rows.shape[0] // 2
    weights = (audio_proj, frame_proj, audio_bias[None, :], frame_bias[None, :])

    def over_ctx(x, m):
        return lax.ppermute(x, "ctx", [(i, i ^ m) for i in range(n)])

    def over_tp(x):
        return lax.ppermute(x, "tp", [(0, 1), (1, 0)])

    own = project_own(row_kind, rows, weights)
    blocks, slots = [own], [row_slot]

    def take(group):
        block, slot = project_parts(group, weights)
        blocks.append(block)
        slots.append(slot)

    def to_core(x, m, d):
        pairs = [(i * 2 + c, (i ^ m) * 2 + (c ^ d)) for i in range(n) for c in range(2)]
        return lax.ppermute(x, ("ctx", "tp"), pairs)

    def own_and_near(total):
        pieces[0, 0], other = select(0, blocks, slots, [half, half])
        pieces[0, 1] = lax.all_gather(other, "tp", axis=0)
        total = squares(total, [pieces[0, 0], pieces[0, 1]], half)
        pair = pieces[1]
        pieces[1, 0], pieces[1, 1] = pair, lax.all_gather(pair[half:], "tp", axis=0)
        return squares(total, [pieces[1, 0], pieces[1, 1]], half)

    pieces = {}
    if n == 4:
        near, second, third, parity = to_send((None, 0, 1), rows, row_slot, row_kind)
        near, second, third = over_ctx(near, 1), over_ctx(second, 2), over_ctx(third, 3)
        first = lax.optimization_barrier((near, second, third, own))[:3]
        shared = [over_ctx(part, 1) for part in first[1:]]
        other = [over_tp(part)[None] for part in first]
        take([part[None] for part in first])
        other = lax.optimization_barrier((*other, blocks[-1]))[:3]
        take(other)

        early, size = len(blocks), 3 * half // 8
        sent = {}
        for m in (3, 2):
            chosen = packet(m, early, blocks, slots, size, False)
            slots[0] = after(slots[0], chosen[0])
            sent[m] = [to_core(piece, m, d) for d, piece in enumerate(chosen)]
        shared = lax.optimization_barrier((*shared, blocks[-1]))[:2]
        take([lax.all_gather(part, "tp", axis=0) for part in shared])

        (chosen,) = select(1, blocks, slots, [2 * half])
        slots[0] = after(slots[0], chosen)
        pieces[1] = over_ctx(chosen, 1)
        rest = {}
        for m in (3, 2):
            chosen = packet(m, early, blocks, slots, half - size, True)
            slots[0] = after(slots[0], chosen[0])
            joined = lax.optimization_barrier((*chosen, *sent[3], *sent[2]))
            chosen, sent[3], sent[2] = joined[:2], list(joined[2:4]), list(joined[4:])
            rest[m] = [to_core(piece, m, d) for d, piece in enumerate(chosen)]

        order3, order2 = order_of(size, parity, slots, half)
        packets = [sent[3][0], rest[3][0], sent[3][1], rest[3][1]]
        pieces[3, 0], pieces[3, 1], total = place(None, order3, packets)
        total = own_and_near(total)
        packets = [sent[2][0], rest[2][0], sent[2][1], rest[2][1]]
        pieces[2, 0], pieces[2, 1], total = place(total, order2, packets)
        order, fresh = [3, 1, 0, 2], ()
    else:
        (mine,) = to_send((None,), rows, row_slot, row_kind)
        arrived = [over_ctx(mine, m) for m in range(1, n)]
        for direct in arrived[:-1]:
            direct = after(direct, blocks[-1])
            take([lax.all_gather(direct, "tp", axis=0)])
        direct = after(arrived[-1], blocks[-1])
        swapped = over_tp(direct)
        take([direct[None]])
        take([swapped[None]])

        order = [n - 1, 1] + list(reversed(range(2, n - 1)))
        for m in order:
            chosen = select(m, blocks, slots, [2 * half] if m == 1 else [half, half])
            slots[0] = after(slots[0], chosen[0])
            if m == 1:
                pieces[m] = over_ctx(chosen[0], m)
                continue
            for d, piece in enumerate(chosen):
                pieces[m, d] = to_core(piece, m, d)
        total = squares(None, [pieces[n - 1, 0], pieces[n - 1, 1]], half)
        total = own_and_near(total)
        for m in order[2:-1]:
            late = [after(pieces[m, d], total) for d in range(2)]
            total = squares(total, late, half)
        fresh = (2 * (n - 1), 2 * (n - 1) + 1)
        for d in range(2):
            pieces[order[-1], d] = after(pieces[order[-1], d], total)
        order = order[:-1] + [0, order[-1]]

    places_of = tuple((m, d) for m in order for d in range(2))
    return norm(places_of, fresh, norm_gain[None, :], total, [pieces[at] for at in places_of])[None]


def solution(mesh):
    return jax.shard_map(
        body,
        mesh=mesh,
        in_specs=(
            P(("groups", "enc"), "ctx", None),
            P(("groups", "enc"), "ctx"),
            P(("groups", "enc"), "ctx"),
            P(None, ("ctx", "tp")),
            P(None, ("ctx", "tp")),
            P(("ctx", "tp")),
            P(("ctx", "tp")),
            P(),
        ),
        out_specs=P(("groups", "enc"), ("ctx", "tp"), None),
        check_vma=False,
    )
```

```python
import functools

import jax
import jax.numpy as jnp
from jax import lax
from jax.experimental import pallas as pl
from jax.experimental.pallas import tpu as pltpu
from jax.sharding import PartitionSpec as P

VMEM = pl.BlockSpec(memory_space=pltpu.VMEM)
HBM = pl.BlockSpec(memory_space=pltpu.HBM)
PARAMS = pltpu.CompilerParams(vmem_limit_bytes=12 << 20)
SUM_FLOPS = 1 << 35
BF16, F32, I32 = jnp.bfloat16, jnp.float32, jnp.int32


def cost(flops, moved):
    return pl.CostEstimate(flops=flops // 16, bytes_accessed=moved // 16, transcendentals=0)


def to_tiles(x, out):
    at = 0
    for r in range(0, x.shape[0], 16):
        for c in range(0, x.shape[1], 128):
            out[at : at + 16, :] = x[r : r + 16, c : c + 128]
            at += 16


def from_tiles(tiles, width):
    per_row = width // 128
    lines = []
    for r in range(0, tiles.shape[0], 16 * per_row):
        line = [tiles[r + 16 * c : r + 16 * (c + 1)] for c in range(per_row)]
        lines.append(jnp.concatenate(line, axis=1))
    return jnp.concatenate(lines, axis=0)


def send_kernel(cuts, rows, slot, kind, *refs):
    outs, (rows_here, slot_here, kind_here, sems) = refs[: len(cuts)], refs[-4:]
    whole, width = rows.shape
    half = whole // 2
    z, t = lax.axis_index("ctx"), lax.axis_index("tp")
    dealt = len(cuts) > 1
    source = rows
    if not dealt:
        source = rows.at[pl.ds(pl.multiple_of(t * half, half), half), :]
    copies = [
        pltpu.make_async_copy(slot, slot_here, sems.at[0]),
        pltpu.make_async_copy(kind, kind_here, sems.at[1]),
        pltpu.make_async_copy(source, rows_here, sems.at[2]),
    ]
    for copy in copies:
        copy.start()
    copies[0].wait()
    copies[1].wait()
    if dealt:
        slot_row, slot_col = slot_here[...], column_of(slot_here[...])
        kind_col = column_of(kind_here[...])
        rank_row = jnp.sum((slot_col < slot_row).astype(I32), axis=0, keepdims=True)
        rank_col = jnp.sum((slot_row < slot_col).astype(I32), axis=1, keepdims=True)
        refs[len(cuts)][...] = lax.rem(rank_row, 2)

        def rank_at(k):
            odd = (k >= half // 2).astype(I32)
            return t * half + 2 * (k - odd * (half // 2)) + odd

        here = rank_col == rank_at(lax.broadcasted_iota(I32, (1, half), 1))
        slots = jnp.sum(jnp.where(here, slot_col, 0), axis=0, keepdims=True)
        kinds = jnp.sum(jnp.where(here, kind_col, 0), axis=0, keepdims=True)
        deal = rank_row == rank_at(lax.broadcasted_iota(I32, (half, 1), 0))
        copies[2].wait()
        rows_out = refs[-5]
        rows_out[...] = jnp.dot(
            deal.astype(F32).astype(BF16), rows_here[...], preferred_element_type=F32
        ).astype(BF16)
    else:
        slots = jnp.where(t == 0, slot_here[:, :half], slot_here[:, half:])
        kinds = jnp.where(t == 0, kind_here[:, :half], kind_here[:, half:])
        copies[2].wait()
        rows_out = rows_here
    for out, parity in zip(outs, cuts):
        x, s, k = rows_out, slots, kinds
        size = half
        if parity is not None:
            size = half // 2
            second = lax.rem(z + parity, 2)
            x = rows_out.at[pl.ds(pl.multiple_of(second * size, size), size), :]
            s = jnp.where(second == 0, slots[:, :size], slots[:, size:])
            k = jnp.where(second == 0, kinds[:, :size], kinds[:, size:])
        to_tiles(x, out)
        line = lax.broadcasted_iota(I32, (16, size), 0)
        index = jnp.where(line == 0, s // 256, jnp.where(line == 1, s % 256, k))
        index = jnp.where(line < 3, index, 0).astype(F32)
        if size < 128:
            index = jnp.concatenate([index, jnp.zeros((16, 128 - size), F32)], axis=1)
        out[size * width // 128 :, :] = index.astype(BF16)


def to_send(cuts, rows, slot, kind):
    half, width = rows.shape[0] // 2, rows.shape[1]
    sizes = [half if parity is None else half // 2 for parity in cuts]
    shapes = [(size * width // 128 + 16, 128) for size in sizes]
    dealt = len(cuts) > 1
    out_shape = [jax.ShapeDtypeStruct(shape, BF16) for shape in shapes]
    scratch = [pltpu.VMEM((half, width), BF16)]
    if dealt:
        out_shape.append(jax.ShapeDtypeStruct(slot.shape, I32))
        scratch.append(pltpu.VMEM(rows.shape, BF16))
    return pl.pallas_call(
        functools.partial(send_kernel, cuts),
        out_shape=out_shape,
        in_specs=[HBM] * 3,
        out_specs=[VMEM] * len(out_shape),
        scratch_shapes=scratch
        + [
            pltpu.VMEM(slot.shape, I32),
            pltpu.VMEM(slot.shape, I32),
            pltpu.SemaphoreType.DMA((3,)),
        ],
        compiler_params=pltpu.CompilerParams(vmem_limit_bytes=60 << 20),
        cost_estimate=cost(0, 4 * half * width),
        name="to_send",
    )(rows, slot, kind)


def column_of(row_vector):
    r = row_vector.shape[1]
    diagonal = lax.broadcasted_iota(I32, (r, r), 0) == lax.broadcasted_iota(I32, (r, r), 1)
    return jnp.sum(jnp.where(diagonal, row_vector, 0), axis=1, keepdims=True)


def project(kind_row, x, w_audio, w_frame, b_audio, b_frame, out):
    is_audio = column_of(kind_row) == 0
    audio = jnp.dot(x, w_audio[...], preferred_element_type=F32)
    frame = jnp.dot(x, w_frame[...], preferred_element_type=F32)
    audio = audio + b_audio[...].astype(F32)
    frame = frame + b_frame[...].astype(F32)
    out[...] = jnp.where(is_audio, audio, frame).astype(out.dtype)


def project_own_kernel(kind, x, wa, wf, ba, bf, out):
    project(kind[...], x[...], wa, wf, ba, bf, out)


def project_own(kind, rows, weights):
    ew, cols = weights[0].shape
    return pl.pallas_call(
        project_own_kernel,
        out_shape=jax.ShapeDtypeStruct((rows.shape[0], cols), BF16),
        in_specs=[VMEM] * 6,
        out_specs=VMEM,
        compiler_params=PARAMS,
        cost_estimate=cost(4 * rows.shape[0] * ew * cols, 4 * ew * cols),
        name="project_own",
    )(kind, rows, *weights)


def project_parts_kernel(wa, wf, ba, bf, *refs):
    parts, out, slots = refs[:-2], refs[-2], refs[-1]
    width = wa.shape[0]
    x, index = [], []
    for ref in parts:
        for k in range(ref.shape[0]):
            lines = ref.shape[1] - 16
            size = lines * 128 // width
            x.append(from_tiles(ref[k, :lines, :], width))
            index.append(ref[k, lines:, :].astype(F32).astype(I32)[:, :size])
    x = x[0] if len(x) == 1 else jnp.concatenate(x, axis=0)
    index = index[0] if len(index) == 1 else jnp.concatenate(index, axis=1)
    slots[...] = index[0:1] * 256 + index[1:2]
    project(index[2:3], x, wa, wf, ba, bf, out)


def project_parts(parts, weights):
    ew, cols = weights[0].shape
    rows = sum(p.shape[0] * (p.shape[1] - 16) * 128 // ew for p in parts)
    return pl.pallas_call(
        project_parts_kernel,
        out_shape=[jax.ShapeDtypeStruct((rows, cols), BF16), jax.ShapeDtypeStruct((1, rows), I32)],
        in_specs=[VMEM] * (4 + len(parts)),
        out_specs=[VMEM] * 2,
        compiler_params=PARAMS,
        cost_estimate=cost(4 * rows * ew * cols, 4 * ew * cols),
        name="project_parts",
    )(*weights, *parts)


def select_kernel(m, count, *refs):
    blocks, slots, outs = refs[:count], refs[count : 2 * count], refs[2 * count :]
    places = sum(out.shape[0] for out in outs) // 2
    z, t = lax.axis_index("ctx"), lax.axis_index("tp")
    first = jnp.bitwise_xor(z, m) * 2 * places
    i = lax.broadcasted_iota(I32, (2 * places, 1), 0)
    position = first + jnp.bitwise_xor(i, t * places)
    total = None
    for block, slot in zip(blocks, slots):
        chosen = (slot[...] == position).astype(F32).astype(BF16)
        part = jnp.dot(chosen, block[...], preferred_element_type=F32)
        total = part if total is None else total + part
    at = 0
    for out in outs:
        out[...] = total[at : at + out.shape[0]].astype(BF16)
        at += out.shape[0]


def select(m, blocks, slots, sizes):
    rows, cols = sum(b.shape[0] for b in blocks), blocks[0].shape[1]
    return pl.pallas_call(
        functools.partial(select_kernel, m, len(blocks)),
        out_shape=[jax.ShapeDtypeStruct((size, cols), BF16) for size in sizes],
        in_specs=[VMEM] * (2 * len(blocks)),
        out_specs=[VMEM] * len(sizes),
        compiler_params=PARAMS,
        cost_estimate=cost(2 * sum(sizes) * rows * cols, 2 * rows * cols),
        name="select",
    )(*blocks, *slots)


def upto(places, width):
    i = lax.broadcasted_iota(I32, (width, width), 0)
    j = lax.broadcasted_iota(I32, (width, width), 1)
    counts = i <= j
    if width > places:
        counts = jnp.logical_and(counts, (i < places) == (j < places))
    return counts.astype(F32).astype(BF16)


def one_hot(found):
    return found.astype(F32).astype(BF16)


def over_rows(a, b):
    return lax.dot_general(a, b, (((1,), (1,)), ((), ())), preferred_element_type=F32)


def running(flags, counts):
    return jnp.dot(one_hot(flags), counts, preferred_element_type=F32)


def packet_kernel(m, early, count, second, *refs):
    blocks, slots, outs = refs[:count], refs[count : 2 * count], refs[2 * count :]
    size = outs[0].shape[0]
    places = blocks[0].shape[0] // 2
    first_size = places - size if second else size
    z, t = lax.axis_index("ctx"), lax.axis_index("tp")
    i = lax.broadcasted_iota(I32, (2 * places, 1), 0)
    position = jnp.bitwise_xor(z, m) * 2 * places + jnp.bitwise_xor(i, t * places)
    holds = [one_hot(slot[...] == position) for slot in slots]
    known = None
    for k in range(early):
        part = over_rows(jnp.ones((8, holds[k].shape[1]), BF16), holds[k])
        known = part if known is None else known + part
    counts = upto(places, 2 * places)
    wanted = known > 0.5
    number = running(wanted, counts)
    if second:
        wanted = jnp.logical_not(jnp.logical_and(wanted, number < first_size + 0.5))
        number = running(wanted, counts)
    number = jnp.where(wanted, number, 0.0)[0:1].astype(I32)
    e = lax.broadcasted_iota(I32, (2 * size, 1), 0)
    upper = (e >= size).astype(I32)
    lane_upper = (lax.broadcasted_iota(I32, (1, 2 * places), 1) >= places).astype(I32)
    pick = jnp.logical_and(number == e - upper * size + 1, lane_upper == upper)
    pick = one_hot(pick)
    total = None
    for block, hold in zip(blocks, holds):
        chosen = jnp.dot(pick, hold, preferred_element_type=F32).astype(BF16)
        part = jnp.dot(chosen, block[...], preferred_element_type=F32)
        total = part if total is None else total + part
    outs[0][...] = total[:size].astype(BF16)
    outs[1][...] = total[size:].astype(BF16)


def packet(m, early, blocks, slots, size, second):
    rows, cols = sum(b.shape[0] for b in blocks), blocks[0].shape[1]
    return pl.pallas_call(
        functools.partial(packet_kernel, m, early, len(blocks), second),
        out_shape=[jax.ShapeDtypeStruct((size, cols), BF16)] * 2,
        in_specs=[VMEM] * (2 * len(blocks)),
        out_specs=[VMEM] * 2,
        compiler_params=PARAMS,
        cost_estimate=cost(4 * size * rows * cols, 2 * rows * cols),
        name="packet",
    )(*blocks, *slots)


def order_kernel(first_size, parity, *refs):
    slots, outs = refs[:-2], refs[-2:]
    places = outs[0].shape[0]
    z, t = lax.axis_index("ctx"), lax.axis_index("tp")
    pair, odd = z // 2, lax.rem(z, 2)
    position = (2 * z + t) * places + lax.broadcasted_iota(I32, (places, 1), 0)
    source = lax.broadcasted_iota(I32, (8, 1), 0)
    known = None
    for k, slot in enumerate(slots):
        width = slot.shape[1]
        lane = lax.broadcasted_iota(I32, (1, width), 1)
        if k == 0:
            near, odd_rank = lane >= 0, parity[...]
        elif k in (1, 2):
            near = lane < places
            odd_rank = jnp.where(near, (lane >= places // 2).astype(I32), odd)
        else:
            near, odd_rank = lane < 0, jnp.zeros((1, width), I32) + 1 - odd
        owner_pair = jnp.where(near, pair, 1 - pair)
        held = jnp.logical_or(owner_pair == source // 2, odd_rank == lax.rem(source, 2))
        part = over_rows(one_hot(held), one_hot(slot[...] == position))
        known = part if known is None else known + part
    counts = upto(places, places)
    early = known > 0.5
    number = running(early, counts)
    early = jnp.logical_and(early, number < first_size + 0.5)
    later = running(jnp.logical_not(early), counts)
    place = jnp.where(early, number, later + first_size) - 1.0
    for m, out in zip((3, 2), outs):
        row = jnp.sum(jnp.where(source == jnp.bitwise_xor(z, m), place, 0.0), axis=0, keepdims=True)
        column = column_of(row.astype(I32))
        out[...] = one_hot(column == lax.broadcasted_iota(I32, (1, places), 1))


def order_of(first_size, parity, slots, places):
    return pl.pallas_call(
        functools.partial(order_kernel, first_size),
        out_shape=[jax.ShapeDtypeStruct((places, places), BF16)] * 2,
        in_specs=[VMEM] * (1 + len(slots)),
        out_specs=[VMEM] * 2,
        compiler_params=PARAMS,
        cost_estimate=cost(SUM_FLOPS, 0),
        name="order_of",
    )(parity, *slots)


def place_kernel(has_total, *refs):
    total = refs[0][...] if has_total else None
    order, packets, outs = refs[has_total], refs[has_total + 1 : has_total + 5], refs[-3:]
    for d in range(2):
        both = jnp.concatenate([packets[2 * d][...], packets[2 * d + 1][...]], axis=0)
        wide = jnp.dot(order[...], both, preferred_element_type=F32)
        outs[d][...] = wide.astype(BF16)
        part = jnp.sum(wide * wide, axis=1, keepdims=True)
        total = part if total is None else total + part
    outs[2][...] = total


def place(total, order, packets):
    places, cols = order.shape[0], packets[0].shape[1]
    operands = ([] if total is None else [total]) + [order] + packets
    return pl.pallas_call(
        functools.partial(place_kernel, len(operands) - 5),
        out_shape=[jax.ShapeDtypeStruct((places, cols), BF16)] * 2
        + [jax.ShapeDtypeStruct((places, 1), F32)],
        in_specs=[VMEM] * len(operands),
        out_specs=[VMEM] * 3,
        compiler_params=PARAMS,
        cost_estimate=cost(SUM_FLOPS, 0),
        name="place",
    )(*operands)


def view(ref, places):
    if len(ref.shape) == 3:
        return ref.at[1 - lax.axis_index("tp")]
    return ref.at[pl.ds(0, places), :]


def square_sum(piece):
    wide = piece[...].astype(F32)
    return jnp.sum(wide * wide, axis=1, keepdims=True)


def squares_kernel(*refs):
    out = refs[-1]
    total = None
    for ref in refs[:-1]:
        part = ref[...] if ref.dtype == F32 else square_sum(view(ref, out.shape[0]))
        total = part if total is None else total + part
    out[...] = total


def squares(total, pieces, places):
    operands = pieces if total is None else [total] + pieces
    return pl.pallas_call(
        squares_kernel,
        out_shape=jax.ShapeDtypeStruct((places, 1), F32),
        in_specs=[VMEM] * len(operands),
        out_specs=VMEM,
        compiler_params=PARAMS,
        cost_estimate=cost(SUM_FLOPS, 0),
        name="squares",
    )(*operands)


def norm_kernel(places_of, fresh, gain, before, *refs):
    n = len(places_of)
    out, scaled, sems = refs[n], refs[n + 1], refs[n + 2]
    places, cols = scaled.shape[1:]
    pieces = [view(ref, places) for ref in refs[:n]]
    z, t = lax.axis_index("ctx"), lax.axis_index("tp")
    total = before[...]
    for k in fresh:
        total = total + square_sum(pieces[k])
    scale = lax.rsqrt(total / (n * cols) + 1e-06)
    copies = []
    for k, ((m, d), piece) in enumerate(zip(places_of, pieces)):
        block = jnp.bitwise_xor(z, m) * 2 + jnp.bitwise_xor(t, d)
        at = pl.ds(pl.multiple_of(block * cols, cols), cols)
        scaled[k] = (piece[...].astype(F32) * scale * gain[:, at].astype(F32)).astype(BF16)
        copies.append(pltpu.make_async_copy(scaled.at[k], out.at[:, at], sems.at[k]))
        copies[k].start()
    for copy in copies:
        copy.wait()


def norm(places_of, fresh, gain, before, pieces):
    n, places, cols = len(pieces), before.shape[0], pieces[0].shape[-1]
    return pl.pallas_call(
        functools.partial(norm_kernel, places_of, fresh),
        out_shape=jax.ShapeDtypeStruct((places, n * cols), BF16),
        in_specs=[VMEM] * (n + 2),
        out_specs=HBM,
        scratch_shapes=[pltpu.VMEM((n, places, cols), BF16), pltpu.SemaphoreType.DMA((n,))],
        compiler_params=PARAMS,
        cost_estimate=cost(4 * places * n * cols, 4 * places * n * cols),
        name="norm",
    )(gain, before, *pieces)


def last_kernel(far, whole, gain, before, order, *refs):
    packets, pieces, (out, scaled, sems) = refs[:4], refs[4:10], refs[10:]
    places, cols = scaled.shape[1:]
    z, t = lax.axis_index("ctx"), lax.axis_index("tp")
    total = before[...]
    for k in range(2):
        both = jnp.concatenate([packets[2 * k][...], packets[2 * k + 1][...]], axis=0)
        wide = jnp.dot(order[...], both, preferred_element_type=F32)
        scaled[k] = wide.astype(BF16)
        total = total + jnp.sum(wide * wide, axis=1, keepdims=True)
    scale = lax.rsqrt(total / (8 * cols) + 1e-06)
    copies = []
    for k, (m, d) in enumerate(far + whole):
        block = jnp.bitwise_xor(z, m) * 2 + jnp.bitwise_xor(t, d)
        at = pl.ds(pl.multiple_of(block * cols, cols), cols)
        piece = scaled[k] if k < 2 else view(pieces[k - 2], places)[...]
        scaled[k] = (piece.astype(F32) * scale * gain[:, at].astype(F32)).astype(BF16)
        copies.append(pltpu.make_async_copy(scaled.at[k], out.at[:, at], sems.at[k]))
        copies[k].start()
    for copy in copies:
        copy.wait()


def place_and_norm(far, whole, gain, before, order, packets, pieces):
    places, cols = before.shape[0], packets[0].shape[1]
    operands = [gain, before, order, *packets, *pieces]
    return pl.pallas_call(
        functools.partial(last_kernel, far, whole),
        out_shape=jax.ShapeDtypeStruct((places, 8 * cols), BF16),
        in_specs=[VMEM] * len(operands),
        out_specs=HBM,
        scratch_shapes=[pltpu.VMEM((8, places, cols), BF16), pltpu.SemaphoreType.DMA((8,))],
        compiler_params=PARAMS,
        cost_estimate=cost(32 * places * cols, 32 * places * cols),
        name="place_and_norm",
    )(*operands)


def after(x, *others):
    return lax.optimization_barrier((x, *others))[0]


def body(enc_rows, row_slot, row_kind, audio_proj, frame_proj, audio_bias, frame_bias, norm_gain):
    n = lax.axis_size("ctx")
    rows = enc_rows[0]
    half = rows.shape[0] // 2
    weights = (audio_proj, frame_proj, audio_bias[None, :], frame_bias[None, :])

    def over_ctx(x, m):
        return lax.ppermute(x, "ctx", [(i, i ^ m) for i in range(n)])

    def over_tp(x):
        return lax.ppermute(x, "tp", [(0, 1), (1, 0)])

    own = project_own(row_kind, rows, weights)
    blocks, slots = [own], [row_slot]

    def take(group):
        block, slot = project_parts(group, weights)
        blocks.append(block)
        slots.append(slot)

    def to_core(x, m, d):
        pairs = [(i * 2 + c, (i ^ m) * 2 + (c ^ d)) for i in range(n) for c in range(2)]
        return lax.ppermute(x, ("ctx", "tp"), pairs)

    def own_and_near(total):
        pieces[0, 0], other = select(0, blocks, slots, [half, half])
        pieces[0, 1] = lax.all_gather(other, "tp", axis=0)
        total = squares(total, [pieces[0, 0], pieces[0, 1]], half)
        pair = pieces[1]
        pieces[1, 0], pieces[1, 1] = pair, lax.all_gather(pair[half:], "tp", axis=0)
        return squares(total, [pieces[1, 0], pieces[1, 1]], half)

    pieces = {}
    if n == 4:
        near, second, third, parity = to_send((None, 0, 1), rows, row_slot, row_kind)
        near, second, third = over_ctx(near, 1), over_ctx(second, 2), over_ctx(third, 3)
        first = lax.optimization_barrier((near, second, third, own))[:3]
        shared = [over_ctx(part, 1) for part in first[1:]]
        other = [over_tp(part)[None] for part in first]
        take([part[None] for part in first])
        other = lax.optimization_barrier((*other, blocks[-1]))[:3]
        take(other)

        early, size = len(blocks), 3 * half // 8
        sent = {}
        for m in (3, 2):
            chosen = packet(m, early, blocks, slots, size, False)
            slots[0] = after(slots[0], chosen[0])
            sent[m] = [to_core(piece, m, d) for d, piece in enumerate(chosen)]
        shared = lax.optimization_barrier((*shared, blocks[-1]))[:2]
        take([lax.all_gather(part, "tp", axis=0) for part in shared])

        (chosen,) = select(1, blocks, slots, [2 * half])
        slots[0] = after(slots[0], chosen)
        pieces[1] = over_ctx(chosen, 1)
        rest = {}
        for m in (2, 3):
            chosen = packet(m, early, blocks, slots, half - size, True)
            slots[0] = after(slots[0], chosen[0])
            joined = lax.optimization_barrier((*chosen, *sent[3], *sent[2]))
            chosen, sent[3], sent[2] = joined[:2], list(joined[2:4]), list(joined[4:])
            rest[m] = [to_core(piece, m, d) for d, piece in enumerate(chosen)]

        order3, order2 = order_of(size, parity, slots, half)
        packets = [sent[2][0], rest[2][0], sent[2][1], rest[2][1]]
        pieces[2, 0], pieces[2, 1], total = place(None, order2, packets)
        total = own_and_near(total)
        packets = [sent[3][0], rest[3][0], sent[3][1], rest[3][1]]
        far, whole = ((3, 0), (3, 1)), ((2, 0), (2, 1), (1, 0), (1, 1), (0, 0), (0, 1))
        whole_pieces = [pieces[at] for at in whole]
        gain = norm_gain[None, :]
        return place_and_norm(far, whole, gain, total, order3, packets, whole_pieces)[None]
    else:
        (mine,) = to_send((None,), rows, row_slot, row_kind)
        arrived = [over_ctx(mine, m) for m in range(1, n)]
        for direct in arrived[:-1]:
            direct = after(direct, blocks[-1])
            take([lax.all_gather(direct, "tp", axis=0)])
        direct = after(arrived[-1], blocks[-1])
        swapped = over_tp(direct)
        take([direct[None]])
        take([swapped[None]])

        order = [n - 1, 1] + list(reversed(range(2, n - 1)))
        for m in order:
            chosen = select(m, blocks, slots, [2 * half] if m == 1 else [half, half])
            slots[0] = after(slots[0], chosen[0])
            if m == 1:
                pieces[m] = over_ctx(chosen[0], m)
                continue
            for d, piece in enumerate(chosen):
                pieces[m, d] = to_core(piece, m, d)
        total = squares(None, [pieces[n - 1, 0], pieces[n - 1, 1]], half)
        total = own_and_near(total)
        for m in order[2:-1]:
            late = [after(pieces[m, d], total) for d in range(2)]
            total = squares(total, late, half)
        fresh = (2 * (n - 1), 2 * (n - 1) + 1)
        for d in range(2):
            pieces[order[-1], d] = after(pieces[order[-1], d], total)
        order = order[:-1] + [0, order[-1]]

    places_of = tuple((m, d) for m in order for d in range(2))
    return norm(places_of, fresh, norm_gain[None, :], total, [pieces[at] for at in places_of])[None]


def solution(mesh):
    return jax.shard_map(
        body,
        mesh=mesh,
        in_specs=(
            P(("groups", "enc"), "ctx", None),
            P(("groups", "enc"), "ctx"),
            P(("groups", "enc"), "ctx"),
            P(None, ("ctx", "tp")),
            P(None, ("ctx", "tp")),
            P(("ctx", "tp")),
            P(("ctx", "tp")),
            P(),
        ),
        out_specs=P(("groups", "enc"), ("ctx", "tp"), None),
        check_vma=False,
    )
```

```python
import functools

import jax
import jax.numpy as jnp
from jax import lax
from jax.experimental import pallas as pl
from jax.experimental.pallas import tpu as pltpu
from jax.sharding import PartitionSpec as P

VMEM = pl.BlockSpec(memory_space=pltpu.VMEM)
HBM = pl.BlockSpec(memory_space=pltpu.HBM)
PARAMS = pltpu.CompilerParams(vmem_limit_bytes=12 << 20)
OWN_FLOPS, NEAR_FLOPS = 1 << 35, 0
BF16, F32, I32 = jnp.bfloat16, jnp.float32, jnp.int32


def cost(flops, moved):
    return pl.CostEstimate(flops=flops // 16, bytes_accessed=moved // 16, transcendentals=0)


def to_tiles(x, out):
    at = 0
    for r in range(0, x.shape[0], 16):
        for c in range(0, x.shape[1], 128):
            out[at : at + 16, :] = x[r : r + 16, c : c + 128]
            at += 16


def from_tiles(tiles, width):
    per_row = width // 128
    lines = []
    for r in range(0, tiles.shape[0], 16 * per_row):
        line = [tiles[r + 16 * c : r + 16 * (c + 1)] for c in range(per_row)]
        lines.append(jnp.concatenate(line, axis=1))
    return jnp.concatenate(lines, axis=0)


def send_kernel(cuts, rows, slot, kind, *refs):
    outs, (rows_here, slot_here, kind_here, sems) = refs[: len(cuts)], refs[-4:]
    whole, width = rows.shape
    half = whole // 2
    z, t = lax.axis_index("ctx"), lax.axis_index("tp")
    dealt = len(cuts) > 1
    source = rows
    if not dealt:
        source = rows.at[pl.ds(pl.multiple_of(t * half, half), half), :]
    copies = [
        pltpu.make_async_copy(slot, slot_here, sems.at[0]),
        pltpu.make_async_copy(kind, kind_here, sems.at[1]),
        pltpu.make_async_copy(source, rows_here, sems.at[2]),
    ]
    for copy in copies:
        copy.start()
    copies[0].wait()
    copies[1].wait()
    if dealt:
        slot_row, slot_col = slot_here[...], column_of(slot_here[...])
        kind_col = column_of(kind_here[...])
        rank_row = jnp.sum((slot_col < slot_row).astype(I32), axis=0, keepdims=True)
        rank_col = jnp.sum((slot_row < slot_col).astype(I32), axis=1, keepdims=True)
        refs[len(cuts)][...] = lax.rem(rank_row, 2)

        def rank_at(k):
            odd = (k >= half // 2).astype(I32)
            return t * half + 2 * (k - odd * (half // 2)) + odd

        here = rank_col == rank_at(lax.broadcasted_iota(I32, (1, half), 1))
        slots = jnp.sum(jnp.where(here, slot_col, 0), axis=0, keepdims=True)
        kinds = jnp.sum(jnp.where(here, kind_col, 0), axis=0, keepdims=True)
        deal = rank_row == rank_at(lax.broadcasted_iota(I32, (half, 1), 0))
        copies[2].wait()
        rows_out = refs[-5]
        rows_out[...] = jnp.dot(
            deal.astype(F32).astype(BF16), rows_here[...], preferred_element_type=F32
        ).astype(BF16)
    else:
        slots = jnp.where(t == 0, slot_here[:, :half], slot_here[:, half:])
        kinds = jnp.where(t == 0, kind_here[:, :half], kind_here[:, half:])
        copies[2].wait()
        rows_out = rows_here
    for out, parity in zip(outs, cuts):
        x, s, k = rows_out, slots, kinds
        size = half
        if parity is not None:
            size = half // 2
            second = lax.rem(z + parity, 2)
            x = rows_out.at[pl.ds(pl.multiple_of(second * size, size), size), :]
            s = jnp.where(second == 0, slots[:, :size], slots[:, size:])
            k = jnp.where(second == 0, kinds[:, :size], kinds[:, size:])
        to_tiles(x, out)
        line = lax.broadcasted_iota(I32, (16, size), 0)
        index = jnp.where(line == 0, s // 256, jnp.where(line == 1, s % 256, k))
        index = jnp.where(line < 3, index, 0).astype(F32)
        if size < 128:
            index = jnp.concatenate([index, jnp.zeros((16, 128 - size), F32)], axis=1)
        out[size * width // 128 :, :] = index.astype(BF16)


def to_send(cuts, rows, slot, kind):
    half, width = rows.shape[0] // 2, rows.shape[1]
    sizes = [half if parity is None else half // 2 for parity in cuts]
    shapes = [(size * width // 128 + 16, 128) for size in sizes]
    dealt = len(cuts) > 1
    out_shape = [jax.ShapeDtypeStruct(shape, BF16) for shape in shapes]
    scratch = [pltpu.VMEM((half, width), BF16)]
    if dealt:
        out_shape.append(jax.ShapeDtypeStruct(slot.shape, I32))
        scratch.append(pltpu.VMEM(rows.shape, BF16))
    return pl.pallas_call(
        functools.partial(send_kernel, cuts),
        out_shape=out_shape,
        in_specs=[HBM] * 3,
        out_specs=[VMEM] * len(out_shape),
        scratch_shapes=scratch
        + [
            pltpu.VMEM(slot.shape, I32),
            pltpu.VMEM(slot.shape, I32),
            pltpu.SemaphoreType.DMA((3,)),
        ],
        compiler_params=pltpu.CompilerParams(vmem_limit_bytes=60 << 20),
        cost_estimate=cost(0, 4 * half * width),
        name="to_send",
    )(rows, slot, kind)


def column_of(row_vector):
    r = row_vector.shape[1]
    diagonal = lax.broadcasted_iota(I32, (r, r), 0) == lax.broadcasted_iota(I32, (r, r), 1)
    return jnp.sum(jnp.where(diagonal, row_vector, 0), axis=1, keepdims=True)


def project(kind_row, x, w_audio, w_frame, b_audio, b_frame, out):
    is_audio = column_of(kind_row) == 0
    audio = jnp.dot(x, w_audio[...], preferred_element_type=F32)
    frame = jnp.dot(x, w_frame[...], preferred_element_type=F32)
    audio = audio + b_audio[...].astype(F32)
    frame = frame + b_frame[...].astype(F32)
    out[...] = jnp.where(is_audio, audio, frame).astype(out.dtype)


def project_own_kernel(kind, x, wa, wf, ba, bf, out):
    project(kind[...], x[...], wa, wf, ba, bf, out)


def project_own(kind, rows, weights):
    ew, cols = weights[0].shape
    return pl.pallas_call(
        project_own_kernel,
        out_shape=jax.ShapeDtypeStruct((rows.shape[0], cols), BF16),
        in_specs=[VMEM] * 6,
        out_specs=VMEM,
        compiler_params=PARAMS,
        cost_estimate=cost(4 * rows.shape[0] * ew * cols, 4 * ew * cols),
        name="project_own",
    )(kind, rows, *weights)


def project_parts_kernel(wa, wf, ba, bf, *refs):
    parts, out, slots = refs[:-2], refs[-2], refs[-1]
    width = wa.shape[0]
    x, index = [], []
    for ref in parts:
        for k in range(ref.shape[0]):
            lines = ref.shape[1] - 16
            size = lines * 128 // width
            x.append(from_tiles(ref[k, :lines, :], width))
            index.append(ref[k, lines:, :].astype(F32).astype(I32)[:, :size])
    x = x[0] if len(x) == 1 else jnp.concatenate(x, axis=0)
    index = index[0] if len(index) == 1 else jnp.concatenate(index, axis=1)
    slots[...] = index[0:1] * 256 + index[1:2]
    project(index[2:3], x, wa, wf, ba, bf, out)


def project_parts(parts, weights):
    ew, cols = weights[0].shape
    rows = sum(p.shape[0] * (p.shape[1] - 16) * 128 // ew for p in parts)
    return pl.pallas_call(
        project_parts_kernel,
        out_shape=[jax.ShapeDtypeStruct((rows, cols), BF16), jax.ShapeDtypeStruct((1, rows), I32)],
        in_specs=[VMEM] * (4 + len(parts)),
        out_specs=[VMEM] * 2,
        compiler_params=PARAMS,
        cost_estimate=cost(4 * rows * ew * cols, 4 * ew * cols),
        name="project_parts",
    )(*weights, *parts)


def select_kernel(m, count, *refs):
    blocks, slots, outs = refs[:count], refs[count : 2 * count], refs[2 * count :]
    places = sum(out.shape[0] for out in outs) // 2
    z, t = lax.axis_index("ctx"), lax.axis_index("tp")
    first = jnp.bitwise_xor(z, m) * 2 * places
    i = lax.broadcasted_iota(I32, (2 * places, 1), 0)
    position = first + jnp.bitwise_xor(i, t * places)
    total = None
    for block, slot in zip(blocks, slots):
        chosen = (slot[...] == position).astype(F32).astype(BF16)
        part = jnp.dot(chosen, block[...], preferred_element_type=F32)
        total = part if total is None else total + part
    at = 0
    for out in outs:
        out[...] = total[at : at + out.shape[0]].astype(BF16)
        at += out.shape[0]


def select(m, blocks, slots, sizes):
    rows, cols = sum(b.shape[0] for b in blocks), blocks[0].shape[1]
    return pl.pallas_call(
        functools.partial(select_kernel, m, len(blocks)),
        out_shape=[jax.ShapeDtypeStruct((size, cols), BF16) for size in sizes],
        in_specs=[VMEM] * (2 * len(blocks)),
        out_specs=[VMEM] * len(sizes),
        compiler_params=PARAMS,
        cost_estimate=cost(2 * sum(sizes) * rows * cols, 2 * rows * cols),
        name="select",
    )(*blocks, *slots)


def upto(places, width):
    i = lax.broadcasted_iota(I32, (width, width), 0)
    j = lax.broadcasted_iota(I32, (width, width), 1)
    counts = i <= j
    if width > places:
        counts = jnp.logical_and(counts, (i < places) == (j < places))
    return counts.astype(F32).astype(BF16)


def one_hot(found):
    return found.astype(F32).astype(BF16)


def over_rows(a, b):
    return lax.dot_general(a, b, (((1,), (1,)), ((), ())), preferred_element_type=F32)


def running(flags, counts):
    return jnp.dot(one_hot(flags), counts, preferred_element_type=F32)


def packet_kernel(m, early, count, second, *refs):
    blocks, slots, outs = refs[:count], refs[count : 2 * count], refs[2 * count :]
    size = sum(out.shape[0] for out in outs) // 2
    places = blocks[0].shape[0] // 2
    first_size = places - size if second else size
    z, t = lax.axis_index("ctx"), lax.axis_index("tp")
    i = lax.broadcasted_iota(I32, (2 * places, 1), 0)
    position = jnp.bitwise_xor(z, m) * 2 * places + jnp.bitwise_xor(i, t * places)
    holds = [one_hot(slot[...] == position) for slot in slots]
    known = None
    for k in range(early):
        part = over_rows(jnp.ones((8, holds[k].shape[1]), BF16), holds[k])
        known = part if known is None else known + part
    counts = upto(places, 2 * places)
    wanted = known > 0.5
    number = running(wanted, counts)
    if second:
        wanted = jnp.logical_not(jnp.logical_and(wanted, number < first_size + 0.5))
        number = running(wanted, counts)
    number = jnp.where(wanted, number, 0.0)[0:1].astype(I32)
    e = lax.broadcasted_iota(I32, (2 * size, 1), 0)
    upper = (e >= size).astype(I32)
    lane_upper = (lax.broadcasted_iota(I32, (1, 2 * places), 1) >= places).astype(I32)
    pick = jnp.logical_and(number == e - upper * size + 1, lane_upper == upper)
    pick = one_hot(pick)
    total = None
    for block, hold in zip(blocks, holds):
        chosen = jnp.dot(pick, hold, preferred_element_type=F32).astype(BF16)
        part = jnp.dot(chosen, block[...], preferred_element_type=F32)
        total = part if total is None else total + part
    if second:
        outs[0][...] = total[:size].astype(BF16)
        outs[1][...] = total[size:].astype(BF16)
    else:
        outs[0][...] = total.astype(BF16)


def packet(m, early, blocks, slots, size, second):
    rows, cols = sum(b.shape[0] for b in blocks), blocks[0].shape[1]
    return pl.pallas_call(
        functools.partial(packet_kernel, m, early, len(blocks), second),
        out_shape=[jax.ShapeDtypeStruct((size if second else 2 * size, cols), BF16)] * (1 + second),
        in_specs=[VMEM] * (2 * len(blocks)),
        out_specs=[VMEM] * (1 + second),
        compiler_params=PARAMS,
        cost_estimate=cost(4 * size * rows * cols, 2 * rows * cols),
        name="packet",
    )(*blocks, *slots)


def order_kernel(first_size, parity, *refs):
    slots, outs = refs[:-2], refs[-2:]
    places = outs[0].shape[0]
    z, t = lax.axis_index("ctx"), lax.axis_index("tp")
    pair, odd = z // 2, lax.rem(z, 2)
    position = (2 * z + t) * places + lax.broadcasted_iota(I32, (places, 1), 0)
    source = lax.broadcasted_iota(I32, (8, 1), 0)
    known = None
    for k, slot in enumerate(slots):
        width = slot.shape[1]
        lane = lax.broadcasted_iota(I32, (1, width), 1)
        if k == 0:
            near, odd_rank = lane >= 0, parity[...]
        elif k in (1, 2):
            near = lane < places
            odd_rank = jnp.where(near, (lane >= places // 2).astype(I32), odd)
        else:
            near, odd_rank = lane < 0, jnp.zeros((1, width), I32) + 1 - odd
        owner_pair = jnp.where(near, pair, 1 - pair)
        held = jnp.logical_or(owner_pair == source // 2, odd_rank == lax.rem(source, 2))
        part = over_rows(one_hot(held), one_hot(slot[...] == position))
        known = part if known is None else known + part
    counts = upto(places, places)
    early = known > 0.5
    number = running(early, counts)
    early = jnp.logical_and(early, number < first_size + 0.5)
    later = running(jnp.logical_not(early), counts)
    place = jnp.where(early, number, later + first_size) - 1.0
    for m, out in zip((3, 2), outs):
        row = jnp.sum(jnp.where(source == jnp.bitwise_xor(z, m), place, 0.0), axis=0, keepdims=True)
        column = column_of(row.astype(I32))
        out[...] = one_hot(column == lax.broadcasted_iota(I32, (1, places), 1))


def order_of(first_size, parity, slots, places):
    return pl.pallas_call(
        functools.partial(order_kernel, first_size),
        out_shape=[jax.ShapeDtypeStruct((places, places), BF16)] * 2,
        in_specs=[VMEM] * (1 + len(slots)),
        out_specs=[VMEM] * 2,
        compiler_params=PARAMS,
        cost_estimate=cost(1 << 34, 0),
        name="order_of",
    )(parity, *slots)


def view(ref, places):
    if len(ref.shape) == 3:
        return ref.at[1 - lax.axis_index("tp")]
    return ref.at[pl.ds(0, places), :]


def square_sum(piece):
    wide = piece[...].astype(F32)
    return jnp.sum(wide * wide, axis=1, keepdims=True)


def squares_kernel(*refs):
    out = refs[-1]
    total = None
    for ref in refs[:-1]:
        part = ref[...] if ref.dtype == F32 else square_sum(view(ref, out.shape[0]))
        total = part if total is None else total + part
    out[...] = total


def squares(total, pieces, places, flops=0):
    operands = pieces if total is None else [total] + pieces
    return pl.pallas_call(
        squares_kernel,
        out_shape=jax.ShapeDtypeStruct((places, 1), F32),
        in_specs=[VMEM] * len(operands),
        out_specs=VMEM,
        compiler_params=PARAMS,
        cost_estimate=cost(flops, 0),
        name="squares",
    )(*operands)


def norm_kernel(places_of, fresh, gain, before, *refs):
    n = len(places_of)
    out, scaled, sems = refs[n], refs[n + 1], refs[n + 2]
    places, cols = scaled.shape[1:]
    pieces = [view(ref, places) for ref in refs[:n]]
    z, t = lax.axis_index("ctx"), lax.axis_index("tp")
    total = before[...]
    for k in fresh:
        total = total + square_sum(pieces[k])
    scale = lax.rsqrt(total / (n * cols) + 1e-06)
    copies = []
    for k, ((m, d), piece) in enumerate(zip(places_of, pieces)):
        block = jnp.bitwise_xor(z, m) * 2 + jnp.bitwise_xor(t, d)
        at = pl.ds(pl.multiple_of(block * cols, cols), cols)
        scaled[k] = (piece[...].astype(F32) * scale * gain[:, at].astype(F32)).astype(BF16)
        copies.append(pltpu.make_async_copy(scaled.at[k], out.at[:, at], sems.at[k]))
        copies[k].start()
    for copy in copies:
        copy.wait()


def norm(places_of, fresh, gain, before, pieces):
    n, places, cols = len(pieces), before.shape[0], pieces[0].shape[-1]
    return pl.pallas_call(
        functools.partial(norm_kernel, places_of, fresh),
        out_shape=jax.ShapeDtypeStruct((places, n * cols), BF16),
        in_specs=[VMEM] * (n + 2),
        out_specs=HBM,
        scratch_shapes=[pltpu.VMEM((n, places, cols), BF16), pltpu.SemaphoreType.DMA((n,))],
        compiler_params=PARAMS,
        cost_estimate=cost(4 * places * n * cols, 4 * places * n * cols),
        name="norm",
    )(gain, before, *pieces)


def last_kernel(far, whole, gain, before, before_too, *refs):
    orders, packets, pieces = refs[:2], refs[2:10], refs[10:14]
    out, scaled, sems = refs[14:]
    places, cols = scaled.shape[1:]
    z, t = lax.axis_index("ctx"), lax.axis_index("tp")
    total = before[...] + before_too[...]
    for k in range(4):
        later = packets[2 * k + 1][...]
        early = view(packets[2 * k], places - later.shape[0])[...]
        both = jnp.concatenate([early, later], axis=0)
        wide = jnp.dot(orders[k // 2][...], both, preferred_element_type=F32)
        scaled[k] = wide.astype(BF16)
        total = total + jnp.sum(wide * wide, axis=1, keepdims=True)
    scale = lax.rsqrt(total / (8 * cols) + 1e-06)
    copies = []
    for k, (m, d) in enumerate(far + whole):
        block = jnp.bitwise_xor(z, m) * 2 + jnp.bitwise_xor(t, d)
        at = pl.ds(pl.multiple_of(block * cols, cols), cols)
        piece = scaled[k] if k < 4 else view(pieces[k - 4], places)[...]
        scaled[k] = (piece.astype(F32) * scale * gain[:, at].astype(F32)).astype(BF16)
        copies.append(pltpu.make_async_copy(scaled.at[k], out.at[:, at], sems.at[k]))
        copies[k].start()
    for copy in copies:
        copy.wait()


def place_and_norm(far, whole, gain, before, orders, packets, pieces):
    places, cols = before[0].shape[0], packets[0].shape[1]
    operands = [gain, *before, *orders, *packets, *pieces]
    return pl.pallas_call(
        functools.partial(last_kernel, far, whole),
        out_shape=jax.ShapeDtypeStruct((places, 8 * cols), BF16),
        in_specs=[VMEM] * len(operands),
        out_specs=HBM,
        scratch_shapes=[pltpu.VMEM((8, places, cols), BF16), pltpu.SemaphoreType.DMA((8,))],
        compiler_params=PARAMS,
        cost_estimate=cost(32 * places * cols, 32 * places * cols),
        name="place_and_norm",
    )(*operands)


def after(x, *others):
    return lax.optimization_barrier((x, *others))[0]


def body(enc_rows, row_slot, row_kind, audio_proj, frame_proj, audio_bias, frame_bias, norm_gain):
    n = lax.axis_size("ctx")
    rows = enc_rows[0]
    half = rows.shape[0] // 2
    weights = (audio_proj, frame_proj, audio_bias[None, :], frame_bias[None, :])

    def over_ctx(x, m):
        return lax.ppermute(x, "ctx", [(i, i ^ m) for i in range(n)])

    def over_tp(x):
        return lax.ppermute(x, "tp", [(0, 1), (1, 0)])

    own = project_own(row_kind, rows, weights)
    blocks, slots = [own], [row_slot]

    def take(group):
        block, slot = project_parts(group, weights)
        blocks.append(block)
        slots.append(slot)

    def to_core(x, m, d):
        pairs = [(i * 2 + c, (i ^ m) * 2 + (c ^ d)) for i in range(n) for c in range(2)]
        return lax.ppermute(x, ("ctx", "tp"), pairs)

    def own_piece():
        pieces[0, 0], other = select(0, blocks, slots, [half, half])
        pieces[0, 1] = lax.all_gather(other, "tp", axis=0)
        return squares(None, [pieces[0, 0], pieces[0, 1]], half, OWN_FLOPS)

    def near_piece(total):
        pair = pieces[1]
        pieces[1, 0], pieces[1, 1] = pair, lax.all_gather(pair[half:], "tp", axis=0)
        return squares(total, [pieces[1, 0], pieces[1, 1]], half, NEAR_FLOPS)

    pieces = {}
    if n == 4:
        near, second, third, parity = to_send((None, 0, 1), rows, row_slot, row_kind)
        near, second, third = over_ctx(near, 1), over_ctx(second, 2), over_ctx(third, 3)
        first = lax.optimization_barrier((near, second, third, own))[:3]
        shared = [over_ctx(part, 1) for part in first[1:]]
        other = [over_tp(part)[None] for part in first]
        take([part[None] for part in first])
        other = lax.optimization_barrier((*other, blocks[-1]))[:3]
        take(other)

        early, size = len(blocks), 3 * half // 8
        sent = {}
        for m in (3, 2):
            chosen = packet(m, early, blocks, slots, size, False)
            slots[0] = after(slots[0], chosen[0])
            sent[m] = over_ctx(chosen[0], m)
        shared = lax.optimization_barrier((*shared, blocks[-1]))[:2]
        take([lax.all_gather(part, "tp", axis=0) for part in shared])

        (chosen,) = select(1, blocks, slots, [2 * half])
        slots[0] = after(slots[0], chosen)
        pieces[1] = over_ctx(chosen, 1)
        rest = {}
        for m in (3, 2):
            chosen = packet(m, early, blocks, slots, half - size, True)
            slots[0] = after(slots[0], chosen[0])
            if m == 3:
                joined = lax.optimization_barrier((*chosen, sent[3], sent[2]))
                chosen, sent[3], sent[2] = joined[:2], joined[2], joined[3]
            rest[m] = [to_core(piece, m, d) for d, piece in enumerate(chosen)]

        orders = order_of(size, parity, slots, half)
        total = [own_piece(), near_piece(None)]
        for m in (3, 2):
            whole_packet = sent[m]
            sent[m] = [whole_packet, lax.all_gather(whole_packet[size:], "tp", axis=0)]
        far, whole = ((3, 0), (3, 1), (2, 0), (2, 1)), ((1, 0), (1, 1), (0, 0), (0, 1))
        packets = [part for m, d in far for part in (sent[m][d], rest[m][d])]
        whole_pieces = [pieces[at] for at in whole]
        gain = norm_gain[None, :]
        return place_and_norm(far, whole, gain, total, orders, packets, whole_pieces)[None]
    else:
        (mine,) = to_send((None,), rows, row_slot, row_kind)
        arrived = [over_ctx(mine, m) for m in range(1, n)]
        for direct in arrived[:-1]:
            direct = after(direct, blocks[-1])
            take([lax.all_gather(direct, "tp", axis=0)])
        direct = after(arrived[-1], blocks[-1])
        swapped = over_tp(direct)
        take([direct[None]])
        take([swapped[None]])

        order = [n - 1, 1] + list(reversed(range(2, n - 1)))
        for m in order:
            chosen = select(m, blocks, slots, [2 * half] if m == 1 else [half, half])
            slots[0] = after(slots[0], chosen[0])
            if m == 1:
                pieces[m] = over_ctx(chosen[0], m)
                continue
            for d, piece in enumerate(chosen):
                pieces[m, d] = to_core(piece, m, d)
        total = squares(None, [pieces[n - 1, 0], pieces[n - 1, 1]], half)
        total = squares(near_piece(total), [own_piece()], half)
        for m in order[2:-1]:
            late = [after(pieces[m, d], total) for d in range(2)]
            total = squares(total, late, half)
        fresh = (2 * (n - 1), 2 * (n - 1) + 1)
        for d in range(2):
            pieces[order[-1], d] = after(pieces[order[-1], d], total)
        order = order[:-1] + [0, order[-1]]

    places_of = tuple((m, d) for m in order for d in range(2))
    return norm(places_of, fresh, norm_gain[None, :], total, [pieces[at] for at in places_of])[None]


def solution(mesh):
    return jax.shard_map(
        body,
        mesh=mesh,
        in_specs=(
            P(("groups", "enc"), "ctx", None),
            P(("groups", "enc"), "ctx"),
            P(("groups", "enc"), "ctx"),
            P(None, ("ctx", "tp")),
            P(None, ("ctx", "tp")),
            P(("ctx", "tp")),
            P(("ctx", "tp")),
            P(),
        ),
        out_specs=P(("groups", "enc"), ("ctx", "tp"), None),
        check_vma=False,
    )
```

```python
import functools

import jax
import jax.numpy as jnp
from jax import lax
from jax.experimental import pallas as pl
from jax.experimental.pallas import tpu as pltpu
from jax.sharding import PartitionSpec as P

VMEM = pl.BlockSpec(memory_space=pltpu.VMEM)
HBM = pl.BlockSpec(memory_space=pltpu.HBM)
PARAMS = pltpu.CompilerParams(vmem_limit_bytes=12 << 20)
OWN_FLOPS, NEAR_FLOPS = 1 << 35, 0
BF16, F32, I32 = jnp.bfloat16, jnp.float32, jnp.int32


def cost(flops, moved):
    return pl.CostEstimate(flops=flops // 16, bytes_accessed=moved // 16, transcendentals=0)


def to_tiles(x, out):
    at = 0
    for r in range(0, x.shape[0], 16):
        for c in range(0, x.shape[1], 128):
            out[at : at + 16, :] = x[r : r + 16, c : c + 128]
            at += 16


def from_tiles(tiles, width):
    per_row = width // 128
    lines = []
    for r in range(0, tiles.shape[0], 16 * per_row):
        line = [tiles[r + 16 * c : r + 16 * (c + 1)] for c in range(per_row)]
        lines.append(jnp.concatenate(line, axis=1))
    return jnp.concatenate(lines, axis=0)


def send_kernel(cuts, rows, slot, kind, *refs):
    outs, (rows_here, slot_here, kind_here, sems) = refs[: len(cuts)], refs[-4:]
    whole, width = rows.shape
    half = whole // 2
    z, t = lax.axis_index("ctx"), lax.axis_index("tp")
    dealt = len(cuts) > 1
    source = rows
    if not dealt:
        source = rows.at[pl.ds(pl.multiple_of(t * half, half), half), :]
    copies = [
        pltpu.make_async_copy(slot, slot_here, sems.at[0]),
        pltpu.make_async_copy(kind, kind_here, sems.at[1]),
        pltpu.make_async_copy(source, rows_here, sems.at[2]),
    ]
    for copy in copies:
        copy.start()
    copies[0].wait()
    copies[1].wait()
    if dealt:
        slot_row, slot_col = slot_here[...], column_of(slot_here[...])
        kind_col = column_of(kind_here[...])
        rank_row = jnp.sum((slot_col < slot_row).astype(I32), axis=0, keepdims=True)
        rank_col = jnp.sum((slot_row < slot_col).astype(I32), axis=1, keepdims=True)
        refs[len(cuts)][...] = lax.rem(rank_row, 2)

        def rank_at(k):
            odd = (k >= half // 2).astype(I32)
            return t * half + 2 * (k - odd * (half // 2)) + odd

        here = rank_col == rank_at(lax.broadcasted_iota(I32, (1, half), 1))
        slots = jnp.sum(jnp.where(here, slot_col, 0), axis=0, keepdims=True)
        kinds = jnp.sum(jnp.where(here, kind_col, 0), axis=0, keepdims=True)
        deal = rank_row == rank_at(lax.broadcasted_iota(I32, (half, 1), 0))
        copies[2].wait()
        rows_out = refs[-5]
        rows_out[...] = jnp.dot(
            deal.astype(F32).astype(BF16), rows_here[...], preferred_element_type=F32
        ).astype(BF16)
    else:
        slots = jnp.where(t == 0, slot_here[:, :half], slot_here[:, half:])
        kinds = jnp.where(t == 0, kind_here[:, :half], kind_here[:, half:])
        copies[2].wait()
        rows_out = rows_here
    for out, parity in zip(outs, cuts):
        x, s, k = rows_out, slots, kinds
        size = half
        if parity is not None:
            size = half // 2
            second = lax.rem(z + parity, 2)
            x = rows_out.at[pl.ds(pl.multiple_of(second * size, size), size), :]
            s = jnp.where(second == 0, slots[:, :size], slots[:, size:])
            k = jnp.where(second == 0, kinds[:, :size], kinds[:, size:])
        to_tiles(x, out)
        line = lax.broadcasted_iota(I32, (16, size), 0)
        index = jnp.where(line == 0, s // 256, jnp.where(line == 1, s % 256, k))
        index = jnp.where(line < 3, index, 0).astype(F32)
        if size < 128:
            index = jnp.concatenate([index, jnp.zeros((16, 128 - size), F32)], axis=1)
        out[size * width // 128 :, :] = index.astype(BF16)


def to_send(cuts, rows, slot, kind):
    half, width = rows.shape[0] // 2, rows.shape[1]
    sizes = [half if parity is None else half // 2 for parity in cuts]
    shapes = [(size * width // 128 + 16, 128) for size in sizes]
    dealt = len(cuts) > 1
    out_shape = [jax.ShapeDtypeStruct(shape, BF16) for shape in shapes]
    scratch = [pltpu.VMEM((half, width), BF16)]
    if dealt:
        out_shape.append(jax.ShapeDtypeStruct(slot.shape, I32))
        scratch.append(pltpu.VMEM(rows.shape, BF16))
    return pl.pallas_call(
        functools.partial(send_kernel, cuts),
        out_shape=out_shape,
        in_specs=[HBM] * 3,
        out_specs=[VMEM] * len(out_shape),
        scratch_shapes=scratch
        + [
            pltpu.VMEM(slot.shape, I32),
            pltpu.VMEM(slot.shape, I32),
            pltpu.SemaphoreType.DMA((3,)),
        ],
        compiler_params=pltpu.CompilerParams(vmem_limit_bytes=60 << 20),
        cost_estimate=cost(0, 4 * half * width),
        name="to_send",
    )(rows, slot, kind)


def column_of(row_vector):
    r = row_vector.shape[1]
    diagonal = lax.broadcasted_iota(I32, (r, r), 0) == lax.broadcasted_iota(I32, (r, r), 1)
    return jnp.sum(jnp.where(diagonal, row_vector, 0), axis=1, keepdims=True)


def project(kind_row, x, w_audio, w_frame, b_audio, b_frame, out):
    is_audio = column_of(kind_row) == 0
    audio = jnp.dot(x, w_audio[...], preferred_element_type=F32)
    frame = jnp.dot(x, w_frame[...], preferred_element_type=F32)
    audio = audio + b_audio[...].astype(F32)
    frame = frame + b_frame[...].astype(F32)
    out[...] = jnp.where(is_audio, audio, frame).astype(out.dtype)


def project_own_kernel(kind, x, wa, wf, ba, bf, out):
    project(kind[...], x[...], wa, wf, ba, bf, out)


def project_own(kind, rows, weights):
    ew, cols = weights[0].shape
    return pl.pallas_call(
        project_own_kernel,
        out_shape=jax.ShapeDtypeStruct((rows.shape[0], cols), BF16),
        in_specs=[VMEM] * 6,
        out_specs=VMEM,
        compiler_params=PARAMS,
        cost_estimate=cost(4 * rows.shape[0] * ew * cols, 4 * ew * cols),
        name="project_own",
    )(kind, rows, *weights)


def project_parts_kernel(wa, wf, ba, bf, *refs):
    parts, out, slots = refs[:-2], refs[-2], refs[-1]
    width = wa.shape[0]
    x, index = [], []
    for ref in parts:
        for k in range(ref.shape[0]):
            lines = ref.shape[1] - 16
            size = lines * 128 // width
            x.append(from_tiles(ref[k, :lines, :], width))
            index.append(ref[k, lines:, :].astype(F32).astype(I32)[:, :size])
    x = x[0] if len(x) == 1 else jnp.concatenate(x, axis=0)
    index = index[0] if len(index) == 1 else jnp.concatenate(index, axis=1)
    slots[...] = index[0:1] * 256 + index[1:2]
    project(index[2:3], x, wa, wf, ba, bf, out)


def project_parts(parts, weights):
    ew, cols = weights[0].shape
    rows = sum(p.shape[0] * (p.shape[1] - 16) * 128 // ew for p in parts)
    return pl.pallas_call(
        project_parts_kernel,
        out_shape=[jax.ShapeDtypeStruct((rows, cols), BF16), jax.ShapeDtypeStruct((1, rows), I32)],
        in_specs=[VMEM] * (4 + len(parts)),
        out_specs=[VMEM] * 2,
        compiler_params=PARAMS,
        cost_estimate=cost(4 * rows * ew * cols, 4 * ew * cols),
        name="project_parts",
    )(*weights, *parts)


def select_kernel(m, count, *refs):
    blocks, slots, outs = refs[:count], refs[count : 2 * count], refs[2 * count :]
    places = sum(out.shape[0] for out in outs) // 2
    z, t = lax.axis_index("ctx"), lax.axis_index("tp")
    first = jnp.bitwise_xor(z, m) * 2 * places
    i = lax.broadcasted_iota(I32, (2 * places, 1), 0)
    position = first + jnp.bitwise_xor(i, t * places)
    total = None
    for block, slot in zip(blocks, slots):
        chosen = (slot[...] == position).astype(F32).astype(BF16)
        part = jnp.dot(chosen, block[...], preferred_element_type=F32)
        total = part if total is None else total + part
    at = 0
    for out in outs:
        out[...] = total[at : at + out.shape[0]].astype(BF16)
        at += out.shape[0]


def select(m, blocks, slots, sizes):
    rows, cols = sum(b.shape[0] for b in blocks), blocks[0].shape[1]
    return pl.pallas_call(
        functools.partial(select_kernel, m, len(blocks)),
        out_shape=[jax.ShapeDtypeStruct((size, cols), BF16) for size in sizes],
        in_specs=[VMEM] * (2 * len(blocks)),
        out_specs=[VMEM] * len(sizes),
        compiler_params=PARAMS,
        cost_estimate=cost(2 * sum(sizes) * rows * cols, 2 * rows * cols),
        name="select",
    )(*blocks, *slots)


def upto(places, width):
    i = lax.broadcasted_iota(I32, (width, width), 0)
    j = lax.broadcasted_iota(I32, (width, width), 1)
    counts = i <= j
    if width > places:
        counts = jnp.logical_and(counts, (i < places) == (j < places))
    return counts.astype(F32).astype(BF16)


def one_hot(found):
    return found.astype(F32).astype(BF16)


def over_rows(a, b):
    return lax.dot_general(a, b, (((1,), (1,)), ((), ())), preferred_element_type=F32)


def running(flags, counts):
    return jnp.dot(one_hot(flags), counts, preferred_element_type=F32)


def packet_kernel(m, early, count, second, *refs):
    blocks, slots, outs = refs[:count], refs[count : 2 * count], refs[2 * count :]
    size = sum(out.shape[0] for out in outs) // 2
    places = blocks[0].shape[0] // 2
    first_size = places - size if second else size
    z, t = lax.axis_index("ctx"), lax.axis_index("tp")
    i = lax.broadcasted_iota(I32, (2 * places, 1), 0)
    position = jnp.bitwise_xor(z, m) * 2 * places + jnp.bitwise_xor(i, t * places)
    holds = [one_hot(slot[...] == position) for slot in slots]
    known = None
    for k in range(early):
        part = over_rows(jnp.ones((8, holds[k].shape[1]), BF16), holds[k])
        known = part if known is None else known + part
    counts = upto(places, 2 * places)
    wanted = known > 0.5
    number = running(wanted, counts)
    if second:
        wanted = jnp.logical_not(jnp.logical_and(wanted, number < first_size + 0.5))
        number = running(wanted, counts)
    number = jnp.where(wanted, number, 0.0)[0:1].astype(I32)
    e = lax.broadcasted_iota(I32, (2 * size, 1), 0)
    upper = (e >= size).astype(I32)
    lane_upper = (lax.broadcasted_iota(I32, (1, 2 * places), 1) >= places).astype(I32)
    pick = jnp.logical_and(number == e - upper * size + 1, lane_upper == upper)
    pick = one_hot(pick)
    total = None
    for block, hold in zip(blocks, holds):
        chosen = jnp.dot(pick, hold, preferred_element_type=F32).astype(BF16)
        part = jnp.dot(chosen, block[...], preferred_element_type=F32)
        total = part if total is None else total + part
    if second:
        outs[0][...] = total[:size].astype(BF16)
        outs[1][...] = total[size:].astype(BF16)
    else:
        outs[0][...] = total.astype(BF16)


def packet(m, early, blocks, slots, size, second):
    rows, cols = sum(b.shape[0] for b in blocks), blocks[0].shape[1]
    return pl.pallas_call(
        functools.partial(packet_kernel, m, early, len(blocks), second),
        out_shape=[jax.ShapeDtypeStruct((size if second else 2 * size, cols), BF16)] * (1 + second),
        in_specs=[VMEM] * (2 * len(blocks)),
        out_specs=[VMEM] * (1 + second),
        compiler_params=PARAMS,
        cost_estimate=cost(4 * size * rows * cols, 2 * rows * cols),
        name="packet",
    )(*blocks, *slots)


def order_kernel(first_size, parity, *refs):
    slots, outs = refs[:-2], refs[-2:]
    places = outs[0].shape[0]
    z, t = lax.axis_index("ctx"), lax.axis_index("tp")
    pair, odd = z // 2, lax.rem(z, 2)
    position = (2 * z + t) * places + lax.broadcasted_iota(I32, (places, 1), 0)
    source = lax.broadcasted_iota(I32, (8, 1), 0)
    known = None
    for k, slot in enumerate(slots):
        width = slot.shape[1]
        lane = lax.broadcasted_iota(I32, (1, width), 1)
        if k == 0:
            near, odd_rank = lane >= 0, parity[...]
        elif k in (1, 2):
            near = lane < places
            odd_rank = jnp.where(near, (lane >= places // 2).astype(I32), odd)
        else:
            near, odd_rank = lane < 0, jnp.zeros((1, width), I32) + 1 - odd
        owner_pair = jnp.where(near, pair, 1 - pair)
        held = jnp.logical_or(owner_pair == source // 2, odd_rank == lax.rem(source, 2))
        part = over_rows(one_hot(held), one_hot(slot[...] == position))
        known = part if known is None else known + part
    counts = upto(places, places)
    early = known > 0.5
    number = running(early, counts)
    early = jnp.logical_and(early, number < first_size + 0.5)
    later = running(jnp.logical_not(early), counts)
    place = jnp.where(early, number, later + first_size) - 1.0
    for m, out in zip((3, 2), outs):
        row = jnp.sum(jnp.where(source == jnp.bitwise_xor(z, m), place, 0.0), axis=0, keepdims=True)
        column = column_of(row.astype(I32))
        out[...] = one_hot(column == lax.broadcasted_iota(I32, (1, places), 1))


def order_of(first_size, parity, slots, places):
    return pl.pallas_call(
        functools.partial(order_kernel, first_size),
        out_shape=[jax.ShapeDtypeStruct((places, places), BF16)] * 2,
        in_specs=[VMEM] * (1 + len(slots)),
        out_specs=[VMEM] * 2,
        compiler_params=PARAMS,
        cost_estimate=cost(1 << 34, 0),
        name="order_of",
    )(parity, *slots)


def view(ref, places):
    if len(ref.shape) == 3:
        return ref.at[1 - lax.axis_index("tp")]
    return ref.at[pl.ds(0, places), :]


def square_sum(piece):
    wide = piece[...].astype(F32)
    return jnp.sum(wide * wide, axis=1, keepdims=True)


def squares_kernel(*refs):
    out = refs[-1]
    total = None
    for ref in refs[:-1]:
        part = ref[...] if ref.dtype == F32 else square_sum(view(ref, out.shape[0]))
        total = part if total is None else total + part
    out[...] = total


def squares(total, pieces, places, flops=0):
    operands = pieces if total is None else [total] + pieces
    return pl.pallas_call(
        squares_kernel,
        out_shape=jax.ShapeDtypeStruct((places, 1), F32),
        in_specs=[VMEM] * len(operands),
        out_specs=VMEM,
        compiler_params=PARAMS,
        cost_estimate=cost(flops, 0),
        name="squares",
    )(*operands)


def norm_kernel(places_of, fresh, gain, before, *refs):
    n = len(places_of)
    out, scaled, sems = refs[n], refs[n + 1], refs[n + 2]
    places, cols = scaled.shape[1:]
    pieces = [view(ref, places) for ref in refs[:n]]
    z, t = lax.axis_index("ctx"), lax.axis_index("tp")
    total = before[...]
    for k in fresh:
        total = total + square_sum(pieces[k])
    scale = lax.rsqrt(total / (n * cols) + 1e-06)
    copies = []
    for k, ((m, d), piece) in enumerate(zip(places_of, pieces)):
        block = jnp.bitwise_xor(z, m) * 2 + jnp.bitwise_xor(t, d)
        at = pl.ds(pl.multiple_of(block * cols, cols), cols)
        scaled[k] = (piece[...].astype(F32) * scale * gain[:, at].astype(F32)).astype(BF16)
        copies.append(pltpu.make_async_copy(scaled.at[k], out.at[:, at], sems.at[k]))
        copies[k].start()
    for copy in copies:
        copy.wait()


def norm(places_of, fresh, gain, before, pieces):
    n, places, cols = len(pieces), before.shape[0], pieces[0].shape[-1]
    return pl.pallas_call(
        functools.partial(norm_kernel, places_of, fresh),
        out_shape=jax.ShapeDtypeStruct((places, n * cols), BF16),
        in_specs=[VMEM] * (n + 2),
        out_specs=HBM,
        scratch_shapes=[pltpu.VMEM((n, places, cols), BF16), pltpu.SemaphoreType.DMA((n,))],
        compiler_params=PARAMS,
        cost_estimate=cost(4 * places * n * cols, 4 * places * n * cols),
        name="norm",
    )(gain, before, *pieces)


def last_kernel(far, whole, gain, before, before_too, *refs):
    orders, packets, pieces = refs[:2], refs[2:10], refs[10:14]
    out, scaled, sems = refs[14:]
    places, cols = scaled.shape[1:]
    z, t = lax.axis_index("ctx"), lax.axis_index("tp")
    total = before[...] + before_too[...]
    for k in range(4):
        later = packets[2 * k + 1][...]
        early = view(packets[2 * k], places - later.shape[0])[...]
        both = jnp.concatenate([early, later], axis=0)
        wide = jnp.dot(orders[k // 2][...], both, preferred_element_type=F32)
        scaled[k] = wide.astype(BF16)
        total = total + jnp.sum(wide * wide, axis=1, keepdims=True)
    scale = lax.rsqrt(total / (8 * cols) + 1e-06)
    copies = []
    for k, (m, d) in enumerate(far + whole):
        block = jnp.bitwise_xor(z, m) * 2 + jnp.bitwise_xor(t, d)
        at = pl.ds(pl.multiple_of(block * cols, cols), cols)
        piece = scaled[k] if k < 4 else view(pieces[k - 4], places)[...]
        scaled[k] = (piece.astype(F32) * scale * gain[:, at].astype(F32)).astype(BF16)
        copies.append(pltpu.make_async_copy(scaled.at[k], out.at[:, at], sems.at[k]))
        copies[k].start()
    for copy in copies:
        copy.wait()


def place_and_norm(far, whole, gain, before, orders, packets, pieces):
    places, cols = before[0].shape[0], packets[0].shape[1]
    operands = [gain, *before, *orders, *packets, *pieces]
    return pl.pallas_call(
        functools.partial(last_kernel, far, whole),
        out_shape=jax.ShapeDtypeStruct((places, 8 * cols), BF16),
        in_specs=[VMEM] * len(operands),
        out_specs=HBM,
        scratch_shapes=[pltpu.VMEM((8, places, cols), BF16), pltpu.SemaphoreType.DMA((8,))],
        compiler_params=PARAMS,
        cost_estimate=cost(32 * places * cols, 32 * places * cols),
        name="place_and_norm",
    )(*operands)


def after(x, *others):
    return lax.optimization_barrier((x, *others))[0]


def body(enc_rows, row_slot, row_kind, audio_proj, frame_proj, audio_bias, frame_bias, norm_gain):
    n = lax.axis_size("ctx")
    rows = enc_rows[0]
    half = rows.shape[0] // 2
    weights = (audio_proj, frame_proj, audio_bias[None, :], frame_bias[None, :])

    def over_ctx(x, m):
        return lax.ppermute(x, "ctx", [(i, i ^ m) for i in range(n)])

    def over_tp(x):
        return lax.ppermute(x, "tp", [(0, 1), (1, 0)])

    own = project_own(row_kind, rows, weights)
    blocks, slots = [own], [row_slot]

    def take(group):
        block, slot = project_parts(group, weights)
        blocks.append(block)
        slots.append(slot)

    def to_core(x, m, d):
        pairs = [(i * 2 + c, (i ^ m) * 2 + (c ^ d)) for i in range(n) for c in range(2)]
        return lax.ppermute(x, ("ctx", "tp"), pairs)

    def own_piece():
        pieces[0, 0], other = select(0, blocks, slots, [half, half])
        pieces[0, 1] = lax.all_gather(other, "tp", axis=0)
        return squares(None, [pieces[0, 0], pieces[0, 1]], half, OWN_FLOPS)

    def near_piece(total):
        pair = pieces[1]
        pieces[1, 0], pieces[1, 1] = pair, lax.all_gather(pair[half:], "tp", axis=0)
        return squares(total, [pieces[1, 0], pieces[1, 1]], half, NEAR_FLOPS)

    pieces = {}
    if n == 4:
        near, second, third, parity = to_send((None, 0, 1), rows, row_slot, row_kind)
        near, second, third = over_ctx(near, 1), over_ctx(second, 2), over_ctx(third, 3)
        first = lax.optimization_barrier((near, second, third, own))[:3]
        shared = [over_ctx(part, 1) for part in first[1:]]
        other = [over_tp(part)[None] for part in first]
        take([part[None] for part in first])
        other = lax.optimization_barrier((*other, blocks[-1]))[:3]
        take(other)

        early, size = len(blocks), 3 * half // 8
        sent = {}
        for m in (3, 2):
            chosen = packet(m, early, blocks, slots, size, False)
            slots[0] = after(slots[0], chosen[0])
            sent[m] = over_ctx(chosen[0], m)
        shared = lax.optimization_barrier((*shared, blocks[-1]))[:2]
        take([lax.all_gather(part, "tp", axis=0) for part in shared])

        (chosen,) = select(1, blocks, slots, [2 * half])
        slots[0] = after(slots[0], chosen)
        pieces[1] = over_ctx(chosen, 1)
        rest = {}
        for m in (2, 3):
            chosen = packet(m, early, blocks, slots, half - size, True)
            slots[0] = after(slots[0], chosen[0])
            waited = 3 if m == 2 else 2
            joined = lax.optimization_barrier((*chosen, sent[waited]))
            chosen, sent[waited] = joined[:2], joined[2]
            rest[m] = [to_core(piece, m, d) for d, piece in enumerate(chosen)]

        orders = order_of(size, parity, slots, half)
        slots[0] = after(slots[0], rest[2][0])
        total = [own_piece(), near_piece(None)]
        for m in (3, 2):
            whole_packet = sent[m]
            sent[m] = [whole_packet, lax.all_gather(whole_packet[size:], "tp", axis=0)]
        far, whole = ((3, 0), (3, 1), (2, 0), (2, 1)), ((1, 0), (1, 1), (0, 0), (0, 1))
        packets = [part for m, d in far for part in (sent[m][d], rest[m][d])]
        whole_pieces = [pieces[at] for at in whole]
        gain = norm_gain[None, :]
        return place_and_norm(far, whole, gain, total, orders, packets, whole_pieces)[None]
    else:
        (mine,) = to_send((None,), rows, row_slot, row_kind)
        arrived = [over_ctx(mine, m) for m in range(1, n)]
        for direct in arrived[:-1]:
            direct = after(direct, blocks[-1])
            take([lax.all_gather(direct, "tp", axis=0)])
        direct = after(arrived[-1], blocks[-1])
        swapped = over_tp(direct)
        take([direct[None]])
        take([swapped[None]])

        order = [n - 1, 1] + list(reversed(range(2, n - 1)))
        for m in order:
            chosen = select(m, blocks, slots, [2 * half] if m == 1 else [half, half])
            slots[0] = after(slots[0], chosen[0])
            if m == 1:
                pieces[m] = over_ctx(chosen[0], m)
                continue
            for d, piece in enumerate(chosen):
                pieces[m, d] = to_core(piece, m, d)
        total = squares(None, [pieces[n - 1, 0], pieces[n - 1, 1]], half)
        total = squares(near_piece(total), [own_piece()], half)
        for m in order[2:-1]:
            late = [after(pieces[m, d], total) for d in range(2)]
            total = squares(total, late, half)
        fresh = (2 * (n - 1), 2 * (n - 1) + 1)
        for d in range(2):
            pieces[order[-1], d] = after(pieces[order[-1], d], total)
        order = order[:-1] + [0, order[-1]]

    places_of = tuple((m, d) for m in order for d in range(2))
    return norm(places_of, fresh, norm_gain[None, :], total, [pieces[at] for at in places_of])[None]


def solution(mesh):
    return jax.shard_map(
        body,
        mesh=mesh,
        in_specs=(
            P(("groups", "enc"), "ctx", None),
            P(("groups", "enc"), "ctx"),
            P(("groups", "enc"), "ctx"),
            P(None, ("ctx", "tp")),
            P(None, ("ctx", "tp")),
            P(("ctx", "tp")),
            P(("ctx", "tp")),
            P(),
        ),
        out_specs=P(("groups", "enc"), ("ctx", "tp"), None),
        check_vma=False,
    )
```

```python
import functools

import jax
import jax.numpy as jnp
from jax import lax
from jax.experimental import pallas as pl
from jax.experimental.pallas import tpu as pltpu
from jax.sharding import PartitionSpec as P

VMEM = pl.BlockSpec(memory_space=pltpu.VMEM)
HBM = pl.BlockSpec(memory_space=pltpu.HBM)
PARAMS = pltpu.CompilerParams(vmem_limit_bytes=12 << 20)
OWN_FLOPS, NEAR_FLOPS = 1 << 35, 0
BF16, F32, I32 = jnp.bfloat16, jnp.float32, jnp.int32


def cost(flops, moved):
    return pl.CostEstimate(flops=flops // 16, bytes_accessed=moved // 16, transcendentals=0)


def to_tiles(x, out):
    at = 0
    for r in range(0, x.shape[0], 16):
        for c in range(0, x.shape[1], 128):
            out[at : at + 16, :] = x[r : r + 16, c : c + 128]
            at += 16


def from_tiles(tiles, width):
    per_row = width // 128
    lines = []
    for r in range(0, tiles.shape[0], 16 * per_row):
        line = [tiles[r + 16 * c : r + 16 * (c + 1)] for c in range(per_row)]
        lines.append(jnp.concatenate(line, axis=1))
    return jnp.concatenate(lines, axis=0)


def send_kernel(cuts, rows, slot, kind, *refs):
    outs, (rows_here, slot_here, kind_here, sems) = refs[: len(cuts)], refs[-4:]
    whole, width = rows.shape
    half = whole // 2
    z, t = lax.axis_index("ctx"), lax.axis_index("tp")
    dealt = len(cuts) > 1
    source = rows
    if not dealt:
        source = rows.at[pl.ds(pl.multiple_of(t * half, half), half), :]
    copies = [
        pltpu.make_async_copy(slot, slot_here, sems.at[0]),
        pltpu.make_async_copy(kind, kind_here, sems.at[1]),
        pltpu.make_async_copy(source, rows_here, sems.at[2]),
    ]
    for copy in copies:
        copy.start()
    copies[0].wait()
    copies[1].wait()
    if dealt:
        slot_row, slot_col = slot_here[...], column_of(slot_here[...])
        kind_col = column_of(kind_here[...])
        rank_row = jnp.sum((slot_col < slot_row).astype(I32), axis=0, keepdims=True)
        rank_col = jnp.sum((slot_row < slot_col).astype(I32), axis=1, keepdims=True)
        refs[len(cuts)][...] = lax.rem(rank_row, 2)

        def rank_at(k):
            odd = (k >= half // 2).astype(I32)
            return t * half + 2 * (k - odd * (half // 2)) + odd

        here = rank_col == rank_at(lax.broadcasted_iota(I32, (1, half), 1))
        slots = jnp.sum(jnp.where(here, slot_col, 0), axis=0, keepdims=True)
        kinds = jnp.sum(jnp.where(here, kind_col, 0), axis=0, keepdims=True)
        deal = rank_row == rank_at(lax.broadcasted_iota(I32, (half, 1), 0))
        copies[2].wait()
        rows_out = refs[-5]
        rows_out[...] = jnp.dot(
            deal.astype(F32).astype(BF16), rows_here[...], preferred_element_type=F32
        ).astype(BF16)
    else:
        slots = jnp.where(t == 0, slot_here[:, :half], slot_here[:, half:])
        kinds = jnp.where(t == 0, kind_here[:, :half], kind_here[:, half:])
        copies[2].wait()
        rows_out = rows_here
    for out, parity in zip(outs, cuts):
        x, s, k = rows_out, slots, kinds
        size = half
        if parity is not None:
            size = half // 2
            second = lax.rem(z + parity, 2)
            x = rows_out.at[pl.ds(pl.multiple_of(second * size, size), size), :]
            s = jnp.where(second == 0, slots[:, :size], slots[:, size:])
            k = jnp.where(second == 0, kinds[:, :size], kinds[:, size:])
        to_tiles(x, out)
        line = lax.broadcasted_iota(I32, (16, size), 0)
        index = jnp.where(line == 0, s // 256, jnp.where(line == 1, s % 256, k))
        index = jnp.where(line < 3, index, 0).astype(F32)
        if size < 128:
            index = jnp.concatenate([index, jnp.zeros((16, 128 - size), F32)], axis=1)
        out[size * width // 128 :, :] = index.astype(BF16)


def to_send(cuts, rows, slot, kind):
    half, width = rows.shape[0] // 2, rows.shape[1]
    sizes = [half if parity is None else half // 2 for parity in cuts]
    shapes = [(size * width // 128 + 16, 128) for size in sizes]
    dealt = len(cuts) > 1
    out_shape = [jax.ShapeDtypeStruct(shape, BF16) for shape in shapes]
    scratch = [pltpu.VMEM((half, width), BF16)]
    if dealt:
        out_shape.append(jax.ShapeDtypeStruct(slot.shape, I32))
        scratch.append(pltpu.VMEM(rows.shape, BF16))
    return pl.pallas_call(
        functools.partial(send_kernel, cuts),
        out_shape=out_shape,
        in_specs=[HBM] * 3,
        out_specs=[VMEM] * len(out_shape),
        scratch_shapes=scratch
        + [
            pltpu.VMEM(slot.shape, I32),
            pltpu.VMEM(slot.shape, I32),
            pltpu.SemaphoreType.DMA((3,)),
        ],
        compiler_params=pltpu.CompilerParams(vmem_limit_bytes=16 << 20),
        cost_estimate=cost(0, 4 * half * width),
        name="to_send",
    )(*[pltpu.with_memory_space_constraint(x, pltpu.HBM) for x in (rows, slot, kind)])


def column_of(row_vector):
    r = row_vector.shape[1]
    diagonal = lax.broadcasted_iota(I32, (r, r), 0) == lax.broadcasted_iota(I32, (r, r), 1)
    return jnp.sum(jnp.where(diagonal, row_vector, 0), axis=1, keepdims=True)


def project(kind_row, x, w_audio, w_frame, b_audio, b_frame, out):
    is_audio = column_of(kind_row) == 0
    audio = jnp.dot(x, w_audio[...], preferred_element_type=F32)
    frame = jnp.dot(x, w_frame[...], preferred_element_type=F32)
    audio = audio + b_audio[...].astype(F32)
    frame = frame + b_frame[...].astype(F32)
    out[...] = jnp.where(is_audio, audio, frame).astype(out.dtype)


def project_own_kernel(kind, x, wa, wf, ba, bf, out):
    project(kind[...], x[...], wa, wf, ba, bf, out)


def project_own(kind, rows, weights):
    ew, cols = weights[0].shape
    return pl.pallas_call(
        project_own_kernel,
        out_shape=jax.ShapeDtypeStruct((rows.shape[0], cols), BF16),
        in_specs=[VMEM] * 6,
        out_specs=VMEM,
        compiler_params=PARAMS,
        cost_estimate=cost(4 * rows.shape[0] * ew * cols, 4 * ew * cols),
        name="project_own",
    )(kind, rows, *weights)


def project_parts_kernel(wa, wf, ba, bf, *refs):
    parts, out, slots = refs[:-2], refs[-2], refs[-1]
    width = wa.shape[0]
    x, index = [], []
    for ref in parts:
        for k in range(ref.shape[0]):
            lines = ref.shape[1] - 16
            size = lines * 128 // width
            x.append(from_tiles(ref[k, :lines, :], width))
            index.append(ref[k, lines:, :].astype(F32).astype(I32)[:, :size])
    x = x[0] if len(x) == 1 else jnp.concatenate(x, axis=0)
    index = index[0] if len(index) == 1 else jnp.concatenate(index, axis=1)
    slots[...] = index[0:1] * 256 + index[1:2]
    project(index[2:3], x, wa, wf, ba, bf, out)


def project_parts(parts, weights):
    ew, cols = weights[0].shape
    rows = sum(p.shape[0] * (p.shape[1] - 16) * 128 // ew for p in parts)
    return pl.pallas_call(
        project_parts_kernel,
        out_shape=[jax.ShapeDtypeStruct((rows, cols), BF16), jax.ShapeDtypeStruct((1, rows), I32)],
        in_specs=[VMEM] * (4 + len(parts)),
        out_specs=[VMEM] * 2,
        compiler_params=PARAMS,
        cost_estimate=cost(4 * rows * ew * cols, 4 * ew * cols),
        name="project_parts",
    )(*weights, *parts)


def select_kernel(m, count, *refs):
    blocks, slots, outs = refs[:count], refs[count : 2 * count], refs[2 * count :]
    places = sum(out.shape[0] for out in outs) // 2
    z, t = lax.axis_index("ctx"), lax.axis_index("tp")
    first = jnp.bitwise_xor(z, m) * 2 * places
    i = lax.broadcasted_iota(I32, (2 * places, 1), 0)
    position = first + jnp.bitwise_xor(i, t * places)
    total = None
    for block, slot in zip(blocks, slots):
        chosen = (slot[...] == position).astype(F32).astype(BF16)
        part = jnp.dot(chosen, block[...], preferred_element_type=F32)
        total = part if total is None else total + part
    at = 0
    for out in outs:
        out[...] = total[at : at + out.shape[0]].astype(BF16)
        at += out.shape[0]


def select(m, blocks, slots, sizes):
    rows, cols = sum(b.shape[0] for b in blocks), blocks[0].shape[1]
    return pl.pallas_call(
        functools.partial(select_kernel, m, len(blocks)),
        out_shape=[jax.ShapeDtypeStruct((size, cols), BF16) for size in sizes],
        in_specs=[VMEM] * (2 * len(blocks)),
        out_specs=[VMEM] * len(sizes),
        compiler_params=PARAMS,
        cost_estimate=cost(2 * sum(sizes) * rows * cols, 2 * rows * cols),
        name="select",
    )(*blocks, *slots)


def upto(places, width):
    i = lax.broadcasted_iota(I32, (width, width), 0)
    j = lax.broadcasted_iota(I32, (width, width), 1)
    counts = i <= j
    if width > places:
        counts = jnp.logical_and(counts, (i < places) == (j < places))
    return counts.astype(F32).astype(BF16)


def one_hot(found):
    return found.astype(F32).astype(BF16)


def over_rows(a, b):
    return lax.dot_general(a, b, (((1,), (1,)), ((), ())), preferred_element_type=F32)


def running(flags, counts):
    return jnp.dot(one_hot(flags), counts, preferred_element_type=F32)


def packet_kernel(m, early, count, second, *refs):
    blocks, slots, outs = refs[:count], refs[count : 2 * count], refs[2 * count :]
    size = sum(out.shape[0] for out in outs) // 2
    places = blocks[0].shape[0] // 2
    first_size = places - size if second else size
    z, t = lax.axis_index("ctx"), lax.axis_index("tp")
    i = lax.broadcasted_iota(I32, (2 * places, 1), 0)
    position = jnp.bitwise_xor(z, m) * 2 * places + jnp.bitwise_xor(i, t * places)
    holds = [one_hot(slot[...] == position) for slot in slots]
    known = None
    for k in range(early):
        part = over_rows(jnp.ones((8, holds[k].shape[1]), BF16), holds[k])
        known = part if known is None else known + part
    counts = upto(places, 2 * places)
    wanted = known > 0.5
    number = running(wanted, counts)
    if second:
        wanted = jnp.logical_not(jnp.logical_and(wanted, number < first_size + 0.5))
        number = running(wanted, counts)
    number = jnp.where(wanted, number, 0.0)[0:1].astype(I32)
    e = lax.broadcasted_iota(I32, (2 * size, 1), 0)
    upper = (e >= size).astype(I32)
    lane_upper = (lax.broadcasted_iota(I32, (1, 2 * places), 1) >= places).astype(I32)
    pick = jnp.logical_and(number == e - upper * size + 1, lane_upper == upper)
    pick = one_hot(pick)
    total = None
    for block, hold in zip(blocks, holds):
        chosen = jnp.dot(pick, hold, preferred_element_type=F32).astype(BF16)
        part = jnp.dot(chosen, block[...], preferred_element_type=F32)
        total = part if total is None else total + part
    if second:
        outs[0][...] = total[:size].astype(BF16)
        outs[1][...] = total[size:].astype(BF16)
    else:
        outs[0][...] = total.astype(BF16)


def packet(m, early, blocks, slots, size, second):
    rows, cols = sum(b.shape[0] for b in blocks), blocks[0].shape[1]
    return pl.pallas_call(
        functools.partial(packet_kernel, m, early, len(blocks), second),
        out_shape=[jax.ShapeDtypeStruct((size if second else 2 * size, cols), BF16)] * (1 + second),
        in_specs=[VMEM] * (2 * len(blocks)),
        out_specs=[VMEM] * (1 + second),
        compiler_params=PARAMS,
        cost_estimate=cost(4 * size * rows * cols, 2 * rows * cols),
        name="packet",
    )(*blocks, *slots)


def order_kernel(first_size, parity, *refs):
    slots, outs = refs[:-2], refs[-2:]
    places = outs[0].shape[0]
    z, t = lax.axis_index("ctx"), lax.axis_index("tp")
    pair, odd = z // 2, lax.rem(z, 2)
    position = (2 * z + t) * places + lax.broadcasted_iota(I32, (places, 1), 0)
    source = lax.broadcasted_iota(I32, (8, 1), 0)
    known = None
    for k, slot in enumerate(slots):
        width = slot.shape[1]
        lane = lax.broadcasted_iota(I32, (1, width), 1)
        if k == 0:
            near, odd_rank = lane >= 0, parity[...]
        elif k in (1, 2):
            near = lane < places
            odd_rank = jnp.where(near, (lane >= places // 2).astype(I32), odd)
        else:
            near, odd_rank = lane < 0, jnp.zeros((1, width), I32) + 1 - odd
        owner_pair = jnp.where(near, pair, 1 - pair)
        held = jnp.logical_or(owner_pair == source // 2, odd_rank == lax.rem(source, 2))
        part = over_rows(one_hot(held), one_hot(slot[...] == position))
        known = part if known is None else known + part
    counts = upto(places, places)
    early = known > 0.5
    number = running(early, counts)
    early = jnp.logical_and(early, number < first_size + 0.5)
    later = running(jnp.logical_not(early), counts)
    place = jnp.where(early, number, later + first_size) - 1.0
    for m, out in zip((3, 2), outs):
        row = jnp.sum(jnp.where(source == jnp.bitwise_xor(z, m), place, 0.0), axis=0, keepdims=True)
        column = column_of(row.astype(I32))
        out[...] = one_hot(column == lax.broadcasted_iota(I32, (1, places), 1))


def order_of(first_size, parity, slots, places):
    return pl.pallas_call(
        functools.partial(order_kernel, first_size),
        out_shape=[jax.ShapeDtypeStruct((places, places), BF16)] * 2,
        in_specs=[VMEM] * (1 + len(slots)),
        out_specs=[VMEM] * 2,
        compiler_params=PARAMS,
        cost_estimate=cost(1 << 34, 0),
        name="order_of",
    )(parity, *slots)


def view(ref, places):
    if len(ref.shape) == 3:
        return ref.at[1 - lax.axis_index("tp")]
    return ref.at[pl.ds(0, places), :]


def square_sum(piece):
    wide = piece[...].astype(F32)
    return jnp.sum(wide * wide, axis=1, keepdims=True)


def squares_kernel(*refs):
    out = refs[-1]
    total = None
    for ref in refs[:-1]:
        part = ref[...] if ref.dtype == F32 else square_sum(view(ref, out.shape[0]))
        total = part if total is None else total + part
    out[...] = total


def squares(total, pieces, places, flops=0):
    operands = pieces if total is None else [total] + pieces
    return pl.pallas_call(
        squares_kernel,
        out_shape=jax.ShapeDtypeStruct((places, 1), F32),
        in_specs=[VMEM] * len(operands),
        out_specs=VMEM,
        compiler_params=PARAMS,
        cost_estimate=cost(flops, 0),
        name="squares",
    )(*operands)


def norm_kernel(places_of, fresh, gain, before, *refs):
    n = len(places_of)
    out, scaled, sems = refs[n], refs[n + 1], refs[n + 2]
    places, cols = scaled.shape[1:]
    pieces = [view(ref, places) for ref in refs[:n]]
    z, t = lax.axis_index("ctx"), lax.axis_index("tp")
    total = before[...]
    for k in fresh:
        total = total + square_sum(pieces[k])
    scale = lax.rsqrt(total / (n * cols) + 1e-06)
    copies = []
    for k, ((m, d), piece) in enumerate(zip(places_of, pieces)):
        block = jnp.bitwise_xor(z, m) * 2 + jnp.bitwise_xor(t, d)
        at = pl.ds(pl.multiple_of(block * cols, cols), cols)
        scaled[k] = (piece[...].astype(F32) * scale * gain[:, at].astype(F32)).astype(BF16)
        copies.append(pltpu.make_async_copy(scaled.at[k], out.at[:, at], sems.at[k]))
        copies[k].start()
    for copy in copies:
        copy.wait()


def norm(places_of, fresh, gain, before, pieces):
    n, places, cols = len(pieces), before.shape[0], pieces[0].shape[-1]
    return pl.pallas_call(
        functools.partial(norm_kernel, places_of, fresh),
        out_shape=jax.ShapeDtypeStruct((places, n * cols), BF16),
        in_specs=[VMEM] * (n + 2),
        out_specs=HBM,
        scratch_shapes=[pltpu.VMEM((n, places, cols), BF16), pltpu.SemaphoreType.DMA((n,))],
        compiler_params=PARAMS,
        cost_estimate=cost(4 * places * n * cols, 4 * places * n * cols),
        name="norm",
    )(gain, before, *pieces)


def last_kernel(far, whole, gain, before, before_too, *refs):
    orders, packets, pieces = refs[:2], refs[2:10], refs[10:14]
    out, scaled, sems = refs[14:]
    places, cols = scaled.shape[1:]
    z, t = lax.axis_index("ctx"), lax.axis_index("tp")
    total = before[...] + before_too[...]
    for k in range(4):
        later = packets[2 * k + 1][...]
        early = view(packets[2 * k], places - later.shape[0])[...]
        both = jnp.concatenate([early, later], axis=0)
        wide = jnp.dot(orders[k // 2][...], both, preferred_element_type=F32)
        scaled[k] = wide.astype(BF16)
        total = total + jnp.sum(wide * wide, axis=1, keepdims=True)
    scale = lax.rsqrt(total / (8 * cols) + 1e-06)
    copies = []
    for k, (m, d) in enumerate(far + whole):
        block = jnp.bitwise_xor(z, m) * 2 + jnp.bitwise_xor(t, d)
        at = pl.ds(pl.multiple_of(block * cols, cols), cols)
        piece = scaled[k] if k < 4 else view(pieces[k - 4], places)[...]
        scaled[k] = (piece.astype(F32) * scale * gain[:, at].astype(F32)).astype(BF16)
        copies.append(pltpu.make_async_copy(scaled.at[k], out.at[:, at], sems.at[k]))
        copies[k].start()
    for copy in copies:
        copy.wait()


def place_and_norm(far, whole, gain, before, orders, packets, pieces):
    places, cols = before[0].shape[0], packets[0].shape[1]
    operands = [gain, *before, *orders, *packets, *pieces]
    return pl.pallas_call(
        functools.partial(last_kernel, far, whole),
        out_shape=jax.ShapeDtypeStruct((places, 8 * cols), BF16),
        in_specs=[VMEM] * len(operands),
        out_specs=HBM,
        scratch_shapes=[pltpu.VMEM((8, places, cols), BF16), pltpu.SemaphoreType.DMA((8,))],
        compiler_params=PARAMS,
        cost_estimate=cost(32 * places * cols, 32 * places * cols),
        name="place_and_norm",
    )(*operands)


def after(x, *others):
    return lax.optimization_barrier((x, *others))[0]


def body(enc_rows, row_slot, row_kind, audio_proj, frame_proj, audio_bias, frame_bias, norm_gain):
    n = lax.axis_size("ctx")
    rows = enc_rows[0]
    half = rows.shape[0] // 2
    weights = (audio_proj, frame_proj, audio_bias[None, :], frame_bias[None, :])

    def over_ctx(x, m):
        return lax.ppermute(x, "ctx", [(i, i ^ m) for i in range(n)])

    def over_tp(x):
        return lax.ppermute(x, "tp", [(0, 1), (1, 0)])

    own = project_own(row_kind, rows, weights)
    blocks, slots = [own], [row_slot]

    def take(group):
        block, slot = project_parts(group, weights)
        blocks.append(block)
        slots.append(slot)

    def to_core(x, m, d):
        pairs = [(i * 2 + c, (i ^ m) * 2 + (c ^ d)) for i in range(n) for c in range(2)]
        return lax.ppermute(x, ("ctx", "tp"), pairs)

    def own_piece():
        pieces[0, 0], other = select(0, blocks, slots, [half, half])
        pieces[0, 1] = lax.all_gather(other, "tp", axis=0)
        return squares(None, [pieces[0, 0], pieces[0, 1]], half, OWN_FLOPS)

    def near_piece(total):
        pair = pieces[1]
        pieces[1, 0], pieces[1, 1] = pair, lax.all_gather(pair[half:], "tp", axis=0)
        return squares(total, [pieces[1, 0], pieces[1, 1]], half, NEAR_FLOPS)

    pieces = {}
    if n == 4:
        near, second, third, parity = to_send((None, 0, 1), rows, row_slot, row_kind)
        near, second, third = over_ctx(near, 1), over_ctx(second, 2), over_ctx(third, 3)
        first = lax.optimization_barrier((near, second, third, own))[:3]
        shared = [over_ctx(part, 1) for part in first[1:]]
        other = [over_tp(part)[None] for part in first]
        take([part[None] for part in first])
        other = lax.optimization_barrier((*other, blocks[-1]))[:3]
        take(other)

        early, size = len(blocks), 3 * half // 8
        sent = {}
        for m in (3, 2):
            chosen = packet(m, early, blocks, slots, size, False)
            slots[0] = after(slots[0], chosen[0])
            sent[m] = over_ctx(chosen[0], m)
        shared = lax.optimization_barrier((*shared, blocks[-1]))[:2]
        take([lax.all_gather(part, "tp", axis=0) for part in shared])

        (chosen,) = select(1, blocks, slots, [2 * half])
        slots[0] = after(slots[0], chosen)
        pieces[1] = over_ctx(chosen, 1)
        rest = {}
        for m in (2, 3):
            chosen = packet(m, early, blocks, slots, half - size, True)
            slots[0] = after(slots[0], chosen[0])
            waited = 3 if m == 2 else 2
            joined = lax.optimization_barrier((*chosen, sent[waited]))
            chosen, sent[waited] = joined[:2], joined[2]
            rest[m] = [to_core(piece, m, d) for d, piece in enumerate(chosen)]

        orders = order_of(size, parity, slots, half)
        slots[0] = after(slots[0], rest[2][0])
        total = [own_piece(), near_piece(None)]
        for m in (3, 2):
            whole_packet = sent[m]
            sent[m] = [whole_packet, lax.all_gather(whole_packet[size:], "tp", axis=0)]
        far, whole = ((3, 0), (3, 1), (2, 0), (2, 1)), ((1, 0), (1, 1), (0, 0), (0, 1))
        packets = [part for m, d in far for part in (sent[m][d], rest[m][d])]
        whole_pieces = [pieces[at] for at in whole]
        gain = norm_gain[None, :]
        return place_and_norm(far, whole, gain, total, orders, packets, whole_pieces)[None]
    else:
        (mine,) = to_send((None,), rows, row_slot, row_kind)
        arrived = [over_ctx(mine, m) for m in range(1, n)]
        for direct in arrived[:-1]:
            direct = after(direct, blocks[-1])
            take([lax.all_gather(direct, "tp", axis=0)])
        direct = after(arrived[-1], blocks[-1])
        swapped = over_tp(direct)
        take([direct[None]])
        take([swapped[None]])

        order = [n - 1, 1] + list(reversed(range(2, n - 1)))
        for m in order:
            chosen = select(m, blocks, slots, [2 * half] if m == 1 else [half, half])
            slots[0] = after(slots[0], chosen[0])
            if m == 1:
                pieces[m] = over_ctx(chosen[0], m)
                continue
            for d, piece in enumerate(chosen):
                pieces[m, d] = to_core(piece, m, d)
        total = squares(None, [pieces[n - 1, 0], pieces[n - 1, 1]], half)
        total = squares(near_piece(total), [own_piece()], half)
        for m in order[2:-1]:
            late = [after(pieces[m, d], total) for d in range(2)]
            total = squares(total, late, half)
        fresh = (2 * (n - 1), 2 * (n - 1) + 1)
        for d in range(2):
            pieces[order[-1], d] = after(pieces[order[-1], d], total)
        order = order[:-1] + [0, order[-1]]

    places_of = tuple((m, d) for m in order for d in range(2))
    return norm(places_of, fresh, norm_gain[None, :], total, [pieces[at] for at in places_of])[None]


def solution(mesh):
    return jax.shard_map(
        body,
        mesh=mesh,
        in_specs=(
            P(("groups", "enc"), "ctx", None),
            P(("groups", "enc"), "ctx"),
            P(("groups", "enc"), "ctx"),
            P(None, ("ctx", "tp")),
            P(None, ("ctx", "tp")),
            P(("ctx", "tp")),
            P(("ctx", "tp")),
            P(),
        ),
        out_specs=P(("groups", "enc"), ("ctx", "tp"), None),
        check_vma=False,
    )
```

```python
import functools

import jax
import jax.numpy as jnp
from jax import lax
from jax.experimental import pallas as pl
from jax.experimental.pallas import tpu as pltpu
from jax.sharding import PartitionSpec as P

VMEM = pl.BlockSpec(memory_space=pltpu.VMEM)
HBM = pl.BlockSpec(memory_space=pltpu.HBM)
PARAMS = pltpu.CompilerParams(vmem_limit_bytes=12 << 20)
OWN_FLOPS, NEAR_FLOPS = 1 << 35, 0
BF16, F32, I32 = jnp.bfloat16, jnp.float32, jnp.int32


def cost(flops, moved):
    return pl.CostEstimate(flops=flops // 16, bytes_accessed=moved // 16, transcendentals=0)


def to_tiles(x, out):
    at = 0
    for r in range(0, x.shape[0], 16):
        for c in range(0, x.shape[1], 128):
            out[at : at + 16, :] = x[r : r + 16, c : c + 128]
            at += 16


def from_tiles(tiles, width):
    per_row = width // 128
    lines = []
    for r in range(0, tiles.shape[0], 16 * per_row):
        line = [tiles[r + 16 * c : r + 16 * (c + 1)] for c in range(per_row)]
        lines.append(jnp.concatenate(line, axis=1))
    return jnp.concatenate(lines, axis=0)


def send_kernel(cuts, rows, slot, kind, *refs):
    outs, (rows_here, slot_here, kind_here, sems) = refs[: len(cuts)], refs[-4:]
    whole, width = rows.shape
    half = whole // 2
    z, t = lax.axis_index("ctx"), lax.axis_index("tp")
    dealt = len(cuts) > 1
    source = rows
    if not dealt:
        source = rows.at[pl.ds(pl.multiple_of(t * half, half), half), :]
    copies = [
        pltpu.make_async_copy(slot, slot_here, sems.at[0]),
        pltpu.make_async_copy(kind, kind_here, sems.at[1]),
        pltpu.make_async_copy(source, rows_here, sems.at[2]),
    ]
    for copy in copies:
        copy.start()
    copies[0].wait()
    copies[1].wait()
    if dealt:
        slot_row, slot_col = slot_here[...], column_of(slot_here[...])
        kind_col = column_of(kind_here[...])
        rank_row = jnp.sum((slot_col < slot_row).astype(I32), axis=0, keepdims=True)
        rank_col = jnp.sum((slot_row < slot_col).astype(I32), axis=1, keepdims=True)
        refs[len(cuts)][...] = lax.rem(rank_row, 2)

        def rank_at(k):
            odd = (k >= half // 2).astype(I32)
            return t * half + 2 * (k - odd * (half // 2)) + odd

        here = rank_col == rank_at(lax.broadcasted_iota(I32, (1, half), 1))
        slots = jnp.sum(jnp.where(here, slot_col, 0), axis=0, keepdims=True)
        kinds = jnp.sum(jnp.where(here, kind_col, 0), axis=0, keepdims=True)
        deal = rank_row == rank_at(lax.broadcasted_iota(I32, (half, 1), 0))
        copies[2].wait()
        rows_out = refs[-5]
        rows_out[...] = jnp.dot(
            deal.astype(F32).astype(BF16), rows_here[...], preferred_element_type=F32
        ).astype(BF16)
    else:
        slots = jnp.where(t == 0, slot_here[:, :half], slot_here[:, half:])
        kinds = jnp.where(t == 0, kind_here[:, :half], kind_here[:, half:])
        copies[2].wait()
        rows_out = rows_here
    for out, parity in zip(outs, cuts):
        x, s, k = rows_out, slots, kinds
        size = half
        if parity is not None:
            size = half // 2
            second = lax.rem(z + parity, 2)
            x = rows_out.at[pl.ds(pl.multiple_of(second * size, size), size), :]
            s = jnp.where(second == 0, slots[:, :size], slots[:, size:])
            k = jnp.where(second == 0, kinds[:, :size], kinds[:, size:])
        to_tiles(x, out)
        line = lax.broadcasted_iota(I32, (16, size), 0)
        index = jnp.where(line == 0, s // 256, jnp.where(line == 1, s % 256, k))
        index = jnp.where(line < 3, index, 0).astype(F32)
        if size < 128:
            index = jnp.concatenate([index, jnp.zeros((16, 128 - size), F32)], axis=1)
        out[size * width // 128 :, :] = index.astype(BF16)


def to_send(cuts, rows, slot, kind):
    half, width = rows.shape[0] // 2, rows.shape[1]
    sizes = [half if parity is None else half // 2 for parity in cuts]
    shapes = [(size * width // 128 + 16, 128) for size in sizes]
    dealt = len(cuts) > 1
    out_shape = [jax.ShapeDtypeStruct(shape, BF16) for shape in shapes]
    scratch = [pltpu.VMEM((half, width), BF16)]
    if dealt:
        out_shape.append(jax.ShapeDtypeStruct(slot.shape, I32))
        scratch.append(pltpu.VMEM(rows.shape, BF16))
    return pl.pallas_call(
        functools.partial(send_kernel, cuts),
        out_shape=out_shape,
        in_specs=[HBM] * 3,
        out_specs=[VMEM] * len(out_shape),
        scratch_shapes=scratch
        + [
            pltpu.VMEM(slot.shape, I32),
            pltpu.VMEM(slot.shape, I32),
            pltpu.SemaphoreType.DMA((3,)),
        ],
        compiler_params=pltpu.CompilerParams(vmem_limit_bytes=16 << 20),
        cost_estimate=cost(0, 4 * half * width),
        name="to_send",
    )(*[pltpu.with_memory_space_constraint(x, pltpu.HBM) for x in (rows, slot, kind)])


def column_of(row_vector):
    r = row_vector.shape[1]
    diagonal = lax.broadcasted_iota(I32, (r, r), 0) == lax.broadcasted_iota(I32, (r, r), 1)
    return jnp.sum(jnp.where(diagonal, row_vector, 0), axis=1, keepdims=True)


def project(kind_row, x, w_audio, w_frame, b_audio, b_frame, out):
    is_audio = column_of(kind_row) == 0
    audio = jnp.dot(x, w_audio[...], preferred_element_type=F32)
    frame = jnp.dot(x, w_frame[...], preferred_element_type=F32)
    audio = audio + b_audio[...].astype(F32)
    frame = frame + b_frame[...].astype(F32)
    out[...] = jnp.where(is_audio, audio, frame).astype(out.dtype)


def project_own_kernel(kind, x, wa, wf, ba, bf, out):
    project(kind[...], x[...], wa, wf, ba, bf, out)


def project_own(kind, rows, weights):
    ew, cols = weights[0].shape
    return pl.pallas_call(
        project_own_kernel,
        out_shape=jax.ShapeDtypeStruct((rows.shape[0], cols), BF16),
        in_specs=[VMEM] * 6,
        out_specs=VMEM,
        compiler_params=PARAMS,
        cost_estimate=cost(4 * rows.shape[0] * ew * cols, 4 * ew * cols),
        name="project_own",
    )(kind, rows, *weights)


def project_parts_kernel(wa, wf, ba, bf, *refs):
    parts, out, slots = refs[:-2], refs[-2], refs[-1]
    width = wa.shape[0]
    x, index = [], []
    for ref in parts:
        for k in range(ref.shape[0]):
            lines = ref.shape[1] - 16
            size = lines * 128 // width
            x.append(from_tiles(ref[k, :lines, :], width))
            index.append(ref[k, lines:, :].astype(F32).astype(I32)[:, :size])
    x = x[0] if len(x) == 1 else jnp.concatenate(x, axis=0)
    index = index[0] if len(index) == 1 else jnp.concatenate(index, axis=1)
    slots[...] = index[0:1] * 256 + index[1:2]
    project(index[2:3], x, wa, wf, ba, bf, out)


def project_parts(parts, weights):
    ew, cols = weights[0].shape
    rows = sum(p.shape[0] * (p.shape[1] - 16) * 128 // ew for p in parts)
    return pl.pallas_call(
        project_parts_kernel,
        out_shape=[jax.ShapeDtypeStruct((rows, cols), BF16), jax.ShapeDtypeStruct((1, rows), I32)],
        in_specs=[VMEM] * (4 + len(parts)),
        out_specs=[VMEM] * 2,
        compiler_params=PARAMS,
        cost_estimate=cost(4 * rows * ew * cols, 4 * ew * cols),
        name="project_parts",
    )(*weights, *parts)


def select_kernel(m, count, *refs):
    blocks, slots, outs = refs[:count], refs[count : 2 * count], refs[2 * count :]
    places = sum(out.shape[0] for out in outs) // 2
    z, t = lax.axis_index("ctx"), lax.axis_index("tp")
    first = jnp.bitwise_xor(z, m) * 2 * places
    i = lax.broadcasted_iota(I32, (2 * places, 1), 0)
    position = first + jnp.bitwise_xor(i, t * places)
    total = None
    for block, slot in zip(blocks, slots):
        chosen = (slot[...] == position).astype(F32).astype(BF16)
        part = jnp.dot(chosen, block[...], preferred_element_type=F32)
        total = part if total is None else total + part
    at = 0
    for out in outs:
        out[...] = total[at : at + out.shape[0]].astype(BF16)
        at += out.shape[0]


def select(m, blocks, slots, sizes):
    rows, cols = sum(b.shape[0] for b in blocks), blocks[0].shape[1]
    return pl.pallas_call(
        functools.partial(select_kernel, m, len(blocks)),
        out_shape=[jax.ShapeDtypeStruct((size, cols), BF16) for size in sizes],
        in_specs=[VMEM] * (2 * len(blocks)),
        out_specs=[VMEM] * len(sizes),
        compiler_params=PARAMS,
        cost_estimate=cost(2 * sum(sizes) * rows * cols, 2 * rows * cols),
        name="select",
    )(*blocks, *slots)


def upto(places, width):
    i = lax.broadcasted_iota(I32, (width, width), 0)
    j = lax.broadcasted_iota(I32, (width, width), 1)
    counts = i <= j
    if width > places:
        counts = jnp.logical_and(counts, (i < places) == (j < places))
    return counts.astype(F32).astype(BF16)


def one_hot(found):
    return found.astype(F32).astype(BF16)


def over_rows(a, b):
    return lax.dot_general(a, b, (((1,), (1,)), ((), ())), preferred_element_type=F32)


def running(flags, counts):
    return jnp.dot(one_hot(flags), counts, preferred_element_type=F32)


def packet_kernel(m, early, count, second, *refs):
    blocks, slots, outs = refs[:count], refs[count : 2 * count], refs[2 * count :]
    size = sum(out.shape[0] for out in outs) // 2
    places = blocks[0].shape[0] // 2
    first_size = places - size if second else size
    z, t = lax.axis_index("ctx"), lax.axis_index("tp")
    i = lax.broadcasted_iota(I32, (2 * places, 1), 0)
    position = jnp.bitwise_xor(z, m) * 2 * places + jnp.bitwise_xor(i, t * places)
    holds = [one_hot(slot[...] == position) for slot in slots]
    known = None
    for k in range(early):
        part = over_rows(jnp.ones((8, holds[k].shape[1]), BF16), holds[k])
        known = part if known is None else known + part
    counts = upto(places, 2 * places)
    wanted = known > 0.5
    number = running(wanted, counts)
    if second:
        wanted = jnp.logical_not(jnp.logical_and(wanted, number < first_size + 0.5))
        number = running(wanted, counts)
    number = jnp.where(wanted, number, 0.0)[0:1].astype(I32)
    e = lax.broadcasted_iota(I32, (2 * size, 1), 0)
    upper = (e >= size).astype(I32)
    lane_upper = (lax.broadcasted_iota(I32, (1, 2 * places), 1) >= places).astype(I32)
    pick = jnp.logical_and(number == e - upper * size + 1, lane_upper == upper)
    pick = one_hot(pick)
    total = None
    for block, hold in zip(blocks, holds):
        chosen = jnp.dot(pick, hold, preferred_element_type=F32).astype(BF16)
        part = jnp.dot(chosen, block[...], preferred_element_type=F32)
        total = part if total is None else total + part
    if second:
        outs[0][...] = total[:size].astype(BF16)
        outs[1][...] = total[size:].astype(BF16)
    else:
        outs[0][...] = total.astype(BF16)


def packet(m, early, blocks, slots, size, second):
    rows, cols = sum(b.shape[0] for b in blocks), blocks[0].shape[1]
    return pl.pallas_call(
        functools.partial(packet_kernel, m, early, len(blocks), second),
        out_shape=[jax.ShapeDtypeStruct((size if second else 2 * size, cols), BF16)] * (1 + second),
        in_specs=[VMEM] * (2 * len(blocks)),
        out_specs=[VMEM] * (1 + second),
        compiler_params=PARAMS,
        cost_estimate=cost(4 * size * rows * cols, 2 * rows * cols),
        name="packet",
    )(*blocks, *slots)


def order_kernel(first_size, parity, *refs):
    slots, outs = refs[:-2], refs[-2:]
    places = outs[0].shape[0]
    z, t = lax.axis_index("ctx"), lax.axis_index("tp")
    pair, odd = z // 2, lax.rem(z, 2)
    position = (2 * z + t) * places + lax.broadcasted_iota(I32, (places, 1), 0)
    source = lax.broadcasted_iota(I32, (8, 1), 0)
    known = None
    for k, slot in enumerate(slots):
        width = slot.shape[1]
        lane = lax.broadcasted_iota(I32, (1, width), 1)
        if k == 0:
            near, odd_rank = lane >= 0, parity[...]
        elif k in (1, 2):
            near = lane < places
            odd_rank = jnp.where(near, (lane >= places // 2).astype(I32), odd)
        else:
            near, odd_rank = lane < 0, jnp.zeros((1, width), I32) + 1 - odd
        owner_pair = jnp.where(near, pair, 1 - pair)
        held = jnp.logical_or(owner_pair == source // 2, odd_rank == lax.rem(source, 2))
        part = over_rows(one_hot(held), one_hot(slot[...] == position))
        known = part if known is None else known + part
    counts = upto(places, places)
    early = known > 0.5
    number = running(early, counts)
    early = jnp.logical_and(early, number < first_size + 0.5)
    later = running(jnp.logical_not(early), counts)
    place = jnp.where(early, number, later + first_size) - 1.0
    for m, out in zip((3, 2), outs):
        row = jnp.sum(jnp.where(source == jnp.bitwise_xor(z, m), place, 0.0), axis=0, keepdims=True)
        column = column_of(row.astype(I32))
        out[...] = one_hot(column == lax.broadcasted_iota(I32, (1, places), 1))


def order_of(first_size, parity, slots, places):
    return pl.pallas_call(
        functools.partial(order_kernel, first_size),
        out_shape=[jax.ShapeDtypeStruct((places, places), BF16)] * 2,
        in_specs=[VMEM] * (1 + len(slots)),
        out_specs=[VMEM] * 2,
        compiler_params=PARAMS,
        cost_estimate=cost(1 << 34, 0),
        name="order_of",
    )(parity, *slots)


def view(ref, places):
    if len(ref.shape) == 3:
        return ref.at[1 - lax.axis_index("tp")]
    return ref.at[pl.ds(0, places), :]


def square_sum(piece):
    wide = piece[...].astype(F32)
    return jnp.sum(wide * wide, axis=1, keepdims=True)


def squares_kernel(*refs):
    out = refs[-1]
    total = None
    for ref in refs[:-1]:
        part = ref[...] if ref.dtype == F32 else square_sum(view(ref, out.shape[0]))
        total = part if total is None else total + part
    out[...] = total


def squares(total, pieces, places, flops=0):
    operands = pieces if total is None else [total] + pieces
    return pl.pallas_call(
        squares_kernel,
        out_shape=jax.ShapeDtypeStruct((places, 1), F32),
        in_specs=[VMEM] * len(operands),
        out_specs=VMEM,
        compiler_params=PARAMS,
        cost_estimate=cost(flops, 0),
        name="squares",
    )(*operands)


def norm_kernel(places_of, fresh, gain, before, *refs):
    n = len(places_of)
    out, scaled, sems = refs[n], refs[n + 1], refs[n + 2]
    places, cols = scaled.shape[1:]
    pieces = [view(ref, places) for ref in refs[:n]]
    z, t = lax.axis_index("ctx"), lax.axis_index("tp")
    total = before[...]
    for k in fresh:
        total = total + square_sum(pieces[k])
    scale = lax.rsqrt(total / (n * cols) + 1e-06)
    copies = []
    for k, ((m, d), piece) in enumerate(zip(places_of, pieces)):
        block = jnp.bitwise_xor(z, m) * 2 + jnp.bitwise_xor(t, d)
        at = pl.ds(pl.multiple_of(block * cols, cols), cols)
        scaled[k] = (piece[...].astype(F32) * scale * gain[:, at].astype(F32)).astype(BF16)
        copies.append(pltpu.make_async_copy(scaled.at[k], out.at[:, at], sems.at[k]))
        copies[k].start()
    for copy in copies:
        copy.wait()


def norm(places_of, fresh, gain, before, pieces):
    n, places, cols = len(pieces), before.shape[0], pieces[0].shape[-1]
    return pl.pallas_call(
        functools.partial(norm_kernel, places_of, fresh),
        out_shape=jax.ShapeDtypeStruct((places, n * cols), BF16),
        in_specs=[VMEM] * (n + 2),
        out_specs=HBM,
        scratch_shapes=[pltpu.VMEM((n, places, cols), BF16), pltpu.SemaphoreType.DMA((n,))],
        compiler_params=PARAMS,
        cost_estimate=cost(4 * places * n * cols, 4 * places * n * cols),
        name="norm",
    )(gain, before, *pieces)


def placed(order, early, later):
    early = view(early, order.shape[0] - later.shape[0])[...]
    both = jnp.concatenate([early, later[...]], axis=0)
    return jnp.dot(order[...], both, preferred_element_type=F32)


def place_kernel(order, *refs):
    packets, outs = refs[:4], refs[4:]
    total = None
    for d in range(2):
        wide = placed(order, packets[2 * d], packets[2 * d + 1])
        outs[d][...] = wide.astype(BF16)
        part = jnp.sum(wide * wide, axis=1, keepdims=True)
        total = part if total is None else total + part
    outs[2][...] = total


def place(order, packets):
    places, cols = order.shape[0], packets[0].shape[-1]
    piece = jax.ShapeDtypeStruct((places, cols), BF16)
    return pl.pallas_call(
        place_kernel,
        out_shape=[piece, piece, jax.ShapeDtypeStruct((places, 1), F32)],
        in_specs=[VMEM] * 5,
        out_specs=[VMEM] * 3,
        compiler_params=PARAMS,
        cost_estimate=cost(0, 0),
        name="place",
    )(order, *packets)


def last_kernel(far, whole, gain, *refs):
    before, order, packets, pieces = refs[:3], refs[3], refs[4:8], refs[8:14]
    out, scaled, sems = refs[14:]
    places, cols = scaled.shape[1:]
    z, t = lax.axis_index("ctx"), lax.axis_index("tp")
    total = before[0][...] + before[1][...] + before[2][...]
    for k in range(2):
        wide = placed(order, packets[2 * k], packets[2 * k + 1])
        scaled[k] = wide.astype(BF16)
        total = total + jnp.sum(wide * wide, axis=1, keepdims=True)
    scale = lax.rsqrt(total / (8 * cols) + 1e-06)
    copies = []
    for k, (m, d) in enumerate(far + whole):
        block = jnp.bitwise_xor(z, m) * 2 + jnp.bitwise_xor(t, d)
        at = pl.ds(pl.multiple_of(block * cols, cols), cols)
        piece = scaled[k] if k < 2 else view(pieces[k - 2], places)[...]
        scaled[k] = (piece.astype(F32) * scale * gain[:, at].astype(F32)).astype(BF16)
        copies.append(pltpu.make_async_copy(scaled.at[k], out.at[:, at], sems.at[k]))
        copies[k].start()
    for copy in copies:
        copy.wait()


def place_and_norm(far, whole, gain, before, order, packets, pieces):
    places, cols = before[0].shape[0], packets[0].shape[1]
    operands = [gain, *before, order, *packets, *pieces]
    return pl.pallas_call(
        functools.partial(last_kernel, far, whole),
        out_shape=jax.ShapeDtypeStruct((places, 8 * cols), BF16),
        in_specs=[VMEM] * len(operands),
        out_specs=HBM,
        scratch_shapes=[pltpu.VMEM((8, places, cols), BF16), pltpu.SemaphoreType.DMA((8,))],
        compiler_params=PARAMS,
        cost_estimate=cost(32 * places * cols, 32 * places * cols),
        name="place_and_norm",
    )(*operands)


def after(x, *others):
    return lax.optimization_barrier((x, *others))[0]


def body(enc_rows, row_slot, row_kind, audio_proj, frame_proj, audio_bias, frame_bias, norm_gain):
    n = lax.axis_size("ctx")
    rows = enc_rows[0]
    half = rows.shape[0] // 2
    weights = (audio_proj, frame_proj, audio_bias[None, :], frame_bias[None, :])

    def over_ctx(x, m):
        return lax.ppermute(x, "ctx", [(i, i ^ m) for i in range(n)])

    def over_tp(x):
        return lax.ppermute(x, "tp", [(0, 1), (1, 0)])

    own = project_own(row_kind, rows, weights)
    blocks, slots = [own], [row_slot]

    def take(group):
        block, slot = project_parts(group, weights)
        blocks.append(block)
        slots.append(slot)

    def to_core(x, m, d):
        pairs = [(i * 2 + c, (i ^ m) * 2 + (c ^ d)) for i in range(n) for c in range(2)]
        return lax.ppermute(x, ("ctx", "tp"), pairs)

    def own_piece():
        pieces[0, 0], other = select(0, blocks, slots, [half, half])
        pieces[0, 1] = lax.all_gather(other, "tp", axis=0)
        return squares(None, [pieces[0, 0], pieces[0, 1]], half, OWN_FLOPS)

    def near_piece(total):
        pair = pieces[1]
        pieces[1, 0], pieces[1, 1] = pair, lax.all_gather(pair[half:], "tp", axis=0)
        return squares(total, [pieces[1, 0], pieces[1, 1]], half, NEAR_FLOPS)

    pieces = {}
    if n == 4:
        near, second, third, parity = to_send((None, 0, 1), rows, row_slot, row_kind)
        near, second, third = over_ctx(near, 1), over_ctx(second, 2), over_ctx(third, 3)
        first = lax.optimization_barrier((near, second, third, own))[:3]
        shared = [over_ctx(part, 1) for part in first[1:]]
        other = [over_tp(part)[None] for part in first]
        take([part[None] for part in first])
        other = lax.optimization_barrier((*other, blocks[-1]))[:3]
        take(other)

        early, size = len(blocks), 3 * half // 8
        sent = {}
        for m in (3, 2):
            chosen = packet(m, early, blocks, slots, size, False)
            slots[0] = after(slots[0], chosen[0])
            sent[m] = over_ctx(chosen[0], m)
        shared = lax.optimization_barrier((*shared, blocks[-1]))[:2]
        take([lax.all_gather(part, "tp", axis=0) for part in shared])

        (chosen,) = select(1, blocks, slots, [2 * half])
        slots[0] = after(slots[0], chosen)
        pieces[1] = over_ctx(chosen, 1)
        rest = {}
        for m in (2, 3):
            chosen = packet(m, early, blocks, slots, half - size, True)
            slots[0] = after(slots[0], chosen[0])
            waited = 3 if m == 2 else 2
            joined = lax.optimization_barrier((*chosen, sent[waited]))
            chosen, sent[waited] = joined[:2], joined[2]
            rest[m] = [to_core(piece, m, d) for d, piece in enumerate(chosen)]

        orders = order_of(size, parity, slots, half)
        slots[0] = after(slots[0], rest[2][0])
        total = [own_piece(), near_piece(None)]
        for m in (3, 2):
            whole_packet = sent[m]
            sent[m] = [whole_packet, lax.all_gather(whole_packet[size:], "tp", axis=0)]
        packets = {m: [part for d in range(2) for part in (sent[m][d], rest[m][d])] for m in (3, 2)}
        order3, order2 = orders
        pieces[2, 0], pieces[2, 1], squared = place(order2, packets[2])
        far, whole = ((3, 0), (3, 1)), ((2, 0), (2, 1), (1, 0), (1, 1), (0, 0), (0, 1))
        whole_pieces = [pieces[at] for at in whole]
        gain, total = norm_gain[None, :], [*total, squared]
        return place_and_norm(far, whole, gain, total, order3, packets[3], whole_pieces)[None]
    else:
        (mine,) = to_send((None,), rows, row_slot, row_kind)
        arrived = [over_ctx(mine, m) for m in range(1, n)]
        for direct in arrived[:-1]:
            direct = after(direct, blocks[-1])
            take([lax.all_gather(direct, "tp", axis=0)])
        direct = after(arrived[-1], blocks[-1])
        swapped = over_tp(direct)
        take([direct[None]])
        take([swapped[None]])

        order = [n - 1, 1] + list(reversed(range(2, n - 1)))
        for m in order:
            chosen = select(m, blocks, slots, [2 * half] if m == 1 else [half, half])
            slots[0] = after(slots[0], chosen[0])
            if m == 1:
                pieces[m] = over_ctx(chosen[0], m)
                continue
            for d, piece in enumerate(chosen):
                pieces[m, d] = to_core(piece, m, d)
        total = squares(None, [pieces[n - 1, 0], pieces[n - 1, 1]], half)
        total = squares(near_piece(total), [own_piece()], half)
        for m in order[2:-1]:
            late = [after(pieces[m, d], total) for d in range(2)]
            total = squares(total, late, half)
        fresh = (2 * (n - 1), 2 * (n - 1) + 1)
        for d in range(2):
            pieces[order[-1], d] = after(pieces[order[-1], d], total)
        order = order[:-1] + [0, order[-1]]

    places_of = tuple((m, d) for m in order for d in range(2))
    return norm(places_of, fresh, norm_gain[None, :], total, [pieces[at] for at in places_of])[None]


def solution(mesh):
    return jax.shard_map(
        body,
        mesh=mesh,
        in_specs=(
            P(("groups", "enc"), "ctx", None),
            P(("groups", "enc"), "ctx"),
            P(("groups", "enc"), "ctx"),
            P(None, ("ctx", "tp")),
            P(None, ("ctx", "tp")),
            P(("ctx", "tp")),
            P(("ctx", "tp")),
            P(),
        ),
        out_specs=P(("groups", "enc"), ("ctx", "tp"), None),
        check_vma=False,
    )
```

```python
import functools

import jax
import jax.numpy as jnp
from jax import lax
from jax.experimental import pallas as pl
from jax.experimental.pallas import tpu as pltpu
from jax.sharding import PartitionSpec as P

VMEM = pl.BlockSpec(memory_space=pltpu.VMEM)
HBM = pl.BlockSpec(memory_space=pltpu.HBM)
PARAMS = pltpu.CompilerParams(vmem_limit_bytes=12 << 20)
OWN_FLOPS, NEAR_FLOPS = 1 << 35, 0
BF16, F32, I32 = jnp.bfloat16, jnp.float32, jnp.int32


def cost(flops, moved):
    return pl.CostEstimate(flops=flops // 16, bytes_accessed=moved // 16, transcendentals=0)


def to_tiles(x, out):
    at = 0
    for r in range(0, x.shape[0], 16):
        for c in range(0, x.shape[1], 128):
            out[at : at + 16, :] = x[r : r + 16, c : c + 128]
            at += 16


def from_tiles(tiles, width):
    per_row = width // 128
    lines = []
    for r in range(0, tiles.shape[0], 16 * per_row):
        line = [tiles[r + 16 * c : r + 16 * (c + 1)] for c in range(per_row)]
        lines.append(jnp.concatenate(line, axis=1))
    return jnp.concatenate(lines, axis=0)


def send_kernel(cuts, rows, slot, kind, *refs):
    outs, (rows_here, slot_here, kind_here, sems) = refs[: len(cuts)], refs[-4:]
    whole, width = rows.shape
    half = whole // 2
    z, t = lax.axis_index("ctx"), lax.axis_index("tp")
    dealt = len(cuts) > 1
    source = rows
    if not dealt:
        source = rows.at[pl.ds(pl.multiple_of(t * half, half), half), :]
    copies = [
        pltpu.make_async_copy(slot, slot_here, sems.at[0]),
        pltpu.make_async_copy(kind, kind_here, sems.at[1]),
        pltpu.make_async_copy(source, rows_here, sems.at[2]),
    ]
    for copy in copies:
        copy.start()
    copies[0].wait()
    copies[1].wait()
    if dealt:
        slot_row, slot_col = slot_here[...], column_of(slot_here[...])
        kind_col = column_of(kind_here[...])
        rank_row = jnp.sum((slot_col < slot_row).astype(I32), axis=0, keepdims=True)
        rank_col = jnp.sum((slot_row < slot_col).astype(I32), axis=1, keepdims=True)
        refs[len(cuts)][...] = lax.rem(rank_row, 2)

        def rank_at(k):
            odd = (k >= half // 2).astype(I32)
            return t * half + 2 * (k - odd * (half // 2)) + odd

        here = rank_col == rank_at(lax.broadcasted_iota(I32, (1, half), 1))
        slots = jnp.sum(jnp.where(here, slot_col, 0), axis=0, keepdims=True)
        kinds = jnp.sum(jnp.where(here, kind_col, 0), axis=0, keepdims=True)
        deal = rank_row == rank_at(lax.broadcasted_iota(I32, (half, 1), 0))
        copies[2].wait()
        rows_out = refs[-5]
        rows_out[...] = jnp.dot(
            deal.astype(F32).astype(BF16), rows_here[...], preferred_element_type=F32
        ).astype(BF16)
    else:
        slots = jnp.where(t == 0, slot_here[:, :half], slot_here[:, half:])
        kinds = jnp.where(t == 0, kind_here[:, :half], kind_here[:, half:])
        copies[2].wait()
        rows_out = rows_here
    for out, parity in zip(outs, cuts):
        x, s, k = rows_out, slots, kinds
        size = half
        if parity is not None:
            size = half // 2
            second = lax.rem(z + parity, 2)
            x = rows_out.at[pl.ds(pl.multiple_of(second * size, size), size), :]
            s = jnp.where(second == 0, slots[:, :size], slots[:, size:])
            k = jnp.where(second == 0, kinds[:, :size], kinds[:, size:])
        to_tiles(x, out)
        line = lax.broadcasted_iota(I32, (16, size), 0)
        index = jnp.where(line == 0, s // 256, jnp.where(line == 1, s % 256, k))
        index = jnp.where(line < 3, index, 0).astype(F32)
        if size < 128:
            index = jnp.concatenate([index, jnp.zeros((16, 128 - size), F32)], axis=1)
        out[size * width // 128 :, :] = index.astype(BF16)


def to_send(cuts, rows, slot, kind):
    half, width = rows.shape[0] // 2, rows.shape[1]
    sizes = [half if parity is None else half // 2 for parity in cuts]
    shapes = [(size * width // 128 + 16, 128) for size in sizes]
    dealt = len(cuts) > 1
    out_shape = [jax.ShapeDtypeStruct(shape, BF16) for shape in shapes]
    scratch = [pltpu.VMEM((half, width), BF16)]
    if dealt:
        out_shape.append(jax.ShapeDtypeStruct(slot.shape, I32))
        scratch.append(pltpu.VMEM(rows.shape, BF16))
    return pl.pallas_call(
        functools.partial(send_kernel, cuts),
        out_shape=out_shape,
        in_specs=[HBM] * 3,
        out_specs=[VMEM] * len(out_shape),
        scratch_shapes=scratch
        + [
            pltpu.VMEM(slot.shape, I32),
            pltpu.VMEM(slot.shape, I32),
            pltpu.SemaphoreType.DMA((3,)),
        ],
        compiler_params=pltpu.CompilerParams(vmem_limit_bytes=16 << 20),
        cost_estimate=cost(0, 4 * half * width),
        name="to_send",
    )(*[pltpu.with_memory_space_constraint(x, pltpu.HBM) for x in (rows, slot, kind)])


def column_of(row_vector):
    r = row_vector.shape[1]
    diagonal = lax.broadcasted_iota(I32, (r, r), 0) == lax.broadcasted_iota(I32, (r, r), 1)
    return jnp.sum(jnp.where(diagonal, row_vector, 0), axis=1, keepdims=True)


def project(kind_row, x, w_audio, w_frame, b_audio, b_frame, out):
    is_audio = column_of(kind_row) == 0
    audio = jnp.dot(x, w_audio[...], preferred_element_type=F32)
    frame = jnp.dot(x, w_frame[...], preferred_element_type=F32)
    audio = audio + b_audio[...].astype(F32)
    frame = frame + b_frame[...].astype(F32)
    out[...] = jnp.where(is_audio, audio, frame).astype(out.dtype)


def project_own_kernel(kind, x, wa, wf, ba, bf, out):
    project(kind[...], x[...], wa, wf, ba, bf, out)


def project_own(kind, rows, weights):
    ew, cols = weights[0].shape
    return pl.pallas_call(
        project_own_kernel,
        out_shape=jax.ShapeDtypeStruct((rows.shape[0], cols), BF16),
        in_specs=[VMEM] * 6,
        out_specs=VMEM,
        compiler_params=PARAMS,
        cost_estimate=cost(4 * rows.shape[0] * ew * cols, 4 * ew * cols),
        name="project_own",
    )(kind, rows, *weights)


def project_parts_kernel(wa, wf, ba, bf, *refs):
    parts, out, slots = refs[:-2], refs[-2], refs[-1]
    width = wa.shape[0]
    x, index = [], []
    for ref in parts:
        for k in range(ref.shape[0]):
            lines = ref.shape[1] - 16
            size = lines * 128 // width
            x.append(from_tiles(ref[k, :lines, :], width))
            index.append(ref[k, lines:, :].astype(F32).astype(I32)[:, :size])
    x = x[0] if len(x) == 1 else jnp.concatenate(x, axis=0)
    index = index[0] if len(index) == 1 else jnp.concatenate(index, axis=1)
    slots[...] = index[0:1] * 256 + index[1:2]
    project(index[2:3], x, wa, wf, ba, bf, out)


def project_parts(parts, weights):
    ew, cols = weights[0].shape
    rows = sum(p.shape[0] * (p.shape[1] - 16) * 128 // ew for p in parts)
    return pl.pallas_call(
        project_parts_kernel,
        out_shape=[jax.ShapeDtypeStruct((rows, cols), BF16), jax.ShapeDtypeStruct((1, rows), I32)],
        in_specs=[VMEM] * (4 + len(parts)),
        out_specs=[VMEM] * 2,
        compiler_params=PARAMS,
        cost_estimate=cost(4 * rows * ew * cols, 4 * ew * cols),
        name="project_parts",
    )(*weights, *parts)


def select_kernel(m, count, *refs):
    blocks, slots, outs = refs[:count], refs[count : 2 * count], refs[2 * count :]
    places = sum(out.shape[0] for out in outs) // 2
    z, t = lax.axis_index("ctx"), lax.axis_index("tp")
    first = jnp.bitwise_xor(z, m) * 2 * places
    i = lax.broadcasted_iota(I32, (2 * places, 1), 0)
    position = first + jnp.bitwise_xor(i, t * places)
    total = None
    for block, slot in zip(blocks, slots):
        chosen = (slot[...] == position).astype(F32).astype(BF16)
        part = jnp.dot(chosen, block[...], preferred_element_type=F32)
        total = part if total is None else total + part
    at = 0
    for out in outs:
        out[...] = total[at : at + out.shape[0]].astype(BF16)
        at += out.shape[0]


def select(m, blocks, slots, sizes):
    rows, cols = sum(b.shape[0] for b in blocks), blocks[0].shape[1]
    return pl.pallas_call(
        functools.partial(select_kernel, m, len(blocks)),
        out_shape=[jax.ShapeDtypeStruct((size, cols), BF16) for size in sizes],
        in_specs=[VMEM] * (2 * len(blocks)),
        out_specs=[VMEM] * len(sizes),
        compiler_params=PARAMS,
        cost_estimate=cost(2 * sum(sizes) * rows * cols, 2 * rows * cols),
        name="select",
    )(*blocks, *slots)


def upto(places, width):
    i = lax.broadcasted_iota(I32, (width, width), 0)
    j = lax.broadcasted_iota(I32, (width, width), 1)
    counts = i <= j
    if width > places:
        counts = jnp.logical_and(counts, (i < places) == (j < places))
    return counts.astype(F32).astype(BF16)


def one_hot(found):
    return found.astype(F32).astype(BF16)


def over_rows(a, b):
    return lax.dot_general(a, b, (((1,), (1,)), ((), ())), preferred_element_type=F32)


def running(flags, counts):
    return jnp.dot(one_hot(flags), counts, preferred_element_type=F32)


def packet_kernel(m, early, count, second, *refs):
    blocks, slots, outs = refs[:count], refs[count : 2 * count], refs[2 * count :]
    size = sum(out.shape[0] for out in outs) // 2
    places = blocks[0].shape[0] // 2
    first_size = places - size if second else size
    z, t = lax.axis_index("ctx"), lax.axis_index("tp")
    i = lax.broadcasted_iota(I32, (2 * places, 1), 0)
    position = jnp.bitwise_xor(z, m) * 2 * places + jnp.bitwise_xor(i, t * places)
    holds = [one_hot(slot[...] == position) for slot in slots]
    known = None
    for k in range(early):
        part = over_rows(jnp.ones((8, holds[k].shape[1]), BF16), holds[k])
        known = part if known is None else known + part
    counts = upto(places, 2 * places)
    wanted = known > 0.5
    number = running(wanted, counts)
    if second:
        wanted = jnp.logical_not(jnp.logical_and(wanted, number < first_size + 0.5))
        number = running(wanted, counts)
    number = jnp.where(wanted, number, 0.0)[0:1].astype(I32)
    e = lax.broadcasted_iota(I32, (2 * size, 1), 0)
    upper = (e >= size).astype(I32)
    lane_upper = (lax.broadcasted_iota(I32, (1, 2 * places), 1) >= places).astype(I32)
    pick = jnp.logical_and(number == e - upper * size + 1, lane_upper == upper)
    pick = one_hot(pick)
    total = None
    for block, hold in zip(blocks, holds):
        chosen = jnp.dot(pick, hold, preferred_element_type=F32).astype(BF16)
        part = jnp.dot(chosen, block[...], preferred_element_type=F32)
        total = part if total is None else total + part
    if second:
        outs[0][...] = total[:size].astype(BF16)
        outs[1][...] = total[size:].astype(BF16)
    else:
        outs[0][...] = total.astype(BF16)


def packet(m, early, blocks, slots, size, second):
    rows, cols = sum(b.shape[0] for b in blocks), blocks[0].shape[1]
    return pl.pallas_call(
        functools.partial(packet_kernel, m, early, len(blocks), second),
        out_shape=[jax.ShapeDtypeStruct((size if second else 2 * size, cols), BF16)] * (1 + second),
        in_specs=[VMEM] * (2 * len(blocks)),
        out_specs=[VMEM] * (1 + second),
        compiler_params=PARAMS,
        cost_estimate=cost(4 * size * rows * cols, 2 * rows * cols),
        name="packet",
    )(*blocks, *slots)


def parts_and_packet_kernel(m, early, n_parts, *refs):
    weights, parts = refs[:4], refs[4 : 4 + n_parts]
    blocks, slots = refs[4 + n_parts : 3 + n_parts + early], refs[3 + n_parts + early : -3]
    block, slot, out = refs[-3:]
    project_parts_kernel(*weights, *parts, block, slot)
    packet_kernel(m, early, early, False, *blocks, block, *slots, slot, out)


def parts_and_packet(m, parts, weights, blocks, slots, size):
    ew, cols = weights[0].shape
    rows = sum(p.shape[0] * (p.shape[1] - 16) * 128 // ew for p in parts)
    operands = [*weights, *parts, *blocks, *slots]
    return pl.pallas_call(
        functools.partial(parts_and_packet_kernel, m, len(blocks) + 1, len(parts)),
        out_shape=[
            jax.ShapeDtypeStruct((rows, cols), BF16),
            jax.ShapeDtypeStruct((1, rows), I32),
            jax.ShapeDtypeStruct((2 * size, cols), BF16),
        ],
        in_specs=[VMEM] * len(operands),
        out_specs=[VMEM] * 3,
        compiler_params=PARAMS,
        cost_estimate=cost(4 * rows * ew * cols, 4 * ew * cols),
        name="parts_and_packet",
    )(*operands)


def order_kernel(first_size, parity, *refs):
    slots, outs = refs[:-2], refs[-2:]
    places = outs[0].shape[0]
    z, t = lax.axis_index("ctx"), lax.axis_index("tp")
    pair, odd = z // 2, lax.rem(z, 2)
    position = (2 * z + t) * places + lax.broadcasted_iota(I32, (places, 1), 0)
    source = lax.broadcasted_iota(I32, (8, 1), 0)
    known = None
    for k, slot in enumerate(slots):
        width = slot.shape[1]
        lane = lax.broadcasted_iota(I32, (1, width), 1)
        if k == 0:
            near, odd_rank = lane >= 0, parity[...]
        elif k in (1, 2):
            near = lane < places
            odd_rank = jnp.where(near, (lane >= places // 2).astype(I32), odd)
        else:
            near, odd_rank = lane < 0, jnp.zeros((1, width), I32) + 1 - odd
        owner_pair = jnp.where(near, pair, 1 - pair)
        held = jnp.logical_or(owner_pair == source // 2, odd_rank == lax.rem(source, 2))
        part = over_rows(one_hot(held), one_hot(slot[...] == position))
        known = part if known is None else known + part
    counts = upto(places, places)
    early = known > 0.5
    number = running(early, counts)
    early = jnp.logical_and(early, number < first_size + 0.5)
    later = running(jnp.logical_not(early), counts)
    place = jnp.where(early, number, later + first_size) - 1.0
    for m, out in zip((3, 2), outs):
        row = jnp.sum(jnp.where(source == jnp.bitwise_xor(z, m), place, 0.0), axis=0, keepdims=True)
        column = column_of(row.astype(I32))
        out[...] = one_hot(column == lax.broadcasted_iota(I32, (1, places), 1))


def order_of(first_size, parity, slots, places):
    return pl.pallas_call(
        functools.partial(order_kernel, first_size),
        out_shape=[jax.ShapeDtypeStruct((places, places), BF16)] * 2,
        in_specs=[VMEM] * (1 + len(slots)),
        out_specs=[VMEM] * 2,
        compiler_params=PARAMS,
        cost_estimate=cost(1 << 34, 0),
        name="order_of",
    )(parity, *slots)


def view(ref, places):
    if len(ref.shape) == 3:
        return ref.at[1 - lax.axis_index("tp")]
    return ref.at[pl.ds(0, places), :]


def square_sum(piece):
    wide = piece[...].astype(F32)
    return jnp.sum(wide * wide, axis=1, keepdims=True)


def squares_kernel(*refs):
    out = refs[-1]
    total = None
    for ref in refs[:-1]:
        part = ref[...] if ref.dtype == F32 else square_sum(view(ref, out.shape[0]))
        total = part if total is None else total + part
    out[...] = total


def squares(total, pieces, places, flops=0):
    operands = pieces if total is None else [total] + pieces
    return pl.pallas_call(
        squares_kernel,
        out_shape=jax.ShapeDtypeStruct((places, 1), F32),
        in_specs=[VMEM] * len(operands),
        out_specs=VMEM,
        compiler_params=PARAMS,
        cost_estimate=cost(flops, 0),
        name="squares",
    )(*operands)


def norm_kernel(places_of, fresh, gain, before, *refs):
    n = len(places_of)
    out, scaled, sems = refs[n], refs[n + 1], refs[n + 2]
    places, cols = scaled.shape[1:]
    pieces = [view(ref, places) for ref in refs[:n]]
    z, t = lax.axis_index("ctx"), lax.axis_index("tp")
    total = before[...]
    for k in fresh:
        total = total + square_sum(pieces[k])
    scale = lax.rsqrt(total / (n * cols) + 1e-06)
    copies = []
    for k, ((m, d), piece) in enumerate(zip(places_of, pieces)):
        block = jnp.bitwise_xor(z, m) * 2 + jnp.bitwise_xor(t, d)
        at = pl.ds(pl.multiple_of(block * cols, cols), cols)
        scaled[k] = (piece[...].astype(F32) * scale * gain[:, at].astype(F32)).astype(BF16)
        copies.append(pltpu.make_async_copy(scaled.at[k], out.at[:, at], sems.at[k]))
        copies[k].start()
    for copy in copies:
        copy.wait()


def norm(places_of, fresh, gain, before, pieces):
    n, places, cols = len(pieces), before.shape[0], pieces[0].shape[-1]
    return pl.pallas_call(
        functools.partial(norm_kernel, places_of, fresh),
        out_shape=jax.ShapeDtypeStruct((places, n * cols), BF16),
        in_specs=[VMEM] * (n + 2),
        out_specs=HBM,
        scratch_shapes=[pltpu.VMEM((n, places, cols), BF16), pltpu.SemaphoreType.DMA((n,))],
        compiler_params=PARAMS,
        cost_estimate=cost(4 * places * n * cols, 4 * places * n * cols),
        name="norm",
    )(gain, before, *pieces)


def placed(order, early, later):
    early = view(early, order.shape[0] - later.shape[0])[...]
    both = jnp.concatenate([early, later[...]], axis=0)
    return jnp.dot(order[...], both, preferred_element_type=F32)


def place_kernel(order, *refs):
    packets, outs = refs[:4], refs[4:]
    total = None
    for d in range(2):
        wide = placed(order, packets[2 * d], packets[2 * d + 1])
        outs[d][...] = wide.astype(BF16)
        part = jnp.sum(wide * wide, axis=1, keepdims=True)
        total = part if total is None else total + part
    outs[2][...] = total


def place(order, packets):
    places, cols = order.shape[0], packets[0].shape[-1]
    piece = jax.ShapeDtypeStruct((places, cols), BF16)
    return pl.pallas_call(
        place_kernel,
        out_shape=[piece, piece, jax.ShapeDtypeStruct((places, 1), F32)],
        in_specs=[VMEM] * 5,
        out_specs=[VMEM] * 3,
        compiler_params=PARAMS,
        cost_estimate=cost(0, 0),
        name="place",
    )(order, *packets)


def last_kernel(far, whole, gain, *refs):
    before, order, packets, pieces = refs[:3], refs[3], refs[4:8], refs[8:14]
    out, scaled, sems = refs[14:]
    places, cols = scaled.shape[1:]
    z, t = lax.axis_index("ctx"), lax.axis_index("tp")
    total = before[0][...] + before[1][...] + before[2][...]
    for k in range(2):
        wide = placed(order, packets[2 * k], packets[2 * k + 1])
        scaled[k] = wide.astype(BF16)
        total = total + jnp.sum(wide * wide, axis=1, keepdims=True)
    scale = lax.rsqrt(total / (8 * cols) + 1e-06)
    copies = []
    for k, (m, d) in enumerate(far + whole):
        block = jnp.bitwise_xor(z, m) * 2 + jnp.bitwise_xor(t, d)
        at = pl.ds(pl.multiple_of(block * cols, cols), cols)
        piece = scaled[k] if k < 2 else view(pieces[k - 2], places)[...]
        scaled[k] = (piece.astype(F32) * scale * gain[:, at].astype(F32)).astype(BF16)
        copies.append(pltpu.make_async_copy(scaled.at[k], out.at[:, at], sems.at[k]))
        copies[k].start()
    for copy in copies:
        copy.wait()


def place_and_norm(far, whole, gain, before, order, packets, pieces):
    places, cols = before[0].shape[0], packets[0].shape[1]
    operands = [gain, *before, order, *packets, *pieces]
    return pl.pallas_call(
        functools.partial(last_kernel, far, whole),
        out_shape=jax.ShapeDtypeStruct((places, 8 * cols), BF16),
        in_specs=[VMEM] * len(operands),
        out_specs=HBM,
        scratch_shapes=[pltpu.VMEM((8, places, cols), BF16), pltpu.SemaphoreType.DMA((8,))],
        compiler_params=PARAMS,
        cost_estimate=cost(32 * places * cols, 32 * places * cols),
        name="place_and_norm",
    )(*operands)


def after(x, *others):
    return lax.optimization_barrier((x, *others))[0]


def body(enc_rows, row_slot, row_kind, audio_proj, frame_proj, audio_bias, frame_bias, norm_gain):
    n = lax.axis_size("ctx")
    rows = enc_rows[0]
    half = rows.shape[0] // 2
    weights = (audio_proj, frame_proj, audio_bias[None, :], frame_bias[None, :])

    def over_ctx(x, m):
        return lax.ppermute(x, "ctx", [(i, i ^ m) for i in range(n)])

    def over_tp(x):
        return lax.ppermute(x, "tp", [(0, 1), (1, 0)])

    own = project_own(row_kind, rows, weights)
    blocks, slots = [own], [row_slot]

    def take(group):
        block, slot = project_parts(group, weights)
        blocks.append(block)
        slots.append(slot)

    def to_core(x, m, d):
        pairs = [(i * 2 + c, (i ^ m) * 2 + (c ^ d)) for i in range(n) for c in range(2)]
        return lax.ppermute(x, ("ctx", "tp"), pairs)

    def own_piece():
        pieces[0, 0], other = select(0, blocks, slots, [half, half])
        pieces[0, 1] = lax.all_gather(other, "tp", axis=0)
        return squares(None, [pieces[0, 0], pieces[0, 1]], half, OWN_FLOPS)

    def near_piece(total):
        pair = pieces[1]
        pieces[1, 0], pieces[1, 1] = pair, lax.all_gather(pair[half:], "tp", axis=0)
        return squares(total, [pieces[1, 0], pieces[1, 1]], half, NEAR_FLOPS)

    pieces = {}
    if n == 4:
        near, second, third, parity = to_send((None, 0, 1), rows, row_slot, row_kind)
        near, second, third = over_ctx(near, 1), over_ctx(second, 2), over_ctx(third, 3)
        first = lax.optimization_barrier((near, second, third, own))[:3]
        shared = [over_ctx(part, 1) for part in first[1:]]
        other = [over_tp(part)[None] for part in first]
        take([part[None] for part in first])
        other = lax.optimization_barrier((*other, blocks[-1]))[:3]
        early, size = len(blocks) + 1, 3 * half // 8
        sent = {}
        block, slot, chosen = parts_and_packet(3, other, weights, blocks, slots, size)
        blocks.append(block)
        slots.append(slot)
        sent[3] = over_ctx(chosen, 3)
        slots[0] = after(slots[0], chosen)
        (chosen,) = packet(2, early, blocks, slots, size, False)
        slots[0] = after(slots[0], chosen)
        sent[2] = over_ctx(chosen, 2)
        shared = lax.optimization_barrier((*shared, blocks[-1]))[:2]
        take([lax.all_gather(part, "tp", axis=0) for part in shared])

        (chosen,) = select(1, blocks, slots, [2 * half])
        slots[0] = after(slots[0], chosen)
        pieces[1] = over_ctx(chosen, 1)
        rest = {}
        for m in (2, 3):
            chosen = packet(m, early, blocks, slots, half - size, True)
            slots[0] = after(slots[0], chosen[0])
            waited = 3 if m == 2 else 2
            joined = lax.optimization_barrier((*chosen, sent[waited]))
            chosen, sent[waited] = joined[:2], joined[2]
            rest[m] = [to_core(piece, m, d) for d, piece in enumerate(chosen)]

        orders = order_of(size, parity, slots, half)
        slots[0] = after(slots[0], rest[2][0])
        total = [own_piece(), near_piece(None)]
        for m in (3, 2):
            whole_packet = sent[m]
            sent[m] = [whole_packet, lax.all_gather(whole_packet[size:], "tp", axis=0)]
        packets = {m: [part for d in range(2) for part in (sent[m][d], rest[m][d])] for m in (3, 2)}
        order3, order2 = orders
        pieces[2, 0], pieces[2, 1], squared = place(order2, packets[2])
        far, whole = ((3, 0), (3, 1)), ((2, 0), (2, 1), (1, 0), (1, 1), (0, 0), (0, 1))
        whole_pieces = [pieces[at] for at in whole]
        gain, total = norm_gain[None, :], [*total, squared]
        return place_and_norm(far, whole, gain, total, order3, packets[3], whole_pieces)[None]
    else:
        (mine,) = to_send((None,), rows, row_slot, row_kind)
        arrived = [over_ctx(mine, m) for m in range(1, n)]
        for direct in arrived[:-1]:
            direct = after(direct, blocks[-1])
            take([lax.all_gather(direct, "tp", axis=0)])
        direct = after(arrived[-1], blocks[-1])
        swapped = over_tp(direct)
        take([direct[None]])
        take([swapped[None]])

        order = [n - 1, 1] + list(reversed(range(2, n - 1)))
        for m in order:
            chosen = select(m, blocks, slots, [2 * half] if m == 1 else [half, half])
            slots[0] = after(slots[0], chosen[0])
            if m == 1:
                pieces[m] = over_ctx(chosen[0], m)
                continue
            for d, piece in enumerate(chosen):
                pieces[m, d] = to_core(piece, m, d)
        total = squares(None, [pieces[n - 1, 0], pieces[n - 1, 1]], half)
        total = squares(near_piece(total), [own_piece()], half)
        for m in order[2:-1]:
            late = [after(pieces[m, d], total) for d in range(2)]
            total = squares(total, late, half)
        fresh = (2 * (n - 1), 2 * (n - 1) + 1)
        for d in range(2):
            pieces[order[-1], d] = after(pieces[order[-1], d], total)
        order = order[:-1] + [0, order[-1]]

    places_of = tuple((m, d) for m in order for d in range(2))
    return norm(places_of, fresh, norm_gain[None, :], total, [pieces[at] for at in places_of])[None]


def solution(mesh):
    return jax.shard_map(
        body,
        mesh=mesh,
        in_specs=(
            P(("groups", "enc"), "ctx", None),
            P(("groups", "enc"), "ctx"),
            P(("groups", "enc"), "ctx"),
            P(None, ("ctx", "tp")),
            P(None, ("ctx", "tp")),
            P(("ctx", "tp")),
            P(("ctx", "tp")),
            P(),
        ),
        out_specs=P(("groups", "enc"), ("ctx", "tp"), None),
        check_vma=False,
    )
```

```python
import functools

import jax
import jax.numpy as jnp
from jax import lax
from jax.experimental import pallas as pl
from jax.experimental.pallas import tpu as pltpu
from jax.sharding import PartitionSpec as P

VMEM = pl.BlockSpec(memory_space=pltpu.VMEM)
HBM = pl.BlockSpec(memory_space=pltpu.HBM)
PARAMS = pltpu.CompilerParams(vmem_limit_bytes=12 << 20)
OWN_FLOPS, NEAR_FLOPS = 1 << 35, 0
BF16, F32, I32 = jnp.bfloat16, jnp.float32, jnp.int32


def cost(flops, moved):
    return pl.CostEstimate(flops=flops // 16, bytes_accessed=moved // 16, transcendentals=0)


def to_tiles(x, out):
    at = 0
    for r in range(0, x.shape[0], 16):
        for c in range(0, x.shape[1], 128):
            out[at : at + 16, :] = x[r : r + 16, c : c + 128]
            at += 16


def from_tiles(tiles, width):
    per_row = width // 128
    lines = []
    for r in range(0, tiles.shape[0], 16 * per_row):
        line = [tiles[r + 16 * c : r + 16 * (c + 1)] for c in range(per_row)]
        lines.append(jnp.concatenate(line, axis=1))
    return jnp.concatenate(lines, axis=0)


def send_kernel(cuts, rows, slot, kind, *refs):
    outs, (rows_here, slot_here, kind_here, sems) = refs[: len(cuts)], refs[-4:]
    whole, width = rows.shape
    half = whole // 2
    z, t = lax.axis_index("ctx"), lax.axis_index("tp")
    dealt = len(cuts) > 1
    source = rows
    if not dealt:
        source = rows.at[pl.ds(pl.multiple_of(t * half, half), half), :]
    copies = [
        pltpu.make_async_copy(slot, slot_here, sems.at[0]),
        pltpu.make_async_copy(kind, kind_here, sems.at[1]),
    ]
    cut = rows_here.shape[0] // 2
    for k in range(2):
        at = pl.ds(k * cut, cut)
        copies.append(
            pltpu.make_async_copy(source.at[at, :], rows_here.at[at, :], sems.at[2 + k])
        )
    for copy in copies:
        copy.start()
    copies[0].wait()
    copies[1].wait()
    if dealt:
        slot_row, slot_col = slot_here[...], column_of(slot_here[...])
        kind_col = column_of(kind_here[...])
        rank_row = jnp.sum((slot_col < slot_row).astype(I32), axis=0, keepdims=True)
        rank_col = jnp.sum((slot_row < slot_col).astype(I32), axis=1, keepdims=True)
        refs[len(cuts)][...] = lax.rem(rank_row, 2)

        def rank_at(k):
            odd = (k >= half // 2).astype(I32)
            return t * half + 2 * (k - odd * (half // 2)) + odd

        here = rank_col == rank_at(lax.broadcasted_iota(I32, (1, half), 1))
        slots = jnp.sum(jnp.where(here, slot_col, 0), axis=0, keepdims=True)
        kinds = jnp.sum(jnp.where(here, kind_col, 0), axis=0, keepdims=True)
        deal = rank_row == rank_at(lax.broadcasted_iota(I32, (half, 1), 0))
        deal = deal.astype(F32).astype(BF16)
        dealt_rows = None
        for k in range(2):
            copies[2 + k].wait()
            part = jnp.dot(
                deal[:, k * cut : (k + 1) * cut],
                rows_here[k * cut : (k + 1) * cut, :],
                preferred_element_type=F32,
            )
            dealt_rows = part if dealt_rows is None else dealt_rows + part
        rows_out = refs[-5]
        rows_out[...] = dealt_rows.astype(BF16)
    else:
        slots = jnp.where(t == 0, slot_here[:, :half], slot_here[:, half:])
        kinds = jnp.where(t == 0, kind_here[:, :half], kind_here[:, half:])
        copies[2].wait()
        copies[3].wait()
        rows_out = rows_here
    for out, parity in zip(outs, cuts):
        x, s, k = rows_out, slots, kinds
        size = half
        if parity is not None:
            size = half // 2
            second = lax.rem(z + parity, 2)
            x = rows_out.at[pl.ds(pl.multiple_of(second * size, size), size), :]
            s = jnp.where(second == 0, slots[:, :size], slots[:, size:])
            k = jnp.where(second == 0, kinds[:, :size], kinds[:, size:])
        to_tiles(x, out)
        line = lax.broadcasted_iota(I32, (16, size), 0)
        index = jnp.where(line == 0, s // 256, jnp.where(line == 1, s % 256, k))
        index = jnp.where(line < 3, index, 0).astype(F32)
        if size < 128:
            index = jnp.concatenate([index, jnp.zeros((16, 128 - size), F32)], axis=1)
        out[size * width // 128 :, :] = index.astype(BF16)


def to_send(cuts, rows, slot, kind):
    half, width = rows.shape[0] // 2, rows.shape[1]
    sizes = [half if parity is None else half // 2 for parity in cuts]
    shapes = [(size * width // 128 + 16, 128) for size in sizes]
    dealt = len(cuts) > 1
    out_shape = [jax.ShapeDtypeStruct(shape, BF16) for shape in shapes]
    scratch = [pltpu.VMEM((half, width), BF16)]
    if dealt:
        out_shape.append(jax.ShapeDtypeStruct(slot.shape, I32))
        scratch.append(pltpu.VMEM(rows.shape, BF16))
    return pl.pallas_call(
        functools.partial(send_kernel, cuts),
        out_shape=out_shape,
        in_specs=[HBM] * 3,
        out_specs=[VMEM] * len(out_shape),
        scratch_shapes=scratch
        + [
            pltpu.VMEM(slot.shape, I32),
            pltpu.VMEM(slot.shape, I32),
            pltpu.SemaphoreType.DMA((4,)),
        ],
        compiler_params=pltpu.CompilerParams(vmem_limit_bytes=16 << 20),
        cost_estimate=cost(0, 4 * half * width),
        name="to_send",
    )(*[pltpu.with_memory_space_constraint(x, pltpu.HBM) for x in (rows, slot, kind)])


def column_of(row_vector):
    r = row_vector.shape[1]
    diagonal = lax.broadcasted_iota(I32, (r, r), 0) == lax.broadcasted_iota(I32, (r, r), 1)
    return jnp.sum(jnp.where(diagonal, row_vector, 0), axis=1, keepdims=True)


def project(kind_row, x, w_audio, w_frame, b_audio, b_frame, out):
    is_audio = column_of(kind_row) == 0
    audio = jnp.dot(x, w_audio[...], preferred_element_type=F32)
    frame = jnp.dot(x, w_frame[...], preferred_element_type=F32)
    audio = audio + b_audio[...].astype(F32)
    frame = frame + b_frame[...].astype(F32)
    out[...] = jnp.where(is_audio, audio, frame).astype(out.dtype)


def project_own_kernel(kind, x, wa, wf, ba, bf, out):
    project(kind[...], x[...], wa, wf, ba, bf, out)


def project_own(kind, rows, weights):
    ew, cols = weights[0].shape
    return pl.pallas_call(
        project_own_kernel,
        out_shape=jax.ShapeDtypeStruct((rows.shape[0], cols), BF16),
        in_specs=[VMEM] * 6,
        out_specs=VMEM,
        compiler_params=PARAMS,
        cost_estimate=cost(4 * rows.shape[0] * ew * cols, 4 * ew * cols),
        name="project_own",
    )(kind, rows, *weights)


def project_parts_kernel(wa, wf, ba, bf, *refs):
    parts, out, slots = refs[:-2], refs[-2], refs[-1]
    width = wa.shape[0]
    x, index = [], []
    for ref in parts:
        for k in range(ref.shape[0]):
            lines = ref.shape[1] - 16
            size = lines * 128 // width
            x.append(from_tiles(ref[k, :lines, :], width))
            index.append(ref[k, lines:, :].astype(F32).astype(I32)[:, :size])
    x = x[0] if len(x) == 1 else jnp.concatenate(x, axis=0)
    index = index[0] if len(index) == 1 else jnp.concatenate(index, axis=1)
    slots[...] = index[0:1] * 256 + index[1:2]
    project(index[2:3], x, wa, wf, ba, bf, out)


def project_parts(parts, weights):
    ew, cols = weights[0].shape
    rows = sum(p.shape[0] * (p.shape[1] - 16) * 128 // ew for p in parts)
    return pl.pallas_call(
        project_parts_kernel,
        out_shape=[jax.ShapeDtypeStruct((rows, cols), BF16), jax.ShapeDtypeStruct((1, rows), I32)],
        in_specs=[VMEM] * (4 + len(parts)),
        out_specs=[VMEM] * 2,
        compiler_params=PARAMS,
        cost_estimate=cost(4 * rows * ew * cols, 4 * ew * cols),
        name="project_parts",
    )(*weights, *parts)


def select_kernel(m, count, *refs):
    blocks, slots, outs = refs[:count], refs[count : 2 * count], refs[2 * count :]
    places = sum(out.shape[0] for out in outs) // 2
    z, t = lax.axis_index("ctx"), lax.axis_index("tp")
    first = jnp.bitwise_xor(z, m) * 2 * places
    i = lax.broadcasted_iota(I32, (2 * places, 1), 0)
    position = first + jnp.bitwise_xor(i, t * places)
    total = None
    for block, slot in zip(blocks, slots):
        chosen = (slot[...] == position).astype(F32).astype(BF16)
        part = jnp.dot(chosen, block[...], preferred_element_type=F32)
        total = part if total is None else total + part
    at = 0
    for out in outs:
        out[...] = total[at : at + out.shape[0]].astype(BF16)
        at += out.shape[0]


def select(m, blocks, slots, sizes):
    rows, cols = sum(b.shape[0] for b in blocks), blocks[0].shape[1]
    return pl.pallas_call(
        functools.partial(select_kernel, m, len(blocks)),
        out_shape=[jax.ShapeDtypeStruct((size, cols), BF16) for size in sizes],
        in_specs=[VMEM] * (2 * len(blocks)),
        out_specs=[VMEM] * len(sizes),
        compiler_params=PARAMS,
        cost_estimate=cost(2 * sum(sizes) * rows * cols, 2 * rows * cols),
        name="select",
    )(*blocks, *slots)


def upto(places, width):
    i = lax.broadcasted_iota(I32, (width, width), 0)
    j = lax.broadcasted_iota(I32, (width, width), 1)
    counts = i <= j
    if width > places:
        counts = jnp.logical_and(counts, (i < places) == (j < places))
    return counts.astype(F32).astype(BF16)


def one_hot(found):
    return found.astype(F32).astype(BF16)


def over_rows(a, b):
    return lax.dot_general(a, b, (((1,), (1,)), ((), ())), preferred_element_type=F32)


def running(flags, counts):
    return jnp.dot(one_hot(flags), counts, preferred_element_type=F32)


def packet_kernel(m, early, count, second, *refs):
    blocks, slots, outs = refs[:count], refs[count : 2 * count], refs[2 * count :]
    size = sum(out.shape[0] for out in outs) // 2
    places = blocks[0].shape[0] // 2
    first_size = places - size if second else size
    z, t = lax.axis_index("ctx"), lax.axis_index("tp")
    i = lax.broadcasted_iota(I32, (2 * places, 1), 0)
    position = jnp.bitwise_xor(z, m) * 2 * places + jnp.bitwise_xor(i, t * places)
    holds = [one_hot(slot[...] == position) for slot in slots]
    known = None
    for k in range(early):
        part = over_rows(jnp.ones((8, holds[k].shape[1]), BF16), holds[k])
        known = part if known is None else known + part
    counts = upto(places, 2 * places)
    wanted = known > 0.5
    number = running(wanted, counts)
    if second:
        wanted = jnp.logical_not(jnp.logical_and(wanted, number < first_size + 0.5))
        number = running(wanted, counts)
    number = jnp.where(wanted, number, 0.0)[0:1].astype(I32)
    e = lax.broadcasted_iota(I32, (2 * size, 1), 0)
    upper = (e >= size).astype(I32)
    lane_upper = (lax.broadcasted_iota(I32, (1, 2 * places), 1) >= places).astype(I32)
    pick = jnp.logical_and(number == e - upper * size + 1, lane_upper == upper)
    pick = one_hot(pick)
    total = None
    for block, hold in zip(blocks, holds):
        chosen = jnp.dot(pick, hold, preferred_element_type=F32).astype(BF16)
        part = jnp.dot(chosen, block[...], preferred_element_type=F32)
        total = part if total is None else total + part
    if second:
        outs[0][...] = total[:size].astype(BF16)
        outs[1][...] = total[size:].astype(BF16)
    else:
        outs[0][...] = total.astype(BF16)


def packet(m, early, blocks, slots, size, second):
    rows, cols = sum(b.shape[0] for b in blocks), blocks[0].shape[1]
    return pl.pallas_call(
        functools.partial(packet_kernel, m, early, len(blocks), second),
        out_shape=[jax.ShapeDtypeStruct((size if second else 2 * size, cols), BF16)] * (1 + second),
        in_specs=[VMEM] * (2 * len(blocks)),
        out_specs=[VMEM] * (1 + second),
        compiler_params=PARAMS,
        cost_estimate=cost(4 * size * rows * cols, 2 * rows * cols),
        name="packet",
    )(*blocks, *slots)


def order_kernel(first_size, parity, *refs):
    slots, outs = refs[:-2], refs[-2:]
    places = outs[0].shape[0]
    z, t = lax.axis_index("ctx"), lax.axis_index("tp")
    pair, odd = z // 2, lax.rem(z, 2)
    position = (2 * z + t) * places + lax.broadcasted_iota(I32, (places, 1), 0)
    source = lax.broadcasted_iota(I32, (8, 1), 0)
    known = None
    for k, slot in enumerate(slots):
        width = slot.shape[1]
        lane = lax.broadcasted_iota(I32, (1, width), 1)
        if k == 0:
            near, odd_rank = lane >= 0, parity[...]
        elif k in (1, 2):
            near = lane < places
            odd_rank = jnp.where(near, (lane >= places // 2).astype(I32), odd)
        else:
            near, odd_rank = lane < 0, jnp.zeros((1, width), I32) + 1 - odd
        owner_pair = jnp.where(near, pair, 1 - pair)
        held = jnp.logical_or(owner_pair == source // 2, odd_rank == lax.rem(source, 2))
        part = over_rows(one_hot(held), one_hot(slot[...] == position))
        known = part if known is None else known + part
    counts = upto(places, places)
    early = known > 0.5
    number = running(early, counts)
    early = jnp.logical_and(early, number < first_size + 0.5)
    later = running(jnp.logical_not(early), counts)
    place = jnp.where(early, number, later + first_size) - 1.0
    for m, out in zip((3, 2), outs):
        row = jnp.sum(jnp.where(source == jnp.bitwise_xor(z, m), place, 0.0), axis=0, keepdims=True)
        column = column_of(row.astype(I32))
        out[...] = one_hot(column == lax.broadcasted_iota(I32, (1, places), 1))


def order_of(first_size, parity, slots, places):
    return pl.pallas_call(
        functools.partial(order_kernel, first_size),
        out_shape=[jax.ShapeDtypeStruct((places, places), BF16)] * 2,
        in_specs=[VMEM] * (1 + len(slots)),
        out_specs=[VMEM] * 2,
        compiler_params=PARAMS,
        cost_estimate=cost(1 << 34, 0),
        name="order_of",
    )(parity, *slots)


def view(ref, places):
    if len(ref.shape) == 3:
        return ref.at[1 - lax.axis_index("tp")]
    return ref.at[pl.ds(0, places), :]


def square_sum(piece):
    wide = piece[...].astype(F32)
    return jnp.sum(wide * wide, axis=1, keepdims=True)


def squares_kernel(*refs):
    out = refs[-1]
    total = None
    for ref in refs[:-1]:
        part = ref[...] if ref.dtype == F32 else square_sum(view(ref, out.shape[0]))
        total = part if total is None else total + part
    out[...] = total


def squares(total, pieces, places, flops=0):
    operands = pieces if total is None else [total] + pieces
    return pl.pallas_call(
        squares_kernel,
        out_shape=jax.ShapeDtypeStruct((places, 1), F32),
        in_specs=[VMEM] * len(operands),
        out_specs=VMEM,
        compiler_params=PARAMS,
        cost_estimate=cost(flops, 0),
        name="squares",
    )(*operands)


def norm_kernel(places_of, fresh, gain, before, *refs):
    n = len(places_of)
    out, scaled, sems = refs[n], refs[n + 1], refs[n + 2]
    places, cols = scaled.shape[1:]
    pieces = [view(ref, places) for ref in refs[:n]]
    z, t = lax.axis_index("ctx"), lax.axis_index("tp")
    total = before[...]
    for k in fresh:
        total = total + square_sum(pieces[k])
    scale = lax.rsqrt(total / (n * cols) + 1e-06)
    copies = []
    for k, ((m, d), piece) in enumerate(zip(places_of, pieces)):
        block = jnp.bitwise_xor(z, m) * 2 + jnp.bitwise_xor(t, d)
        at = pl.ds(pl.multiple_of(block * cols, cols), cols)
        scaled[k] = (piece[...].astype(F32) * scale * gain[:, at].astype(F32)).astype(BF16)
        copies.append(pltpu.make_async_copy(scaled.at[k], out.at[:, at], sems.at[k]))
        copies[k].start()
    for copy in copies:
        copy.wait()


def norm(places_of, fresh, gain, before, pieces):
    n, places, cols = len(pieces), before.shape[0], pieces[0].shape[-1]
    return pl.pallas_call(
        functools.partial(norm_kernel, places_of, fresh),
        out_shape=jax.ShapeDtypeStruct((places, n * cols), BF16),
        in_specs=[VMEM] * (n + 2),
        out_specs=HBM,
        scratch_shapes=[pltpu.VMEM((n, places, cols), BF16), pltpu.SemaphoreType.DMA((n,))],
        compiler_params=PARAMS,
        cost_estimate=cost(4 * places * n * cols, 4 * places * n * cols),
        name="norm",
    )(gain, before, *pieces)


def placed(order, early, later):
    early = view(early, order.shape[0] - later.shape[0])[...]
    both = jnp.concatenate([early, later[...]], axis=0)
    return jnp.dot(order[...], both, preferred_element_type=F32)


def place_kernel(order, *refs):
    packets, outs = refs[:4], refs[4:]
    total = None
    for d in range(2):
        wide = placed(order, packets[2 * d], packets[2 * d + 1])
        outs[d][...] = wide.astype(BF16)
        part = jnp.sum(wide * wide, axis=1, keepdims=True)
        total = part if total is None else total + part
    outs[2][...] = total


def place(order, packets):
    places, cols = order.shape[0], packets[0].shape[-1]
    piece = jax.ShapeDtypeStruct((places, cols), BF16)
    return pl.pallas_call(
        place_kernel,
        out_shape=[piece, piece, jax.ShapeDtypeStruct((places, 1), F32)],
        in_specs=[VMEM] * 5,
        out_specs=[VMEM] * 3,
        compiler_params=PARAMS,
        cost_estimate=cost(0, 0),
        name="place",
    )(order, *packets)


def last_kernel(far, whole, gain, *refs):
    before, order, packets, pieces = refs[:3], refs[3], refs[4:8], refs[8:14]
    out, scaled, sems = refs[14:]
    places, cols = scaled.shape[1:]
    z, t = lax.axis_index("ctx"), lax.axis_index("tp")
    total = before[0][...] + before[1][...] + before[2][...]
    for k in range(2):
        wide = placed(order, packets[2 * k], packets[2 * k + 1])
        scaled[k] = wide.astype(BF16)
        total = total + jnp.sum(wide * wide, axis=1, keepdims=True)
    scale = lax.rsqrt(total / (8 * cols) + 1e-06)
    copies = []
    for k, (m, d) in enumerate(far + whole):
        block = jnp.bitwise_xor(z, m) * 2 + jnp.bitwise_xor(t, d)
        at = pl.ds(pl.multiple_of(block * cols, cols), cols)
        piece = scaled[k] if k < 2 else view(pieces[k - 2], places)[...]
        scaled[k] = (piece.astype(F32) * scale * gain[:, at].astype(F32)).astype(BF16)
        copies.append(pltpu.make_async_copy(scaled.at[k], out.at[:, at], sems.at[k]))
        copies[k].start()
    for copy in copies:
        copy.wait()


def place_and_norm(far, whole, gain, before, order, packets, pieces):
    places, cols = before[0].shape[0], packets[0].shape[1]
    operands = [gain, *before, order, *packets, *pieces]
    return pl.pallas_call(
        functools.partial(last_kernel, far, whole),
        out_shape=jax.ShapeDtypeStruct((places, 8 * cols), BF16),
        in_specs=[VMEM] * len(operands),
        out_specs=HBM,
        scratch_shapes=[pltpu.VMEM((8, places, cols), BF16), pltpu.SemaphoreType.DMA((8,))],
        compiler_params=PARAMS,
        cost_estimate=cost(32 * places * cols, 32 * places * cols),
        name="place_and_norm",
    )(*operands)


def after(x, *others):
    return lax.optimization_barrier((x, *others))[0]


def body(enc_rows, row_slot, row_kind, audio_proj, frame_proj, audio_bias, frame_bias, norm_gain):
    n = lax.axis_size("ctx")
    rows = enc_rows[0]
    half = rows.shape[0] // 2
    weights = (audio_proj, frame_proj, audio_bias[None, :], frame_bias[None, :])

    def over_ctx(x, m):
        return lax.ppermute(x, "ctx", [(i, i ^ m) for i in range(n)])

    def over_tp(x):
        return lax.ppermute(x, "tp", [(0, 1), (1, 0)])

    own = project_own(row_kind, rows, weights)
    blocks, slots = [own], [row_slot]

    def take(group):
        block, slot = project_parts(group, weights)
        blocks.append(block)
        slots.append(slot)

    def to_core(x, m, d):
        pairs = [(i * 2 + c, (i ^ m) * 2 + (c ^ d)) for i in range(n) for c in range(2)]
        return lax.ppermute(x, ("ctx", "tp"), pairs)

    def own_piece():
        pieces[0, 0], other = select(0, blocks, slots, [half, half])
        pieces[0, 1] = lax.all_gather(other, "tp", axis=0)
        return squares(None, [pieces[0, 0], pieces[0, 1]], half, OWN_FLOPS)

    def near_piece(total):
        pair = pieces[1]
        pieces[1, 0], pieces[1, 1] = pair, lax.all_gather(pair[half:], "tp", axis=0)
        return squares(total, [pieces[1, 0], pieces[1, 1]], half, NEAR_FLOPS)

    pieces = {}
    if n == 4:
        near, second, third, parity = to_send((None, 0, 1), rows, row_slot, row_kind)
        near, second, third = over_ctx(near, 1), over_ctx(second, 2), over_ctx(third, 3)
        first = lax.optimization_barrier((near, second, third, own))[:3]
        shared = [over_ctx(part, 1) for part in first[1:]]
        other = [over_tp(part)[None] for part in first]
        take([part[None] for part in first])
        other = lax.optimization_barrier((*other, blocks[-1]))[:3]
        take(other)

        early, size = len(blocks), 3 * half // 8
        sent = {}
        for m in (3, 2):
            chosen = packet(m, early, blocks, slots, size, False)
            slots[0] = after(slots[0], chosen[0])
            sent[m] = over_ctx(chosen[0], m)
        shared = lax.optimization_barrier((*shared, blocks[-1]))[:2]
        take([lax.all_gather(part, "tp", axis=0) for part in shared])

        (chosen,) = select(1, blocks, slots, [2 * half])
        slots[0] = after(slots[0], chosen)
        pieces[1] = over_ctx(chosen, 1)
        rest = {}
        for m in (2, 3):
            chosen = packet(m, early, blocks, slots, half - size, True)
            slots[0] = after(slots[0], chosen[0])
            waited = 3 if m == 2 else 2
            joined = lax.optimization_barrier((*chosen, sent[waited]))
            chosen, sent[waited] = joined[:2], joined[2]
            rest[m] = [to_core(piece, m, d) for d, piece in enumerate(chosen)]

        orders = order_of(size, parity, slots, half)
        slots[0] = after(slots[0], rest[2][0])
        total = [own_piece(), near_piece(None)]
        for m in (3, 2):
            whole_packet = sent[m]
            sent[m] = [whole_packet, lax.all_gather(whole_packet[size:], "tp", axis=0)]
        packets = {m: [part for d in range(2) for part in (sent[m][d], rest[m][d])] for m in (3, 2)}
        order3, order2 = orders
        pieces[2, 0], pieces[2, 1], squared = place(order2, packets[2])
        far, whole = ((3, 0), (3, 1)), ((2, 0), (2, 1), (1, 0), (1, 1), (0, 0), (0, 1))
        whole_pieces = [pieces[at] for at in whole]
        gain, total = norm_gain[None, :], [*total, squared]
        return place_and_norm(far, whole, gain, total, order3, packets[3], whole_pieces)[None]
    else:
        (mine,) = to_send((None,), rows, row_slot, row_kind)
        arrived = [over_ctx(mine, m) for m in range(1, n)]
        for direct in arrived[:-1]:
            direct = after(direct, blocks[-1])
            take([lax.all_gather(direct, "tp", axis=0)])
        direct = after(arrived[-1], blocks[-1])
        swapped = over_tp(direct)
        take([direct[None]])
        take([swapped[None]])

        order = [n - 1, 1] + list(reversed(range(2, n - 1)))
        for m in order:
            chosen = select(m, blocks, slots, [2 * half] if m == 1 else [half, half])
            slots[0] = after(slots[0], chosen[0])
            if m == 1:
                pieces[m] = over_ctx(chosen[0], m)
                continue
            for d, piece in enumerate(chosen):
                pieces[m, d] = to_core(piece, m, d)
        total = squares(None, [pieces[n - 1, 0], pieces[n - 1, 1]], half)
        total = squares(near_piece(total), [own_piece()], half)
        for m in order[2:-1]:
            late = [after(pieces[m, d], total) for d in range(2)]
            total = squares(total, late, half)
        fresh = (2 * (n - 1), 2 * (n - 1) + 1)
        for d in range(2):
            pieces[order[-1], d] = after(pieces[order[-1], d], total)
        order = order[:-1] + [0, order[-1]]

    places_of = tuple((m, d) for m in order for d in range(2))
    return norm(places_of, fresh, norm_gain[None, :], total, [pieces[at] for at in places_of])[None]


def solution(mesh):
    return jax.shard_map(
        body,
        mesh=mesh,
        in_specs=(
            P(("groups", "enc"), "ctx", None),
            P(("groups", "enc"), "ctx"),
            P(("groups", "enc"), "ctx"),
            P(None, ("ctx", "tp")),
            P(None, ("ctx", "tp")),
            P(("ctx", "tp")),
            P(("ctx", "tp")),
            P(),
        ),
        out_specs=P(("groups", "enc"), ("ctx", "tp"), None),
        check_vma=False,
    )
```
